32 devices in a mesh: dp: 16 (over z, x, core), fsdp: 2 (over y).
Axes of the slice: x: 2, y: 2, z: 4, core: 2. Of those that a mesh axis runs over, the one named last changes fastest.
Arguments:
- x_prompt: bfloat16 [2, 16, 960, 768], P(None, 'dp', 'fsdp'), may hold values from -6 to 6
- x_cont: bfloat16 [2, 16, 2, 64, 768], P(None, 'dp', 'fsdp'), may hold values from -6 to 6
- dy_prompt: bfloat16 [2, 16, 960, 768], P(None, 'dp', 'fsdp'), may hold values from -6 to 6
- dy_cont: bfloat16 [2, 16, 2, 64, 768], P(None, 'dp', 'fsdp'), may hold values from -6 to 6
- ln1_gain: bfloat16 [768], P(('dp', 'fsdp')), may hold values from 0.5 to 1.5
- ln1_bias: bfloat16 [768], P(('dp', 'fsdp')), may hold values from -3 to 3
- w_qkv: bfloat16 [768, 2304], P(('dp', 'fsdp')), may hold values from -0.21875 to 0.21875
- b_qv: bfloat16 [1536], P(('dp', 'fsdp')), may hold values from -1.5 to 1.5
- w_out: bfloat16 [768, 768], P(('dp', 'fsdp')), may hold values from -1.25 to 1.25
- b_out: bfloat16 [768], P(('dp', 'fsdp')), may hold values from -3 to 3
- ln2_gain: bfloat16 [768], P(('dp', 'fsdp')), may hold values from 0.5 to 1.5
- ln2_bias: bfloat16 [768], P(('dp', 'fsdp')), may hold values from -3 to 3
- w_up: bfloat16 [768, 3072], P(('dp', 'fsdp')), may hold values from -0.21875 to 0.21875
- b_up: bfloat16 [3072], P(('dp', 'fsdp')), may hold values from -4 to 4
- w_down: bfloat16 [3072, 768], P(('dp', 'fsdp')), may hold values from -0.109375 to 0.109375
- b_down: bfloat16 [768], P(('dp', 'fsdp')), may hold values from -3 to 3
Outputs:
- y_prompt: bfloat16 [2, 16, 960, 768], P(None, 'dp', 'fsdp')
- y_cont: bfloat16 [2, 16, 2, 64, 768], P(None, 'dp', 'fsdp')
- dx_prompt: float32 [2, 16, 960, 768], P(None, 'dp', 'fsdp')
- dx_cont: float32 [2, 16, 2, 64, 768], P(None, 'dp', 'fsdp')
- grad_ln1_gain: float32 [768], P(('dp', 'fsdp'))
- grad_ln1_bias: float32 [768], P(('dp', 'fsdp'))
- grad_w_qkv: float32 [768, 2304], P(('dp', 'fsdp'))
- grad_b_qv: float32 [1536], P(('dp', 'fsdp'))
- grad_w_out: float32 [768, 768], P(('dp', 'fsdp'))
- grad_b_out: float32 [768], P(('dp', 'fsdp'))
- grad_ln2_gain: float32 [768], P(('dp', 'fsdp'))
- grad_ln2_bias: float32 [768], P(('dp', 'fsdp'))
- grad_w_up: float32 [768, 3072], P(('dp', 'fsdp'))
- grad_b_up: float32 [3072], P(('dp', 'fsdp'))
- grad_w_down: float32 [3072, 768], P(('dp', 'fsdp'))
- grad_b_down: float32 [768], P(('dp', 'fsdp'))
The draws below stay inside these ranges and needn't reach their ends.
All inputs are finite; a program needn't handle non-finite values.
Results may differ from the reference program's by a relative error of at most 0.012.
Values may be sent and summed in bfloat16 or wider, within the bound.
No kernel may reach another device: no remote copies, remote signals or barrier semaphores. Data moves between devices by JAX's collectives and lax.ppermute only.
A program may use at most 248 MiB of HBM per device.

```python
import jax
import jax.numpy as jnp
from jax import lax

D = 768
HEADS = 12
HEAD_DIM = 64
FF = 3072
PROMPT = 960
CONT = 64
MICRO = 2
NCONT = 2
GROUPS = 16


def block_scale(stream_key, shape, shards, low, top_value):
    factor_of = 1.0
    for dim, blocks in shards:
        steps = jax.random.uniform(jax.random.fold_in(jax.random.fold_in(stream_key, 6), dim), (blocks,), jnp.float32, low / len(shards), top_value / len(shards))
        factor_of = factor_of * jnp.repeat(jnp.exp(steps), shape[dim] // blocks).reshape((-1,) + (1,) * (len(shape) - 1 - dim))
    return factor_of


def noise(key, dims, scale, reach, pieces=(), kind=jnp.bfloat16):
    level = block_scale(key, dims, pieces, -0.22, 0.18) if pieces else 1.0
    array = jax.random.normal(key, dims, jnp.float32) * scale * level
    return jnp.minimum(jnp.maximum(array, -reach), reach).astype(kind)


def setup_inputs(seed: int = 0) -> dict:
    keys = jax.random.split(jax.random.key(seed), 17)
    x_prompt = noise(keys[0], (MICRO, GROUPS, PROMPT, D), 1.0, 6.0, ((1, 16), (2, 2)))
    x_cont = noise(keys[1], (MICRO, GROUPS, NCONT, CONT, D), 1.0, 6.0, ((1, 16), (2, 2)))
    dy_prompt = noise(keys[2], (MICRO, GROUPS, PROMPT, D), 1.0, 6.0, ((1, 16), (2, 2)))
    dy_cont = noise(keys[3], (MICRO, GROUPS, NCONT, CONT, D), 1.0, 6.0, ((1, 16), (2, 2)))
    ln1_gain = jnp.clip(1.0 + 0.1 * jax.random.normal(keys[4], (D,), jnp.float32), 0.5, 1.5).astype(jnp.bfloat16)
    ln1_bias = noise(keys[5], (D,), 0.2, 3.0, ((0, 32),))
    w_qkv = noise(keys[6], (D, 3 * D), D ** -0.5, 0.21875, ((0, 32),))
    b_qv = noise(keys[7], (2 * D,), 0.1, 1.5, ((0, 32),))
    w_out = noise(keys[8], (D, D), (D // 32) ** -0.5, 1.25, ((0, 32),))
    b_out = noise(keys[9], (D,), 0.2, 3.0, ((0, 32),))
    ln2_gain = jnp.clip(1.0 + 0.1 * jax.random.normal(keys[10], (D,), jnp.float32), 0.5, 1.5).astype(jnp.bfloat16)
    ln2_bias = noise(keys[11], (D,), 0.2, 3.0, ((0, 32),))
    w_up = noise(keys[12], (D, FF), D ** -0.5, 0.21875, ((0, 32),))
    b_up = noise(keys[13], (FF,), 0.3, 4.0, ((0, 32),))
    w_down = noise(keys[14], (FF, D), FF ** -0.5, 0.109375, ((0, 32),))
    b_down = noise(keys[15], (D,), 0.2, 3.0, ((0, 32),))
    return dict(x_prompt=x_prompt, x_cont=x_cont, dy_prompt=dy_prompt, dy_cont=dy_cont, ln1_gain=ln1_gain, ln1_bias=ln1_bias, w_qkv=w_qkv, b_qv=b_qv, w_out=w_out, b_out=b_out, ln2_gain=ln2_gain, ln2_bias=ln2_bias, w_up=w_up, b_up=b_up, w_down=w_down, b_down=b_down)


EPS = 1e-05
NEG = -1e+30
HIGH = lax.Precision.HIGHEST

@jax.custom_vjp
def low(v):
    return lax.optimization_barrier(v.astype(jnp.bfloat16)).astype(jnp.float32)

@jax.custom_vjp
def low_back(v):
    return v

def low_keep(v):
    return (low(v), None)

def low_pass(kept, grad):
    return (grad,)

def back_keep(v):
    return (v, None)

def back_low(kept, grad):
    return (low(grad),)
low.defvjp(low_keep, low_pass)
low_back.defvjp(back_keep, back_low)

def normalize(values, gain, shift):
    center = values - lax.optimization_barrier(jnp.mean(values, -1, keepdims=True))
    spread = lax.optimization_barrier(jnp.mean(center * center, -1, keepdims=True))
    return center * lax.rsqrt(spread + EPS) * gain + shift

def project(values, params):
    normed = low(normalize(values, params[0], params[1]))
    joined = jnp.dot(normed, params[2], precision=HIGH)
    queries = low_back(low(joined[:, :D] + params[3][:D]))
    keys_out = low_back(low(joined[:, D:2 * D]))
    values_out = low_back(low(joined[:, 2 * D:] + params[3][D:]))
    return (queries, keys_out, values_out)

def attend(queries, keys_in, values_in, query_pos, column_base):
    heads_q = queries.reshape(-1, HEADS, HEAD_DIM)
    heads_k = keys_in.reshape(-1, HEADS, HEAD_DIM)
    heads_v = values_in.reshape(-1, HEADS, HEAD_DIM)
    scores = low_back(jnp.einsum('rhd,khd->hrk', heads_q, heads_k, precision=HIGH) * HEAD_DIM ** (-0.5))
    key_pos = jnp.arange(keys_in.shape[0], dtype=jnp.int32)
    causal = key_pos[None, :] <= query_pos[:, None]
    chosen = (key_pos[None, :] < query_pos[:, None]) & (key_pos[None, :] > 0)
    select = jnp.where(chosen, jnp.maximum(scores[0], 0.0), 0.0)
    earlier = jnp.cumsum(select, 0) - select
    penalty = 4.0 / (PROMPT + CONT) * (column_base[None, :] + earlier)
    logits = jnp.where(causal[None], scores - penalty[None], NEG)
    softmax_w = low(jax.nn.softmax(logits, -1))
    mixture = jnp.einsum('hrk,khd->rhd', softmax_w, heads_v, precision=HIGH).reshape(-1, D)
    return (low_back(low(mixture)), lax.optimization_barrier(jnp.sum(select, 0)))

def group_forward(params, prompt_x, cont_x):
    query_p, key_p, value_p = project(prompt_x, params)
    cont_flat = cont_x.reshape(-1, D)
    query_c, key_c, value_c = project(cont_flat, params)
    prompt_pos = jnp.arange(PROMPT, dtype=jnp.int32)
    mixed_p, colsum = attend(query_p, key_p, value_p, prompt_pos, jnp.zeros((PROMPT,), jnp.float32))
    column_base = jnp.concatenate([colsum, jnp.zeros((CONT,), jnp.float32)])
    cont_pos = PROMPT + jnp.arange(CONT, dtype=jnp.int32)

    def one_cont(query_one, key_one, value_one):
        keys_all = jnp.concatenate([key_p, key_one], 0)
        values_all = jnp.concatenate([value_p, value_one], 0)
        mixture, unused = attend(query_one, keys_all, values_all, cont_pos, column_base)
        return mixture
    mixed_c = jax.vmap(one_cont)(query_c.reshape(NCONT, CONT, D), key_c.reshape(NCONT, CONT, D), value_c.reshape(NCONT, CONT, D))
    all_rows = jnp.concatenate([prompt_x, cont_flat], 0)
    mixed = jnp.concatenate([mixed_p, mixed_c.reshape(-1, D)], 0)
    branch = low_back(jnp.dot(mixed, params[4], precision=HIGH) + params[5])
    residual = all_rows + branch
    normed = low(normalize(residual, params[6], params[7]))
    upward = low_back(jnp.dot(normed, params[8], precision=HIGH) + params[9])
    active = low(jax.nn.gelu(upward, approximate=True))
    output = residual + low_back(jnp.dot(active, params[10], precision=HIGH) + params[11])
    return (output[:PROMPT], output[PROMPT:].reshape(NCONT, CONT, D))

def reference(x_prompt, x_cont, dy_prompt, dy_cont, ln1_gain, ln1_bias, w_qkv, b_qv, w_out, b_out, ln2_gain, ln2_bias, w_up, b_up, w_down, b_down):
    params = tuple((single.astype(jnp.float32) for single in (ln1_gain, ln1_bias, w_qkv, b_qv, w_out, b_out, ln2_gain, ln2_bias, w_up, b_up, w_down, b_down)))
    group_count = MICRO * GROUPS
    prompts = x_prompt.reshape(group_count, PROMPT, D).astype(jnp.float32)
    cont_x_all = x_cont.reshape(group_count, NCONT, CONT, D).astype(jnp.float32)
    cot_prompt = dy_prompt.reshape(group_count, PROMPT, D).astype(jnp.float32)
    cot_cont = dy_cont.reshape(group_count, NCONT, CONT, D).astype(jnp.float32)

    def step_group(totals, inputs_g):
        prompt_x, cont_x, prompt_dy, cont_dy = inputs_g
        outputs, backward = jax.vjp(group_forward, params, prompt_x, cont_x)
        grads_params, grad_prompt, grad_cont = backward((prompt_dy, cont_dy))
        totals = jax.tree.map(lambda first, second: first + second, totals, grads_params)
        return (totals, (outputs[0], outputs[1], grad_prompt, grad_cont))
    zero_grads = jax.tree.map(jnp.zeros_like, params)
    totals, stacked = lax.scan(step_group, zero_grads, (prompts, cont_x_all, cot_prompt, cot_cont))
    return (stacked[0].reshape(x_prompt.shape).astype(jnp.bfloat16), stacked[1].reshape(x_cont.shape).astype(jnp.bfloat16), stacked[2].reshape(x_prompt.shape), stacked[3].reshape(x_cont.shape), totals[0], totals[1], totals[2], totals[3], totals[4], totals[5], totals[6], totals[7], totals[8], totals[9], totals[10], totals[11])
```

```python
from functools import partial

import jax
import jax.numpy as jnp
from jax import lax
from jax.experimental import pallas as pl
from jax.experimental.pallas import tpu as pltpu
from jax.sharding import PartitionSpec as P

D = 768
HEADS = 12
HEAD_DIM = 64
PROMPT = 960
CONT = 64
MICRO = 2


EPS = 1e-05
NEG = -1e30


def normalize(values, gain, shift):
    center = values - jnp.mean(values, -1, keepdims=True)
    spread = jnp.mean(center * center, -1, keepdims=True)
    return center * lax.rsqrt(spread + EPS) * gain + shift


def later_sum(values):
    return jnp.flip(jnp.cumsum(jnp.flip(values, 1), 1), 1) - values


def attend_group(inputs_g, causal, score_scale):
    query_g, key_g, value_g, penalty_g = inputs_g
    rows_here = query_g.shape[0]
    heads_q = query_g.reshape(rows_here, HEADS, HEAD_DIM)
    heads_k = key_g.reshape(-1, HEADS, HEAD_DIM)
    heads_v = value_g.reshape(-1, HEADS, HEAD_DIM)
    scores = (
        jnp.einsum("rhd,khd->hrk", heads_q, heads_k, preferred_element_type=jnp.float32)
        * score_scale
    )
    logits = jnp.where(causal[None], scores - penalty_g[None], NEG)
    highest = jnp.max(logits, -1, keepdims=True)
    raised = jnp.exp(logits - highest)
    totals = jnp.sum(raised, -1, keepdims=True)
    weights_b = (raised / totals).astype(jnp.bfloat16)
    mixture = jnp.einsum("hrk,khd->rhd", weights_b, heads_v, preferred_element_type=jnp.float32)
    return (
        mixture.reshape(rows_here, -1).astype(jnp.bfloat16),
        (highest + jnp.log(totals))[..., 0],
    )


def attend_back(inputs_g, causal, score_scale):
    query_g, key_g, value_g, penalty_g, grad_mix, log_totals = inputs_g
    rows_here = query_g.shape[0]
    heads_q = query_g.reshape(rows_here, HEADS, HEAD_DIM)
    heads_k = key_g.reshape(-1, HEADS, HEAD_DIM)
    heads_v = value_g.reshape(-1, HEADS, HEAD_DIM)
    heads_g = grad_mix.reshape(rows_here, HEADS, HEAD_DIM)
    scores = (
        jnp.einsum("rhd,khd->hrk", heads_q, heads_k, preferred_element_type=jnp.float32)
        * score_scale
    )
    logits = jnp.where(causal[None], scores - penalty_g[None], NEG)
    softmax_w = jnp.exp(logits - log_totals[..., None])
    grad_soft = jnp.einsum("rhd,khd->hrk", heads_g, heads_v, preferred_element_type=jnp.float32)
    inner_sum = jnp.sum(softmax_w * grad_soft, -1, keepdims=True)
    grad_logit = softmax_w * (grad_soft - inner_sum)
    grad_value = jnp.einsum(
        "hrk,rhd->khd", softmax_w.astype(jnp.bfloat16), heads_g, preferred_element_type=jnp.float32
    )
    grad_penalty = -jnp.sum(grad_logit, 0)
    rest_b = grad_logit[1:].astype(jnp.bfloat16)
    grad_query = (
        jnp.einsum("hrk,khd->rhd", rest_b, heads_k[:, 1:], preferred_element_type=jnp.float32)
        * score_scale
    )
    grad_key = (
        jnp.einsum("hrk,rhd->khd", rest_b, heads_q[:, 1:], preferred_element_type=jnp.float32)
        * score_scale
    )
    return (
        grad_value.reshape(-1, D),
        grad_query.reshape(rows_here, -1),
        grad_key.reshape(grad_key.shape[0], -1),
        grad_logit[0],
        grad_penalty,
    )


def spread_layer(
    x_prompt,
    x_cont,
    dy_prompt,
    dy_cont,
    ln1_gain,
    ln1_bias,
    w_qkv,
    b_qv,
    w_out,
    b_out,
    ln2_gain,
    ln2_bias,
    w_up,
    b_up,
    w_down,
    b_down,
):
    shards = (
        ln1_gain,
        ln1_bias,
        w_qkv,
        b_qv,
        w_out,
        b_out,
        ln2_gain,
        ln2_bias,
        w_up,
        b_up,
        w_down,
        b_down,
    )
    groups_here = x_prompt.shape[1]
    prompt_rows = x_prompt.shape[2]
    fsdp_count = lax.axis_size("fsdp")
    fsdp_place = lax.axis_index("fsdp")
    key_count = PROMPT + CONT
    score_scale = HEAD_DIM ** (-0.5)
    select_gain = 4.0 / (PROMPT + CONT)
    query_pos = jnp.concatenate(
        [
            fsdp_place * prompt_rows + jnp.arange(prompt_rows, dtype=jnp.int32),
            PROMPT + jnp.arange(CONT, dtype=jnp.int32),
        ]
    )
    key_pos = jnp.arange(key_count, dtype=jnp.int32)
    causal = key_pos[None, :] <= query_pos[:, None]
    chosen = (key_pos[None, :] < query_pos[:, None]) & (key_pos[None, :] > 0)
    lower_mask = (jnp.arange(fsdp_count, dtype=jnp.int32) < fsdp_place).astype(jnp.float32)
    pad_zeros = jnp.zeros((groups_here, CONT), jnp.float32)
    forward_attend = partial(attend_group, causal=causal, score_scale=score_scale)
    backward_attend = partial(attend_back, causal=causal, score_scale=score_scale)
    totals = tuple(
        (
            jnp.zeros(
                (single.shape[0] * lax.axis_size(("dp", "fsdp")),) + single.shape[1:], jnp.float32
            )
            for single in shards
        )
    )
    outputs_yp, outputs_yc, outputs_dxp, outputs_dxc = ([], [], [], [])
    for batch_index in range(MICRO):
        gathered = (
            lax.all_gather(shards[0], ("dp", "fsdp"), axis=0, tiled=True),
            lax.all_gather(shards[1], ("dp", "fsdp"), axis=0, tiled=True),
            lax.all_gather(shards[2], ("dp", "fsdp"), axis=0, tiled=True),
            lax.all_gather(shards[3], ("dp", "fsdp"), axis=0, tiled=True),
            lax.all_gather(shards[4], ("dp", "fsdp"), axis=0, tiled=True),
            lax.all_gather(shards[5], ("dp", "fsdp"), axis=0, tiled=True),
            lax.all_gather(shards[6], ("dp", "fsdp"), axis=0, tiled=True),
            lax.all_gather(shards[7], ("dp", "fsdp"), axis=0, tiled=True),
            lax.all_gather(shards[8], ("dp", "fsdp"), axis=0, tiled=True),
            lax.all_gather(shards[9], ("dp", "fsdp"), axis=0, tiled=True),
            lax.all_gather(shards[10], ("dp", "fsdp"), axis=0, tiled=True),
            lax.all_gather(shards[11], ("dp", "fsdp"), axis=0, tiled=True),
        )
        inputs_x = jnp.concatenate([x_prompt[batch_index], x_cont[batch_index][:, 0]], 1).astype(
            jnp.float32
        )
        local_rows = inputs_x.shape[1]
        flat_x = inputs_x.reshape(-1, D)
        normed_one = normalize(
            flat_x, gathered[0].astype(jnp.float32), gathered[1].astype(jnp.float32)
        ).astype(jnp.bfloat16)
        joined = jnp.dot(normed_one, gathered[2], preferred_element_type=jnp.float32)
        bias_qv = gathered[3].astype(jnp.float32)
        queries = (
            (joined[:, :D] + bias_qv[:D]).astype(jnp.bfloat16).reshape(groups_here, local_rows, D)
        )
        keys_own = joined[:, D : 2 * D].astype(jnp.bfloat16).reshape(groups_here, local_rows, D)
        values_own = (
            (joined[:, 2 * D :] + bias_qv[D:])
            .astype(jnp.bfloat16)
            .reshape(groups_here, local_rows, D)
        )
        prompt_pair = jnp.concatenate([keys_own[:, :prompt_rows], values_own[:, :prompt_rows]], 2)
        whole_kv = lax.all_gather(prompt_pair, "fsdp", axis=1, tiled=True)
        keys_all = jnp.concatenate([whole_kv[..., :D], keys_own[:, prompt_rows:]], 1)
        values_all = jnp.concatenate([whole_kv[..., D:], values_own[:, prompt_rows:]], 1)
        score_zero = (
            jnp.einsum(
                "grd,gkd->grk",
                queries[..., :HEAD_DIM],
                keys_all[..., :HEAD_DIM],
                preferred_element_type=jnp.float32,
            )
            * score_scale
        )
        select = jnp.where(chosen[None], jnp.maximum(score_zero, 0.0), 0.0)
        own_part = jnp.sum(select[:, :prompt_rows, :PROMPT], 1)
        all_parts = lax.all_gather(own_part[None], "fsdp", axis=0, tiled=True)
        prefix = jnp.sum(all_parts * lower_mask[:, None, None], 0)
        whole_sum = jnp.sum(all_parts, 0)
        select_p = select[:, :prompt_rows]
        select_c = select[:, prompt_rows:]
        penalty = select_gain * jnp.concatenate(
            [
                jnp.concatenate([prefix, pad_zeros], 1)[:, None]
                + (jnp.cumsum(select_p, 1) - select_p),
                jnp.concatenate([whole_sum, pad_zeros], 1)[:, None]
                + (jnp.cumsum(select_c, 1) - select_c),
            ],
            1,
        )
        mixture, log_totals = lax.map(forward_attend, (queries, keys_all, values_all, penalty))
        mixed_flat = mixture.reshape(-1, D)
        residual = flat_x + (
            jnp.dot(mixed_flat, gathered[4], preferred_element_type=jnp.float32)
            + gathered[5].astype(jnp.float32)
        )
        normed_two = normalize(
            residual, gathered[6].astype(jnp.float32), gathered[7].astype(jnp.float32)
        ).astype(jnp.bfloat16)
        upward = jnp.dot(normed_two, gathered[8], preferred_element_type=jnp.float32) + gathered[
            9
        ].astype(jnp.float32)
        active, gelu_back = jax.vjp(partial(jax.nn.gelu, approximate=True), upward)
        active_b = active.astype(jnp.bfloat16)
        output = residual + (
            jnp.dot(active_b, gathered[10], preferred_element_type=jnp.float32)
            + gathered[11].astype(jnp.float32)
        )
        output_b = output.astype(jnp.bfloat16).reshape(groups_here, local_rows, D)
        outputs_yp.append(output_b[:, :prompt_rows])
        outputs_yc.append(output_b[:, prompt_rows:][:, None])
        back_set = (
            lax.all_gather(shards[0], ("dp", "fsdp"), axis=0, tiled=True),
            lax.all_gather(shards[1], ("dp", "fsdp"), axis=0, tiled=True),
            lax.all_gather(shards[2], ("dp", "fsdp"), axis=0, tiled=True),
            lax.all_gather(shards[3], ("dp", "fsdp"), axis=0, tiled=True),
            lax.all_gather(shards[4], ("dp", "fsdp"), axis=0, tiled=True),
            lax.all_gather(shards[5], ("dp", "fsdp"), axis=0, tiled=True),
            lax.all_gather(shards[6], ("dp", "fsdp"), axis=0, tiled=True),
            lax.all_gather(shards[7], ("dp", "fsdp"), axis=0, tiled=True),
            lax.all_gather(shards[8], ("dp", "fsdp"), axis=0, tiled=True),
            lax.all_gather(shards[9], ("dp", "fsdp"), axis=0, tiled=True),
            lax.all_gather(shards[10], ("dp", "fsdp"), axis=0, tiled=True),
            lax.all_gather(shards[11], ("dp", "fsdp"), axis=0, tiled=True),
        )
        grad_out_y = jnp.concatenate(
            [dy_prompt[batch_index], dy_cont[batch_index][:, 0]], 1
        ).reshape(-1, D)
        grad_down = jnp.einsum(
            "rf,rd->fd", active_b, grad_out_y, preferred_element_type=jnp.float32
        )
        grad_bdown = jnp.sum(grad_out_y.astype(jnp.float32), 0)
        grad_active = jnp.einsum(
            "rd,fd->rf", grad_out_y, back_set[10], preferred_element_type=jnp.float32
        )
        grad_upward = gelu_back(grad_active)[0].astype(jnp.bfloat16)
        grad_up = jnp.einsum(
            "rd,rf->df", normed_two, grad_upward, preferred_element_type=jnp.float32
        )
        grad_bup = jnp.sum(grad_upward.astype(jnp.float32), 0)
        grad_normed = jnp.einsum(
            "rf,df->rd", grad_upward, back_set[8], preferred_element_type=jnp.float32
        )
        unused, norm_back = jax.vjp(
            normalize, residual, back_set[6].astype(jnp.float32), back_set[7].astype(jnp.float32)
        )
        grad_resid, grad_gain_two, grad_shift_two = norm_back(grad_normed)
        grad_resid = grad_out_y.astype(jnp.float32) + grad_resid
        grad_branch = grad_resid.astype(jnp.bfloat16)
        grad_wout = jnp.einsum(
            "rd,re->de", mixed_flat, grad_branch, preferred_element_type=jnp.float32
        )
        grad_bout = jnp.sum(grad_branch.astype(jnp.float32), 0)
        grad_mixed = jnp.einsum(
            "re,de->rd", grad_branch, back_set[4], preferred_element_type=jnp.float32
        )
        grad_mixed = grad_mixed.astype(jnp.bfloat16).reshape(groups_here, local_rows, D)
        back_values, back_queries, back_keys, back_zero, back_penalty = lax.map(
            backward_attend, (queries, keys_all, values_all, penalty, grad_mixed, log_totals)
        )
        prefix_grad = select_gain * jnp.sum(back_penalty[:, :prompt_rows, :PROMPT], 1)
        whole_grad = select_gain * jnp.sum(back_penalty[:, prompt_rows:, :PROMPT], 1)
        spread_back = prefix_grad[None] * lower_mask[:, None, None] + whole_grad[None]
        part_grad = lax.psum_scatter(spread_back, "fsdp", scatter_dimension=0, tiled=True)[0]
        select_back = jnp.concatenate(
            [
                select_gain * later_sum(back_penalty[:, :prompt_rows])
                + jnp.concatenate([part_grad, pad_zeros], 1)[:, None],
                select_gain * later_sum(back_penalty[:, prompt_rows:]),
            ],
            1,
        )
        grad_zero = (
            back_zero + jnp.where(chosen[None] & (score_zero > 0), select_back, 0.0)
        ).astype(jnp.bfloat16)
        query_zero = (
            jnp.einsum(
                "grk,gkd->grd",
                grad_zero,
                keys_all[..., :HEAD_DIM],
                preferred_element_type=jnp.float32,
            )
            * score_scale
        )
        key_zero = (
            jnp.einsum(
                "grk,grd->gkd",
                grad_zero,
                queries[..., :HEAD_DIM],
                preferred_element_type=jnp.float32,
            )
            * score_scale
        )
        grad_queries = jnp.concatenate([query_zero, back_queries], 2)
        grad_keys = jnp.concatenate([key_zero, back_keys], 2)
        prompt_back = jnp.concatenate([grad_keys[:, :PROMPT], back_values[:, :PROMPT]], 2)
        own_back = lax.psum_scatter(
            prompt_back.astype(jnp.bfloat16), "fsdp", scatter_dimension=1, tiled=True
        ).astype(jnp.float32)
        keys_back = jnp.concatenate([own_back[..., :D], grad_keys[:, PROMPT:]], 1)
        values_back = jnp.concatenate([own_back[..., D:], back_values[:, PROMPT:]], 1)
        grad_joined = (
            jnp.concatenate([grad_queries, keys_back, values_back], 2)
            .astype(jnp.bfloat16)
            .reshape(-1, 3 * D)
        )
        grad_wqkv = jnp.einsum(
            "rd,re->de", normed_one, grad_joined, preferred_element_type=jnp.float32
        )
        grad_bqv = jnp.concatenate(
            [
                jnp.sum(grad_joined[:, :D].astype(jnp.float32), 0),
                jnp.sum(grad_joined[:, 2 * D :].astype(jnp.float32), 0),
            ]
        )
        grad_normed_one = jnp.einsum(
            "re,de->rd", grad_joined, back_set[2], preferred_element_type=jnp.float32
        )
        unused_one, norm_back_one = jax.vjp(
            normalize, flat_x, back_set[0].astype(jnp.float32), back_set[1].astype(jnp.float32)
        )
        grad_input, grad_gain_one, grad_shift_one = norm_back_one(grad_normed_one)
        grad_input = (grad_resid + grad_input).reshape(groups_here, local_rows, D)
        outputs_dxp.append(grad_input[:, :prompt_rows])
        outputs_dxc.append(grad_input[:, prompt_rows:][:, None])
        micro_grads = (
            grad_gain_one,
            grad_shift_one,
            grad_wqkv,
            grad_bqv,
            grad_wout,
            grad_bout,
            grad_gain_two,
            grad_shift_two,
            grad_up,
            grad_bup,
            grad_down,
            grad_bdown,
        )
        totals = tuple((first + second for first, second in zip(totals, micro_grads)))
    results = (
        lax.psum_scatter(totals[0], ("dp", "fsdp"), scatter_dimension=0, tiled=True),
        lax.psum_scatter(totals[1], ("dp", "fsdp"), scatter_dimension=0, tiled=True),
        lax.psum_scatter(totals[2], ("dp", "fsdp"), scatter_dimension=0, tiled=True),
        lax.psum_scatter(totals[3], ("dp", "fsdp"), scatter_dimension=0, tiled=True),
        lax.psum_scatter(totals[4], ("dp", "fsdp"), scatter_dimension=0, tiled=True),
        lax.psum_scatter(totals[5], ("dp", "fsdp"), scatter_dimension=0, tiled=True),
        lax.psum_scatter(totals[6], ("dp", "fsdp"), scatter_dimension=0, tiled=True),
        lax.psum_scatter(totals[7], ("dp", "fsdp"), scatter_dimension=0, tiled=True),
        lax.psum_scatter(totals[8], ("dp", "fsdp"), scatter_dimension=0, tiled=True),
        lax.psum_scatter(totals[9], ("dp", "fsdp"), scatter_dimension=0, tiled=True),
        lax.psum_scatter(totals[10], ("dp", "fsdp"), scatter_dimension=0, tiled=True),
        lax.psum_scatter(totals[11], ("dp", "fsdp"), scatter_dimension=0, tiled=True),
    )
    return (
        jnp.stack(outputs_yp),
        jnp.stack(outputs_yc),
        jnp.stack(outputs_dxp),
        jnp.stack(outputs_dxc),
        results[0],
        results[1],
        results[2],
        results[3],
        results[4],
        results[5],
        results[6],
        results[7],
        results[8],
        results[9],
        results[10],
        results[11],
    )


NCONT = 2
ROWS = PROMPT + NCONT * CONT
SEQ = PROMPT + CONT
SCALE = HEAD_DIM ** (-0.5)
SELECT_GAIN = 4.0 / SEQ
PAIR = 2 * HEAD_DIM
BLOCKS = ((0, 256, 256), (256, 256, 512), (512, 256, 768), (768, 256, 1024), (1024, 64, ROWS))
TAIL = PROMPT - 768
F32 = jnp.float32
B16 = jnp.bfloat16


def mm(a, b):
    return lax.dot_general(a, b, (((1,), (0,)), ((), ())), preferred_element_type=F32)


def mm_nt(a, b):
    return lax.dot_general(a, b, (((1,), (1,)), ((), ())), preferred_element_type=F32)


def masked_half(values, half):
    lane = lax.broadcasted_iota(jnp.int32, values.shape, 1)
    return jnp.where(lane // HEAD_DIM == half, values, 0.0).astype(B16)


def block_masks(place):
    first, rows, keys = BLOCKS[place]
    key_id = lax.broadcasted_iota(jnp.int32, (keys, rows), 0)
    row_id = first + lax.broadcasted_iota(jnp.int32, (keys, rows), 1)
    visible = key_id <= row_id
    if first >= SEQ:
        visible = visible & ((key_id < PROMPT) | (key_id >= SEQ))
    chosen = visible & (key_id < row_id) & (key_id > 0)
    return visible, chosen


def split_mm(values, ones):
    high = values.astype(B16)
    low = (values - high.astype(F32)).astype(B16)
    return mm(high, ones) + mm(low, ones)


def triangle(rows, later):
    a = lax.broadcasted_iota(jnp.int32, (rows, rows), 0)
    b = lax.broadcasted_iota(jnp.int32, (rows, rows), 1)
    return jnp.where((a > b) if later else (a < b), 1.0, 0.0).astype(B16)


def forward_kernel(q_ref, k_ref, v_ref, o_ref, lse_ref, b0, b1, b2, b3, b4, vt_ref, ot_ref):
    bias_refs = (b0, b1, b2, b3, b4)
    head = pl.program_id(0)
    half = head % 2
    queries = masked_half(q_ref[...].astype(F32) * SCALE, half)

    @pl.when(head == 0)
    def _():
        carry = None
        for place, (first, rows, keys) in enumerate(BLOCKS):
            scores = mm_nt(k_ref[:keys], queries[first : first + rows])
            visible, chosen = block_masks(place)
            select = jnp.where(chosen, jnp.maximum(scores, 0.0), 0.0)
            penalty = split_mm(select, triangle(rows, False))
            if carry is not None:
                grown = jnp.zeros((keys - carry.shape[0], 1), F32)
                penalty = penalty + jnp.concatenate([carry, grown], 0)
            bias_refs[place][...] = jnp.where(visible, -SELECT_GAIN * penalty, NEG)
            if first + rows == SEQ:
                lane = lax.broadcasted_iota(jnp.int32, select.shape, 1)
                select = jnp.where(lane < TAIL, select, 0.0)
            if place + 1 < len(BLOCKS):
                total = jnp.sum(select, 1, keepdims=True)
                if carry is not None:
                    total = total + jnp.concatenate([carry, grown], 0)
                carry = total

    @pl.when(half == 0)
    def _():
        vt_ref[...] = v_ref[...].astype(F32).T.astype(B16)

    own = pl.ds(pl.multiple_of(half * HEAD_DIM, HEAD_DIM), HEAD_DIM)
    for place, (first, rows, keys) in enumerate(BLOCKS):
        logits = mm_nt(k_ref[:keys], queries[first : first + rows]) + bias_refs[place][...]
        highest = jnp.max(logits, 0, keepdims=True)
        raised = jnp.exp(logits - highest)
        total = jnp.sum(raised, 0, keepdims=True)
        mixed = mm(vt_ref[own, :keys], raised.astype(B16))
        ot_ref[own, first : first + rows] = mixed * (1.0 / total)
        lse_ref[0, :, first : first + rows] = highest + jnp.log(total)

    @pl.when(half == 1)
    def _():
        o_ref[...] = ot_ref[...].T.astype(B16)


def backward_kernel(
    q_ref, k_ref, v_ref, g_ref, lse_ref, b0, b1, b2, b3, b4,
    dq_ref, dk_ref, dv_ref,
    kt_ref, dqt_ref, dk_acc, dv_acc, p0, p1, p2, p3, p4,
):
    bias_refs = (b0, b1, b2, b3, b4)
    pen_refs = (p0, p1, p2, p3, p4)
    head = HEADS - 1 - pl.program_id(0)
    half = head % 2
    queries = masked_half(q_ref[...].astype(F32) * SCALE, half)
    grads = masked_half(g_ref[...].astype(F32), half)
    own = pl.ds(pl.multiple_of(half * HEAD_DIM, HEAD_DIM), HEAD_DIM)

    @pl.when(head == HEADS - 1)
    def _():
        for pen in pen_refs:
            pen[...] = jnp.zeros_like(pen)

    @pl.when(half == 1)
    def _():
        kt_ref[...] = k_ref[...].astype(F32).T.astype(B16)
        dk_acc[...] = jnp.zeros_like(dk_acc)
        dv_acc[...] = jnp.zeros_like(dv_acc)

    def softmax_grad(place):
        first, rows, keys = BLOCKS[place]
        scores = mm_nt(k_ref[:keys], queries[first : first + rows])
        shares = jnp.exp(scores + bias_refs[place][...] - lse_ref[0, :, first : first + rows])
        back = mm_nt(v_ref[:keys], grads[first : first + rows])
        inner = jnp.sum(shares * back, 0, keepdims=True)
        dv_acc[:keys] += mm(shares.astype(B16), grads[first : first + rows])
        return scores, shares * (back - inner)

    def score_grad(place, grad):
        first, rows, keys = BLOCKS[place]
        grad = grad.astype(B16)
        dqt_ref[own, first : first + rows] = mm(kt_ref[own, :keys], grad)
        dk_acc[:keys] += mm(grad, queries[first : first + rows])

    @pl.when(head != 0)
    def _():
        for place in range(len(BLOCKS)):
            _, grad = softmax_grad(place)
            pen_refs[place][...] += grad
            score_grad(place, grad)

    @pl.when(head == 0)
    def _():
        carry = None
        for place in reversed(range(len(BLOCKS))):
            first, rows, keys = BLOCKS[place]
            scores, grad = softmax_grad(place)
            whole = pen_refs[place][...] + grad
            later = split_mm(whole, triangle(rows, True))
            total = jnp.sum(whole, 1, keepdims=True)
            if carry is not None:
                if first + rows == SEQ:
                    lane = lax.broadcasted_iota(jnp.int32, (keys, rows), 1)
                    later = later + jnp.where(lane < TAIL, carry[:keys], 0.0)
                else:
                    later = later + carry[:keys]
                total = total + carry[:keys]
            carry = total
            _, chosen = block_masks(place)
            grad = grad + jnp.where(chosen & (scores > 0.0), -SELECT_GAIN * later, 0.0)
            score_grad(place, grad)

    @pl.when(half == 0)
    def _():
        dq_ref[...] = (dqt_ref[...].T * SCALE).astype(B16)
        dk_ref[...] = dk_acc[...].astype(B16)
        dv_ref[...] = dv_acc[...].astype(B16)


def pair_spec(index):
    return pl.BlockSpec((ROWS, PAIR), index)


def whole_specs():
    return [pl.BlockSpec((keys, rows), lambda i: (0, 0)) for _, rows, keys in BLOCKS]


PAIRS = HEADS // 2


def attend_forward(joined):
    return pl.pallas_call(
        forward_kernel,
        grid=(HEADS,),
        in_specs=[
            pair_spec(lambda i: (0, i // 2)),
            pair_spec(lambda i: (0, PAIRS + i // 2)),
            pair_spec(lambda i: (0, 2 * PAIRS + i // 2)),
        ],
        out_specs=[
            pair_spec(lambda i: (0, i // 2)),
            pl.BlockSpec((1, 1, ROWS), lambda i: (i, 0, 0)),
            *whole_specs(),
        ],
        out_shape=[
            jax.ShapeDtypeStruct((ROWS, D), B16),
            jax.ShapeDtypeStruct((HEADS, 1, ROWS), F32),
            *(jax.ShapeDtypeStruct((keys, rows), F32) for _, rows, keys in BLOCKS),
        ],
        scratch_shapes=[pltpu.VMEM((PAIR, ROWS), B16), pltpu.VMEM((PAIR, ROWS), F32)],
        name="attend_forward",
    )(joined, joined, joined)


def attend_backward(joined, grad_mixed, lse, biases):
    last = PAIRS - 1
    return pl.pallas_call(
        backward_kernel,
        grid=(HEADS,),
        in_specs=[
            pair_spec(lambda i: (0, last - i // 2)),
            pair_spec(lambda i: (0, PAIRS + last - i // 2)),
            pair_spec(lambda i: (0, 2 * PAIRS + last - i // 2)),
            pair_spec(lambda i: (0, last - i // 2)),
            pl.BlockSpec((1, 1, ROWS), lambda i: (HEADS - 1 - i, 0, 0)),
            *whole_specs(),
        ],
        out_specs=[pair_spec(lambda i: (0, last - i // 2)) for _ in range(3)],
        out_shape=[jax.ShapeDtypeStruct((ROWS, D), B16) for _ in range(3)],
        scratch_shapes=[
            pltpu.VMEM((PAIR, ROWS), B16),
            pltpu.VMEM((PAIR, ROWS), F32),
            pltpu.VMEM((ROWS, PAIR), F32),
            pltpu.VMEM((ROWS, PAIR), F32),
            *(pltpu.VMEM((keys, rows), F32) for _, rows, keys in BLOCKS),
        ],
        name="attend_backward",
    )(joined, joined, joined, grad_mixed, lse, *biases)


def axis_bits():
    bits = []
    for axis in ("dp", "fsdp"):
        mask = lax.axis_size(axis) // 2
        while mask:
            bits.append((axis, mask))
            mask //= 2
    return bits


def swap(value, bit):
    axis, mask = bit
    size = lax.axis_size(axis)
    return lax.ppermute(value, axis, [(i, i ^ mask) for i in range(size)])


def own_bit(bit):
    axis, mask = bit
    return (lax.axis_index(axis) // mask) % 2


def split_orders(bits):
    core, others, y = bits[-2], bits[:-2], bits[-1]
    x, far = others[-1:], others[:-1][::-1]
    return [core, y, *x, *far], [core, *x, y, *far]


def gather_steps(shard, bits, order):
    value = shard.reshape((1,) * len(bits) + shard.shape)
    for bit in order:
        value = join(value, swap(value, bit), bit, bits)
    return value


def join(value, other, bit, bits):
    place = bits.index(bit)
    low = own_bit(bit) == 0
    first = jnp.where(low, value, other)
    second = jnp.where(low, other, value)
    return jnp.concatenate([first, second], place)


def gather_weight(shard):
    bits = axis_bits()
    orders = [order[::-1] for order in split_orders(bits)]
    width = shard.shape[1] // 2
    parts = [
        gather_steps(shard[:, i * width : (i + 1) * width], bits, orders[i][:-1]) for i in range(2)
    ]
    value = jnp.concatenate(parts, -1)
    value = join(value, swap(value, orders[0][-1]), orders[0][-1], bits)
    return value.reshape(-1, shard.shape[1])


def halve(value, bit, bits, last=False):
    place = bits.index(bit)
    mine = own_bit(bit)
    keep = lax.dynamic_index_in_dim(value, mine, place, keepdims=True)
    send = lax.dynamic_index_in_dim(value, 1 - mine, place, keepdims=True)
    other = swap(send, bit)
    if last:
        return keep.astype(F32) + other.astype(F32)
    return keep + other


def scatter_grad(grad):
    bits = axis_bits()
    orders = split_orders(bits)
    count = 2 ** len(bits)
    value = grad.reshape((2,) * len(bits) + (grad.shape[0] // count, grad.shape[1]))
    value = halve(value, orders[0][0], bits)
    width = grad.shape[1] // 2
    parts = []
    for i in range(2):
        part = value[..., i * width : (i + 1) * width]
        for bit in orders[i][1:]:
            part = halve(part, bit, bits, last=bit == orders[i][-1])
        parts.append(part)
    return jnp.concatenate(parts, -1).reshape(-1, grad.shape[1])


def scatter_small(rows):
    bits = axis_bits()
    value = rows.reshape((2,) * len(bits) + (1, rows.shape[1]))
    for bit in split_orders(bits)[0]:
        value = halve(value, bit, bits)
    return value.reshape(-1)


def pick(first, second, when):
    return jnp.where(when, first, second)


def trade_rows(prompt, cont):
    place = lax.axis_index("fsdp")
    low = place == 0
    swap_pairs = [(0, 1), (1, 0)]
    mine = [pick(t[0], t[1], low).reshape(-1, D) for t in (prompt, cont)]
    away = [pick(t[1], t[0], low).reshape(-1, D) for t in (prompt, cont)]
    came = lax.ppermute(jnp.concatenate(away, 0), "fsdp", swap_pairs)
    half = mine[0].shape[0]
    parts = (came[:half], came[half:])
    return jnp.concatenate(
        [
            pick(mine[0], parts[0], low),
            pick(parts[0], mine[0], low),
            pick(mine[1], parts[1], low),
            pick(parts[1], mine[1], low),
        ],
        0,
    )


def return_rows(whole, kind):
    place = lax.axis_index("fsdp")
    low = place == 0
    half = PROMPT // 2
    parts = (
        (whole[:half], whole[PROMPT:SEQ]),
        (whole[half:PROMPT], whole[SEQ:]),
    )
    mine = [pick(parts[0][i], parts[1][i], low) for i in range(2)]
    away = [pick(parts[1][i], parts[0][i], low) for i in range(2)]
    came = lax.ppermute(jnp.concatenate(away, 0).astype(B16), "fsdp", [(0, 1), (1, 0)])
    came = (came[:half], came[half:])
    out = []
    for i in range(2):
        own, other = mine[i].astype(kind), came[i].astype(kind)
        out.append(jnp.stack([pick(own, other, low), pick(other, own, low)]))
    return out[0][:, None], out[1][:, None, None]


def whole_layer(
    x_prompt, x_cont, dy_prompt, dy_cont,
    ln1_gain, ln1_bias, w_qkv, b_qv, w_out, b_out,
    ln2_gain, ln2_bias, w_up, b_up, w_down, b_down,
):
    bits = axis_bits()
    devices = 2 ** len(bits)
    vectors = (ln1_gain, ln1_bias, b_qv, b_out, ln2_gain, ln2_bias, b_up, b_down)
    sizes = [v.shape[0] for v in vectors]
    packed = gather_steps(
        jnp.concatenate(vectors)[None], bits, split_orders(bits)[0][::-1]
    ).reshape(devices, -1)
    whole_vectors, start = [], 0
    for size in sizes:
        whole_vectors.append(packed[:, start : start + size].reshape(-1).astype(F32))
        start += size
    gain_one, shift_one, bias_qv, bias_out, gain_two, shift_two, bias_up, bias_down = whole_vectors

    flat_x = trade_rows(x_prompt, x_cont).astype(F32)
    full_qkv = gather_weight(w_qkv)
    full_out = gather_weight(w_out)
    full_up = gather_weight(w_up)
    full_down = gather_weight(w_down)
    grad_y = trade_rows(dy_prompt, dy_cont)

    normed_one = normalize(flat_x, gain_one, shift_one).astype(B16)
    bias_joined = jnp.concatenate([bias_qv[:D], jnp.zeros((D,), F32), bias_qv[D:]])
    joined = (
        jnp.dot(normed_one, full_qkv, preferred_element_type=F32) + bias_joined
    ).astype(B16)
    mixed, lse, *biases = attend_forward(joined)
    residual = flat_x + (jnp.dot(mixed, full_out, preferred_element_type=F32) + bias_out)
    normed_two = normalize(residual, gain_two, shift_two).astype(B16)
    upward = jnp.dot(normed_two, full_up, preferred_element_type=F32) + bias_up
    active, gelu_back = jax.vjp(partial(jax.nn.gelu, approximate=True), upward)
    active = active.astype(B16)
    output = residual + (jnp.dot(active, full_down, preferred_element_type=F32) + bias_down)
    y_prompt, y_cont = return_rows(output.astype(B16), B16)

    def weight_grad(left, right):
        return jnp.einsum("rd,re->de", left, right, preferred_element_type=F32).astype(B16)

    def through(grad, weight):
        return jnp.einsum("re,de->rd", grad, weight, preferred_element_type=F32)

    def column_sum(values):
        return jnp.sum(values.astype(F32), 0)

    grad_w_down = scatter_grad(weight_grad(active, grad_y))
    grad_b_down = column_sum(grad_y)
    grad_upward = gelu_back(through(grad_y, full_down))[0].astype(B16)
    grad_w_up = scatter_grad(weight_grad(normed_two, grad_upward))
    grad_b_up = column_sum(grad_upward)
    _, norm_back = jax.vjp(normalize, residual, gain_two, shift_two)
    grad_resid, grad_gain_two, grad_shift_two = norm_back(through(grad_upward, full_up))
    grad_resid = grad_y.astype(F32) + grad_resid
    grad_branch = grad_resid.astype(B16)
    grad_w_out = scatter_grad(weight_grad(mixed, grad_branch))
    grad_b_out = column_sum(grad_branch)
    grad_mixed = through(grad_branch, full_out).astype(B16)
    grad_joined = jnp.concatenate(attend_backward(joined, grad_mixed, lse, biases), 1)
    grad_w_qkv = scatter_grad(weight_grad(normed_one, grad_joined))
    grad_b_qv = jnp.concatenate(
        [column_sum(grad_joined[:, :D]), column_sum(grad_joined[:, 2 * D :])]
    )
    _, norm_back_one = jax.vjp(normalize, flat_x, gain_one, shift_one)
    grad_input, grad_gain_one, grad_shift_one = norm_back_one(through(grad_joined, full_qkv))
    dx_prompt, dx_cont = return_rows(grad_resid + grad_input, F32)

    small = (
        grad_gain_one, grad_shift_one, grad_b_qv, grad_b_out,
        grad_gain_two, grad_shift_two, grad_b_up, grad_b_down,
    )
    own_small = scatter_small(jnp.concatenate([v.reshape(devices, -1) for v in small], 1))
    pieces, start = [], 0
    for size in sizes:
        pieces.append(own_small[start : start + size])
        start += size
    return (
        y_prompt, y_cont, dx_prompt, dx_cont,
        pieces[0], pieces[1], grad_w_qkv, pieces[2], grad_w_out, pieces[3],
        pieces[4], pieces[5], grad_w_up, pieces[6], grad_w_down, pieces[7],
    )


def solution(mesh):
    sizes = dict(mesh.shape)
    whole = sizes["fsdp"] == MICRO == NCONT and sizes["dp"] & (sizes["dp"] - 1) == 0
    return jax.shard_map(
        whole_layer if whole else spread_layer,
        mesh=mesh,
        in_specs=(
            P(None, "dp", "fsdp", None),
            P(None, "dp", "fsdp", None, None),
            P(None, "dp", "fsdp", None),
            P(None, "dp", "fsdp", None, None),
            P(("dp", "fsdp")),
            P(("dp", "fsdp")),
            P(("dp", "fsdp"), None),
            P(("dp", "fsdp")),
            P(("dp", "fsdp"), None),
            P(("dp", "fsdp")),
            P(("dp", "fsdp")),
            P(("dp", "fsdp")),
            P(("dp", "fsdp"), None),
            P(("dp", "fsdp")),
            P(("dp", "fsdp"), None),
            P(("dp", "fsdp")),
        ),
        out_specs=(
            P(None, "dp", "fsdp", None),
            P(None, "dp", "fsdp", None, None),
            P(None, "dp", "fsdp", None),
            P(None, "dp", "fsdp", None, None),
            P(("dp", "fsdp")),
            P(("dp", "fsdp")),
            P(("dp", "fsdp"), None),
            P(("dp", "fsdp")),
            P(("dp", "fsdp"), None),
            P(("dp", "fsdp")),
            P(("dp", "fsdp")),
            P(("dp", "fsdp")),
            P(("dp", "fsdp"), None),
            P(("dp", "fsdp")),
            P(("dp", "fsdp"), None),
            P(("dp", "fsdp")),
        ),
        check_vma=False,
    )
```

```python
from functools import partial

import jax
import jax.numpy as jnp
from jax import lax
from jax.experimental import pallas as pl
from jax.experimental.pallas import tpu as pltpu
from jax.sharding import PartitionSpec as P

D = 768
HEADS = 12
HEAD_DIM = 64
PROMPT = 960
CONT = 64
MICRO = 2


EPS = 1e-05
NEG = -1e30


def normalize(values, gain, shift):
    center = values - jnp.mean(values, -1, keepdims=True)
    spread = jnp.mean(center * center, -1, keepdims=True)
    return center * lax.rsqrt(spread + EPS) * gain + shift


def later_sum(values):
    return jnp.flip(jnp.cumsum(jnp.flip(values, 1), 1), 1) - values


def attend_group(inputs_g, causal, score_scale):
    query_g, key_g, value_g, penalty_g = inputs_g
    rows_here = query_g.shape[0]
    heads_q = query_g.reshape(rows_here, HEADS, HEAD_DIM)
    heads_k = key_g.reshape(-1, HEADS, HEAD_DIM)
    heads_v = value_g.reshape(-1, HEADS, HEAD_DIM)
    scores = (
        jnp.einsum("rhd,khd->hrk", heads_q, heads_k, preferred_element_type=jnp.float32)
        * score_scale
    )
    logits = jnp.where(causal[None], scores - penalty_g[None], NEG)
    highest = jnp.max(logits, -1, keepdims=True)
    raised = jnp.exp(logits - highest)
    totals = jnp.sum(raised, -1, keepdims=True)
    weights_b = (raised / totals).astype(jnp.bfloat16)
    mixture = jnp.einsum("hrk,khd->rhd", weights_b, heads_v, preferred_element_type=jnp.float32)
    return (
        mixture.reshape(rows_here, -1).astype(jnp.bfloat16),
        (highest + jnp.log(totals))[..., 0],
    )


def attend_back(inputs_g, causal, score_scale):
    query_g, key_g, value_g, penalty_g, grad_mix, log_totals = inputs_g
    rows_here = query_g.shape[0]
    heads_q = query_g.reshape(rows_here, HEADS, HEAD_DIM)
    heads_k = key_g.reshape(-1, HEADS, HEAD_DIM)
    heads_v = value_g.reshape(-1, HEADS, HEAD_DIM)
    heads_g = grad_mix.reshape(rows_here, HEADS, HEAD_DIM)
    scores = (
        jnp.einsum("rhd,khd->hrk", heads_q, heads_k, preferred_element_type=jnp.float32)
        * score_scale
    )
    logits = jnp.where(causal[None], scores - penalty_g[None], NEG)
    softmax_w = jnp.exp(logits - log_totals[..., None])
    grad_soft = jnp.einsum("rhd,khd->hrk", heads_g, heads_v, preferred_element_type=jnp.float32)
    inner_sum = jnp.sum(softmax_w * grad_soft, -1, keepdims=True)
    grad_logit = softmax_w * (grad_soft - inner_sum)
    grad_value = jnp.einsum(
        "hrk,rhd->khd", softmax_w.astype(jnp.bfloat16), heads_g, preferred_element_type=jnp.float32
    )
    grad_penalty = -jnp.sum(grad_logit, 0)
    rest_b = grad_logit[1:].astype(jnp.bfloat16)
    grad_query = (
        jnp.einsum("hrk,khd->rhd", rest_b, heads_k[:, 1:], preferred_element_type=jnp.float32)
        * score_scale
    )
    grad_key = (
        jnp.einsum("hrk,rhd->khd", rest_b, heads_q[:, 1:], preferred_element_type=jnp.float32)
        * score_scale
    )
    return (
        grad_value.reshape(-1, D),
        grad_query.reshape(rows_here, -1),
        grad_key.reshape(grad_key.shape[0], -1),
        grad_logit[0],
        grad_penalty,
    )


def spread_layer(
    x_prompt,
    x_cont,
    dy_prompt,
    dy_cont,
    ln1_gain,
    ln1_bias,
    w_qkv,
    b_qv,
    w_out,
    b_out,
    ln2_gain,
    ln2_bias,
    w_up,
    b_up,
    w_down,
    b_down,
):
    shards = (
        ln1_gain,
        ln1_bias,
        w_qkv,
        b_qv,
        w_out,
        b_out,
        ln2_gain,
        ln2_bias,
        w_up,
        b_up,
        w_down,
        b_down,
    )
    groups_here = x_prompt.shape[1]
    prompt_rows = x_prompt.shape[2]
    fsdp_count = lax.axis_size("fsdp")
    fsdp_place = lax.axis_index("fsdp")
    key_count = PROMPT + CONT
    score_scale = HEAD_DIM ** (-0.5)
    select_gain = 4.0 / (PROMPT + CONT)
    query_pos = jnp.concatenate(
        [
            fsdp_place * prompt_rows + jnp.arange(prompt_rows, dtype=jnp.int32),
            PROMPT + jnp.arange(CONT, dtype=jnp.int32),
        ]
    )
    key_pos = jnp.arange(key_count, dtype=jnp.int32)
    causal = key_pos[None, :] <= query_pos[:, None]
    chosen = (key_pos[None, :] < query_pos[:, None]) & (key_pos[None, :] > 0)
    lower_mask = (jnp.arange(fsdp_count, dtype=jnp.int32) < fsdp_place).astype(jnp.float32)
    pad_zeros = jnp.zeros((groups_here, CONT), jnp.float32)
    forward_attend = partial(attend_group, causal=causal, score_scale=score_scale)
    backward_attend = partial(attend_back, causal=causal, score_scale=score_scale)
    totals = tuple(
        (
            jnp.zeros(
                (single.shape[0] * lax.axis_size(("dp", "fsdp")),) + single.shape[1:], jnp.float32
            )
            for single in shards
        )
    )
    outputs_yp, outputs_yc, outputs_dxp, outputs_dxc = ([], [], [], [])
    for batch_index in range(MICRO):
        gathered = (
            lax.all_gather(shards[0], ("dp", "fsdp"), axis=0, tiled=True),
            lax.all_gather(shards[1], ("dp", "fsdp"), axis=0, tiled=True),
            lax.all_gather(shards[2], ("dp", "fsdp"), axis=0, tiled=True),
            lax.all_gather(shards[3], ("dp", "fsdp"), axis=0, tiled=True),
            lax.all_gather(shards[4], ("dp", "fsdp"), axis=0, tiled=True),
            lax.all_gather(shards[5], ("dp", "fsdp"), axis=0, tiled=True),
            lax.all_gather(shards[6], ("dp", "fsdp"), axis=0, tiled=True),
            lax.all_gather(shards[7], ("dp", "fsdp"), axis=0, tiled=True),
            lax.all_gather(shards[8], ("dp", "fsdp"), axis=0, tiled=True),
            lax.all_gather(shards[9], ("dp", "fsdp"), axis=0, tiled=True),
            lax.all_gather(shards[10], ("dp", "fsdp"), axis=0, tiled=True),
            lax.all_gather(shards[11], ("dp", "fsdp"), axis=0, tiled=True),
        )
        inputs_x = jnp.concatenate([x_prompt[batch_index], x_cont[batch_index][:, 0]], 1).astype(
            jnp.float32
        )
        local_rows = inputs_x.shape[1]
        flat_x = inputs_x.reshape(-1, D)
        normed_one = normalize(
            flat_x, gathered[0].astype(jnp.float32), gathered[1].astype(jnp.float32)
        ).astype(jnp.bfloat16)
        joined = jnp.dot(normed_one, gathered[2], preferred_element_type=jnp.float32)
        bias_qv = gathered[3].astype(jnp.float32)
        queries = (
            (joined[:, :D] + bias_qv[:D]).astype(jnp.bfloat16).reshape(groups_here, local_rows, D)
        )
        keys_own = joined[:, D : 2 * D].astype(jnp.bfloat16).reshape(groups_here, local_rows, D)
        values_own = (
            (joined[:, 2 * D :] + bias_qv[D:])
            .astype(jnp.bfloat16)
            .reshape(groups_here, local_rows, D)
        )
        prompt_pair = jnp.concatenate([keys_own[:, :prompt_rows], values_own[:, :prompt_rows]], 2)
        whole_kv = lax.all_gather(prompt_pair, "fsdp", axis=1, tiled=True)
        keys_all = jnp.concatenate([whole_kv[..., :D], keys_own[:, prompt_rows:]], 1)
        values_all = jnp.concatenate([whole_kv[..., D:], values_own[:, prompt_rows:]], 1)
        score_zero = (
            jnp.einsum(
                "grd,gkd->grk",
                queries[..., :HEAD_DIM],
                keys_all[..., :HEAD_DIM],
                preferred_element_type=jnp.float32,
            )
            * score_scale
        )
        select = jnp.where(chosen[None], jnp.maximum(score_zero, 0.0), 0.0)
        own_part = jnp.sum(select[:, :prompt_rows, :PROMPT], 1)
        all_parts = lax.all_gather(own_part[None], "fsdp", axis=0, tiled=True)
        prefix = jnp.sum(all_parts * lower_mask[:, None, None], 0)
        whole_sum = jnp.sum(all_parts, 0)
        select_p = select[:, :prompt_rows]
        select_c = select[:, prompt_rows:]
        penalty = select_gain * jnp.concatenate(
            [
                jnp.concatenate([prefix, pad_zeros], 1)[:, None]
                + (jnp.cumsum(select_p, 1) - select_p),
                jnp.concatenate([whole_sum, pad_zeros], 1)[:, None]
                + (jnp.cumsum(select_c, 1) - select_c),
            ],
            1,
        )
        mixture, log_totals = lax.map(forward_attend, (queries, keys_all, values_all, penalty))
        mixed_flat = mixture.reshape(-1, D)
        residual = flat_x + (
            jnp.dot(mixed_flat, gathered[4], preferred_element_type=jnp.float32)
            + gathered[5].astype(jnp.float32)
        )
        normed_two = normalize(
            residual, gathered[6].astype(jnp.float32), gathered[7].astype(jnp.float32)
        ).astype(jnp.bfloat16)
        upward = jnp.dot(normed_two, gathered[8], preferred_element_type=jnp.float32) + gathered[
            9
        ].astype(jnp.float32)
        active, gelu_back = jax.vjp(partial(jax.nn.gelu, approximate=True), upward)
        active_b = active.astype(jnp.bfloat16)
        output = residual + (
            jnp.dot(active_b, gathered[10], preferred_element_type=jnp.float32)
            + gathered[11].astype(jnp.float32)
        )
        output_b = output.astype(jnp.bfloat16).reshape(groups_here, local_rows, D)
        outputs_yp.append(output_b[:, :prompt_rows])
        outputs_yc.append(output_b[:, prompt_rows:][:, None])
        back_set = (
            lax.all_gather(shards[0], ("dp", "fsdp"), axis=0, tiled=True),
            lax.all_gather(shards[1], ("dp", "fsdp"), axis=0, tiled=True),
            lax.all_gather(shards[2], ("dp", "fsdp"), axis=0, tiled=True),
            lax.all_gather(shards[3], ("dp", "fsdp"), axis=0, tiled=True),
            lax.all_gather(shards[4], ("dp", "fsdp"), axis=0, tiled=True),
            lax.all_gather(shards[5], ("dp", "fsdp"), axis=0, tiled=True),
            lax.all_gather(shards[6], ("dp", "fsdp"), axis=0, tiled=True),
            lax.all_gather(shards[7], ("dp", "fsdp"), axis=0, tiled=True),
            lax.all_gather(shards[8], ("dp", "fsdp"), axis=0, tiled=True),
            lax.all_gather(shards[9], ("dp", "fsdp"), axis=0, tiled=True),
            lax.all_gather(shards[10], ("dp", "fsdp"), axis=0, tiled=True),
            lax.all_gather(shards[11], ("dp", "fsdp"), axis=0, tiled=True),
        )
        grad_out_y = jnp.concatenate(
            [dy_prompt[batch_index], dy_cont[batch_index][:, 0]], 1
        ).reshape(-1, D)
        grad_down = jnp.einsum(
            "rf,rd->fd", active_b, grad_out_y, preferred_element_type=jnp.float32
        )
        grad_bdown = jnp.sum(grad_out_y.astype(jnp.float32), 0)
        grad_active = jnp.einsum(
            "rd,fd->rf", grad_out_y, back_set[10], preferred_element_type=jnp.float32
        )
        grad_upward = gelu_back(grad_active)[0].astype(jnp.bfloat16)
        grad_up = jnp.einsum(
            "rd,rf->df", normed_two, grad_upward, preferred_element_type=jnp.float32
        )
        grad_bup = jnp.sum(grad_upward.astype(jnp.float32), 0)
        grad_normed = jnp.einsum(
            "rf,df->rd", grad_upward, back_set[8], preferred_element_type=jnp.float32
        )
        unused, norm_back = jax.vjp(
            normalize, residual, back_set[6].astype(jnp.float32), back_set[7].astype(jnp.float32)
        )
        grad_resid, grad_gain_two, grad_shift_two = norm_back(grad_normed)
        grad_resid = grad_out_y.astype(jnp.float32) + grad_resid
        grad_branch = grad_resid.astype(jnp.bfloat16)
        grad_wout = jnp.einsum(
            "rd,re->de", mixed_flat, grad_branch, preferred_element_type=jnp.float32
        )
        grad_bout = jnp.sum(grad_branch.astype(jnp.float32), 0)
        grad_mixed = jnp.einsum(
            "re,de->rd", grad_branch, back_set[4], preferred_element_type=jnp.float32
        )
        grad_mixed = grad_mixed.astype(jnp.bfloat16).reshape(groups_here, local_rows, D)
        back_values, back_queries, back_keys, back_zero, back_penalty = lax.map(
            backward_attend, (queries, keys_all, values_all, penalty, grad_mixed, log_totals)
        )
        prefix_grad = select_gain * jnp.sum(back_penalty[:, :prompt_rows, :PROMPT], 1)
        whole_grad = select_gain * jnp.sum(back_penalty[:, prompt_rows:, :PROMPT], 1)
        spread_back = prefix_grad[None] * lower_mask[:, None, None] + whole_grad[None]
        part_grad = lax.psum_scatter(spread_back, "fsdp", scatter_dimension=0, tiled=True)[0]
        select_back = jnp.concatenate(
            [
                select_gain * later_sum(back_penalty[:, :prompt_rows])
                + jnp.concatenate([part_grad, pad_zeros], 1)[:, None],
                select_gain * later_sum(back_penalty[:, prompt_rows:]),
            ],
            1,
        )
        grad_zero = (
            back_zero + jnp.where(chosen[None] & (score_zero > 0), select_back, 0.0)
        ).astype(jnp.bfloat16)
        query_zero = (
            jnp.einsum(
                "grk,gkd->grd",
                grad_zero,
                keys_all[..., :HEAD_DIM],
                preferred_element_type=jnp.float32,
            )
            * score_scale
        )
        key_zero = (
            jnp.einsum(
                "grk,grd->gkd",
                grad_zero,
                queries[..., :HEAD_DIM],
                preferred_element_type=jnp.float32,
            )
            * score_scale
        )
        grad_queries = jnp.concatenate([query_zero, back_queries], 2)
        grad_keys = jnp.concatenate([key_zero, back_keys], 2)
        prompt_back = jnp.concatenate([grad_keys[:, :PROMPT], back_values[:, :PROMPT]], 2)
        own_back = lax.psum_scatter(
            prompt_back.astype(jnp.bfloat16), "fsdp", scatter_dimension=1, tiled=True
        ).astype(jnp.float32)
        keys_back = jnp.concatenate([own_back[..., :D], grad_keys[:, PROMPT:]], 1)
        values_back = jnp.concatenate([own_back[..., D:], back_values[:, PROMPT:]], 1)
        grad_joined = (
            jnp.concatenate([grad_queries, keys_back, values_back], 2)
            .astype(jnp.bfloat16)
            .reshape(-1, 3 * D)
        )
        grad_wqkv = jnp.einsum(
            "rd,re->de", normed_one, grad_joined, preferred_element_type=jnp.float32
        )
        grad_bqv = jnp.concatenate(
            [
                jnp.sum(grad_joined[:, :D].astype(jnp.float32), 0),
                jnp.sum(grad_joined[:, 2 * D :].astype(jnp.float32), 0),
            ]
        )
        grad_normed_one = jnp.einsum(
            "re,de->rd", grad_joined, back_set[2], preferred_element_type=jnp.float32
        )
        unused_one, norm_back_one = jax.vjp(
            normalize, flat_x, back_set[0].astype(jnp.float32), back_set[1].astype(jnp.float32)
        )
        grad_input, grad_gain_one, grad_shift_one = norm_back_one(grad_normed_one)
        grad_input = (grad_resid + grad_input).reshape(groups_here, local_rows, D)
        outputs_dxp.append(grad_input[:, :prompt_rows])
        outputs_dxc.append(grad_input[:, prompt_rows:][:, None])
        micro_grads = (
            grad_gain_one,
            grad_shift_one,
            grad_wqkv,
            grad_bqv,
            grad_wout,
            grad_bout,
            grad_gain_two,
            grad_shift_two,
            grad_up,
            grad_bup,
            grad_down,
            grad_bdown,
        )
        totals = tuple((first + second for first, second in zip(totals, micro_grads)))
    results = (
        lax.psum_scatter(totals[0], ("dp", "fsdp"), scatter_dimension=0, tiled=True),
        lax.psum_scatter(totals[1], ("dp", "fsdp"), scatter_dimension=0, tiled=True),
        lax.psum_scatter(totals[2], ("dp", "fsdp"), scatter_dimension=0, tiled=True),
        lax.psum_scatter(totals[3], ("dp", "fsdp"), scatter_dimension=0, tiled=True),
        lax.psum_scatter(totals[4], ("dp", "fsdp"), scatter_dimension=0, tiled=True),
        lax.psum_scatter(totals[5], ("dp", "fsdp"), scatter_dimension=0, tiled=True),
        lax.psum_scatter(totals[6], ("dp", "fsdp"), scatter_dimension=0, tiled=True),
        lax.psum_scatter(totals[7], ("dp", "fsdp"), scatter_dimension=0, tiled=True),
        lax.psum_scatter(totals[8], ("dp", "fsdp"), scatter_dimension=0, tiled=True),
        lax.psum_scatter(totals[9], ("dp", "fsdp"), scatter_dimension=0, tiled=True),
        lax.psum_scatter(totals[10], ("dp", "fsdp"), scatter_dimension=0, tiled=True),
        lax.psum_scatter(totals[11], ("dp", "fsdp"), scatter_dimension=0, tiled=True),
    )
    return (
        jnp.stack(outputs_yp),
        jnp.stack(outputs_yc),
        jnp.stack(outputs_dxp),
        jnp.stack(outputs_dxc),
        results[0],
        results[1],
        results[2],
        results[3],
        results[4],
        results[5],
        results[6],
        results[7],
        results[8],
        results[9],
        results[10],
        results[11],
    )


NCONT = 2
ROWS = PROMPT + NCONT * CONT
SEQ = PROMPT + CONT
SCALE = HEAD_DIM ** (-0.5)
SELECT_GAIN = 4.0 / SEQ
PAIR = 2 * HEAD_DIM
BLOCKS = ((0, 256, 256), (256, 256, 512), (512, 256, 768), (768, 256, 1024), (1024, 64, ROWS))
TAIL = PROMPT - 768
F32 = jnp.float32
B16 = jnp.bfloat16


def mm(a, b):
    return lax.dot_general(a, b, (((1,), (0,)), ((), ())), preferred_element_type=F32)


def mm_nt(a, b):
    return lax.dot_general(a, b, (((1,), (1,)), ((), ())), preferred_element_type=F32)


def masked_half(values, half):
    lane = lax.broadcasted_iota(jnp.int32, values.shape, 1)
    return jnp.where(lane // HEAD_DIM == half, values, 0.0).astype(B16)


def block_masks(place):
    first, rows, keys = BLOCKS[place]
    key_id = lax.broadcasted_iota(jnp.int32, (keys, rows), 0)
    row_id = first + lax.broadcasted_iota(jnp.int32, (keys, rows), 1)
    visible = key_id <= row_id
    if first >= SEQ:
        visible = visible & ((key_id < PROMPT) | (key_id >= SEQ))
    chosen = visible & (key_id < row_id) & (key_id > 0)
    return visible, chosen


def split_mm(values, ones):
    high = values.astype(B16)
    low = (values - high.astype(F32)).astype(B16)
    return mm(high, ones) + mm(low, ones)


def triangle(rows, later):
    a = lax.broadcasted_iota(jnp.int32, (rows, rows), 0)
    b = lax.broadcasted_iota(jnp.int32, (rows, rows), 1)
    return jnp.where((a > b) if later else (a < b), 1.0, 0.0).astype(B16)


def forward_kernel(q_ref, k_ref, v_ref, o_ref, lse_ref, b0, b1, b2, b3, b4, vt_ref, ot_ref):
    bias_refs = (b0, b1, b2, b3, b4)
    head = pl.program_id(0)
    half = head % 2
    queries = masked_half(q_ref[...].astype(F32) * SCALE, half)

    @pl.when(head == 0)
    def _():
        carry = None
        for place, (first, rows, keys) in enumerate(BLOCKS):
            scores = mm_nt(k_ref[:keys], queries[first : first + rows])
            visible, chosen = block_masks(place)
            select = jnp.where(chosen, jnp.maximum(scores, 0.0), 0.0)
            penalty = split_mm(select, triangle(rows, False))
            if carry is not None:
                grown = jnp.zeros((keys - carry.shape[0], 1), F32)
                penalty = penalty + jnp.concatenate([carry, grown], 0)
            bias_refs[place][...] = jnp.where(visible, -SELECT_GAIN * penalty, NEG)
            if first + rows == SEQ:
                lane = lax.broadcasted_iota(jnp.int32, select.shape, 1)
                select = jnp.where(lane < TAIL, select, 0.0)
            if place + 1 < len(BLOCKS):
                total = jnp.sum(select, 1, keepdims=True)
                if carry is not None:
                    total = total + jnp.concatenate([carry, grown], 0)
                carry = total

    @pl.when(half == 0)
    def _():
        vt_ref[...] = v_ref[...].astype(F32).T.astype(B16)

    own = pl.ds(pl.multiple_of(half * HEAD_DIM, HEAD_DIM), HEAD_DIM)
    for place, (first, rows, keys) in enumerate(BLOCKS):
        logits = mm_nt(k_ref[:keys], queries[first : first + rows]) + bias_refs[place][...]
        highest = jnp.max(logits, 0, keepdims=True)
        raised = jnp.exp(logits - highest)
        total = jnp.sum(raised, 0, keepdims=True)
        mixed = mm(vt_ref[own, :keys], raised.astype(B16))
        ot_ref[own, first : first + rows] = mixed * (1.0 / total)
        lse_ref[0, :, first : first + rows] = highest + jnp.log(total)

    @pl.when(half == 1)
    def _():
        o_ref[...] = ot_ref[...].T.astype(B16)


def backward_kernel(
    q_ref, k_ref, v_ref, g_ref, lse_ref, b0, b1, b2, b3, b4,
    dq_ref, dk_ref, dv_ref,
    kt_ref, dqt_ref, dk_acc, dv_acc, p0, p1, p2, p3, p4,
):
    bias_refs = (b0, b1, b2, b3, b4)
    pen_refs = (p0, p1, p2, p3, p4)
    head = HEADS - 1 - pl.program_id(0)
    half = head % 2
    queries = masked_half(q_ref[...].astype(F32) * SCALE, half)
    grads = masked_half(g_ref[...].astype(F32), half)
    own = pl.ds(pl.multiple_of(half * HEAD_DIM, HEAD_DIM), HEAD_DIM)

    @pl.when(head == HEADS - 1)
    def _():
        for pen in pen_refs:
            pen[...] = jnp.zeros_like(pen)

    @pl.when(half == 1)
    def _():
        kt_ref[...] = k_ref[...].astype(F32).T.astype(B16)
        dk_acc[...] = jnp.zeros_like(dk_acc)
        dv_acc[...] = jnp.zeros_like(dv_acc)

    def softmax_grad(place):
        first, rows, keys = BLOCKS[place]
        scores = mm_nt(k_ref[:keys], queries[first : first + rows])
        shares = jnp.exp(scores + bias_refs[place][...] - lse_ref[0, :, first : first + rows])
        back = mm_nt(v_ref[:keys], grads[first : first + rows])
        inner = jnp.sum(shares * back, 0, keepdims=True)
        dv_acc[:keys] += mm(shares.astype(B16), grads[first : first + rows])
        return scores, shares * (back - inner)

    def score_grad(place, grad):
        first, rows, keys = BLOCKS[place]
        grad = grad.astype(B16)
        dqt_ref[own, first : first + rows] = mm(kt_ref[own, :keys], grad)
        dk_acc[:keys] += mm(grad, queries[first : first + rows])

    @pl.when(head != 0)
    def _():
        for place in range(len(BLOCKS)):
            _, grad = softmax_grad(place)
            pen_refs[place][...] += grad
            score_grad(place, grad)

    @pl.when(head == 0)
    def _():
        carry = None
        for place in reversed(range(len(BLOCKS))):
            first, rows, keys = BLOCKS[place]
            scores, grad = softmax_grad(place)
            whole = pen_refs[place][...] + grad
            later = split_mm(whole, triangle(rows, True))
            total = jnp.sum(whole, 1, keepdims=True)
            if carry is not None:
                if first + rows == SEQ:
                    lane = lax.broadcasted_iota(jnp.int32, (keys, rows), 1)
                    later = later + jnp.where(lane < TAIL, carry[:keys], 0.0)
                else:
                    later = later + carry[:keys]
                total = total + carry[:keys]
            carry = total
            _, chosen = block_masks(place)
            grad = grad + jnp.where(chosen & (scores > 0.0), -SELECT_GAIN * later, 0.0)
            score_grad(place, grad)

    @pl.when(half == 0)
    def _():
        dq_ref[...] = (dqt_ref[...].T * SCALE).astype(B16)
        dk_ref[...] = dk_acc[...].astype(B16)
        dv_ref[...] = dv_acc[...].astype(B16)


def pair_spec(index):
    return pl.BlockSpec((ROWS, PAIR), index)


def whole_specs():
    return [pl.BlockSpec((keys, rows), lambda i: (0, 0)) for _, rows, keys in BLOCKS]


PAIRS = HEADS // 2


def attend_forward(joined):
    return pl.pallas_call(
        forward_kernel,
        grid=(HEADS,),
        in_specs=[
            pair_spec(lambda i: (0, i // 2)),
            pair_spec(lambda i: (0, PAIRS + i // 2)),
            pair_spec(lambda i: (0, 2 * PAIRS + i // 2)),
        ],
        out_specs=[
            pair_spec(lambda i: (0, i // 2)),
            pl.BlockSpec((1, 1, ROWS), lambda i: (i, 0, 0)),
            *whole_specs(),
        ],
        out_shape=[
            jax.ShapeDtypeStruct((ROWS, D), B16),
            jax.ShapeDtypeStruct((HEADS, 1, ROWS), F32),
            *(jax.ShapeDtypeStruct((keys, rows), F32) for _, rows, keys in BLOCKS),
        ],
        scratch_shapes=[pltpu.VMEM((PAIR, ROWS), B16), pltpu.VMEM((PAIR, ROWS), F32)],
        name="attend_forward",
    )(joined, joined, joined)


def attend_backward(joined, grad_mixed, lse, biases):
    last = PAIRS - 1
    return pl.pallas_call(
        backward_kernel,
        grid=(HEADS,),
        in_specs=[
            pair_spec(lambda i: (0, last - i // 2)),
            pair_spec(lambda i: (0, PAIRS + last - i // 2)),
            pair_spec(lambda i: (0, 2 * PAIRS + last - i // 2)),
            pair_spec(lambda i: (0, last - i // 2)),
            pl.BlockSpec((1, 1, ROWS), lambda i: (HEADS - 1 - i, 0, 0)),
            *whole_specs(),
        ],
        out_specs=[pair_spec(lambda i: (0, last - i // 2)) for _ in range(3)],
        out_shape=[jax.ShapeDtypeStruct((ROWS, D), B16) for _ in range(3)],
        scratch_shapes=[
            pltpu.VMEM((PAIR, ROWS), B16),
            pltpu.VMEM((PAIR, ROWS), F32),
            pltpu.VMEM((ROWS, PAIR), F32),
            pltpu.VMEM((ROWS, PAIR), F32),
            *(pltpu.VMEM((keys, rows), F32) for _, rows, keys in BLOCKS),
        ],
        name="attend_backward",
    )(joined, joined, joined, grad_mixed, lse, *biases)


EVERY = ("dp", "fsdp")
CORE = 2
PLANE = (0, 1, 4, 5)


def device_count():
    return lax.axis_size("dp") * lax.axis_size("fsdp")


def depth():
    return device_count() // 8


def place_of():
    number = lax.axis_index("dp")
    return number // 4, number // 2 % 2, number % 2, lax.axis_index("fsdp")


def swap(value, mask):
    return lax.ppermute(value, EVERY, [(i, i ^ mask) for i in range(device_count())])


def arrange(pieces, own):
    pieces = list(pieces)
    bit = 1
    while bit < len(pieces):
        odd = (own // bit) % 2 == 1
        pieces = [jnp.where(odd, pieces[k ^ bit], pieces[k]) for k in range(len(pieces))]
        bit *= 2
    return pieces


def gather_steps(shard):
    z, x, core, y = place_of()
    column = [shard] + [swap(shard, 8 * k) for k in range(1, depth())]
    value = jnp.stack(arrange(column, z))
    plane = [value] + [swap(value, mask) for mask in PLANE[1:]]
    plane = arrange(plane, 2 * x + y)
    value = jnp.stack([jnp.stack(plane[:2], 1), jnp.stack(plane[2:], 1)], 1)
    value = jnp.stack(arrange([value, swap(value, CORE)], core), 2)
    return value.reshape(-1, shard.shape[1])


def take(value, index, axis):
    return lax.dynamic_index_in_dim(value, index, axis, keepdims=False)


def add_up(pieces):
    total = pieces[0].astype(F32)
    for piece in pieces[1:]:
        total = total + piece.astype(F32)
    return total


def scatter_steps(grad):
    z, x, core, y = place_of()
    rows = grad.shape[0] // device_count()
    value = grad.reshape(depth(), 2, 2, 2, rows, grad.shape[1])
    value = take(value, core, 2) + swap(take(value, 1 - core, 2), CORE)
    plane = [
        take(take(value, x ^ (mask // 4), 1), y ^ (mask % 2), 1) for mask in PLANE
    ]
    value = add_up(
        plane[:1] + [swap(piece, mask) for piece, mask in zip(plane[1:], PLANE[1:])]
    ).astype(B16)
    column = [take(value, z ^ k, 0) for k in range(depth())]
    return add_up(column[:1] + [swap(column[k], 8 * k) for k in range(1, depth())])


def pack_vectors(vectors, kind):
    rows = D // device_count()
    flat = jnp.concatenate([v.reshape(-1, v.shape[0] // vectors[0].shape[0] * rows) for v in vectors], 1)
    flat = flat.astype(kind).reshape(-1, 3, flat.shape[1] // 3)
    flat = jnp.pad(flat, ((0, 0), (0, rows - 3), (0, 128 - flat.shape[2])))
    return flat.reshape(-1, 128)


def unpack_vectors(columns, sizes):
    rows = D // device_count()
    width = sum(sizes) // 3
    flat = columns.reshape(-1, rows, 128)[:, :3, :width].reshape(-1, 3 * width)
    out, start = [], 0
    for size in sizes:
        out.append(flat[:, start : start + size].reshape(-1).astype(F32))
        start += size
    return out


def pick(first, second, when):
    return jnp.where(when, first, second)


def trade_rows(prompt, cont):
    place = lax.axis_index("fsdp")
    low = place == 0
    swap_pairs = [(0, 1), (1, 0)]
    mine = [pick(t[0], t[1], low).reshape(-1, D) for t in (prompt, cont)]
    away = [pick(t[1], t[0], low).reshape(-1, D) for t in (prompt, cont)]
    came = lax.ppermute(jnp.concatenate(away, 0), "fsdp", swap_pairs)
    half = mine[0].shape[0]
    parts = (came[:half], came[half:])
    return jnp.concatenate(
        [
            pick(mine[0], parts[0], low),
            pick(parts[0], mine[0], low),
            pick(mine[1], parts[1], low),
            pick(parts[1], mine[1], low),
        ],
        0,
    )


def return_rows(whole, kind):
    place = lax.axis_index("fsdp")
    low = place == 0
    half = PROMPT // 2
    parts = (
        (whole[:half], whole[PROMPT:SEQ]),
        (whole[half:PROMPT], whole[SEQ:]),
    )
    mine = [pick(parts[0][i], parts[1][i], low) for i in range(2)]
    away = [pick(parts[1][i], parts[0][i], low) for i in range(2)]
    came = lax.ppermute(jnp.concatenate(away, 0).astype(B16), "fsdp", [(0, 1), (1, 0)])
    came = (came[:half], came[half:])
    out = []
    for i in range(2):
        own, other = mine[i].astype(kind), came[i].astype(kind)
        out.append(jnp.stack([pick(own, other, low), pick(other, own, low)]))
    return out[0][:, None], out[1][:, None, None]


def whole_layer(
    x_prompt, x_cont, dy_prompt, dy_cont,
    ln1_gain, ln1_bias, w_qkv, b_qv, w_out, b_out,
    ln2_gain, ln2_bias, w_up, b_up, w_down, b_down,
):
    devices = device_count()
    vectors = (ln1_gain, ln1_bias, b_qv, b_out, ln2_gain, ln2_bias, b_up, b_down)
    sizes = [v.shape[0] for v in vectors]
    chunks = w_down.shape[0] // w_qkv.shape[0]
    down_chunks = w_down.reshape(chunks, -1, D).transpose(1, 0, 2).reshape(-1, chunks * D)
    full_rest = lax.all_gather(
        jnp.concatenate([w_out, w_up, down_chunks], 1), EVERY, axis=0, tiled=True
    )
    full_first = gather_steps(jnp.concatenate([w_qkv, pack_vectors(vectors, B16)], 1))
    full_qkv = full_first[:, : 3 * D]
    (
        gain_one, shift_one, bias_qv, bias_out, gain_two, shift_two, bias_up, bias_down,
    ) = unpack_vectors(full_first[:, 3 * D :], sizes)
    hidden = w_up.shape[1]
    full_out = full_rest[:, :D]
    full_up = full_rest[:, D : D + hidden]
    full_down = (
        full_rest[:, D + hidden :]
        .reshape(devices, -1, chunks, D)
        .transpose(0, 2, 1, 3)
        .reshape(hidden, D)
    )

    flat_x = trade_rows(x_prompt, x_cont).astype(F32)
    grad_y = trade_rows(dy_prompt, dy_cont)

    normed_one = normalize(flat_x, gain_one, shift_one).astype(B16)
    bias_joined = jnp.concatenate([bias_qv[:D], jnp.zeros((D,), F32), bias_qv[D:]])
    joined = (
        jnp.dot(normed_one, full_qkv, preferred_element_type=F32) + bias_joined
    ).astype(B16)
    mixed, lse, *biases = attend_forward(joined)
    residual = flat_x + (jnp.dot(mixed, full_out, preferred_element_type=F32) + bias_out)
    normed_two = normalize(residual, gain_two, shift_two).astype(B16)
    upward = jnp.dot(normed_two, full_up, preferred_element_type=F32) + bias_up
    active, gelu_back = jax.vjp(partial(jax.nn.gelu, approximate=True), upward)
    active = active.astype(B16)
    output = residual + (jnp.dot(active, full_down, preferred_element_type=F32) + bias_down)
    y_prompt, y_cont = return_rows(output.astype(B16), B16)

    def weight_grad(left, right):
        return jnp.einsum("rd,re->de", left, right, preferred_element_type=F32).astype(B16)

    def through(grad, weight):
        return jnp.einsum("re,de->rd", grad, weight, preferred_element_type=F32)

    def column_sum(values):
        return jnp.sum(values.astype(F32), 0)

    grad_down = weight_grad(active, grad_y)
    grad_b_down = column_sum(grad_y)
    grad_upward = gelu_back(through(grad_y, full_down))[0].astype(B16)
    grad_up = weight_grad(normed_two, grad_upward)
    grad_down = (
        grad_down.reshape(devices, chunks, -1, D).transpose(0, 2, 1, 3).reshape(D, chunks * D)
    )
    own_hidden = lax.psum_scatter(
        jnp.concatenate([grad_up, grad_down], 1), EVERY, scatter_dimension=0, tiled=True
    ).astype(F32)
    grad_w_up = own_hidden[:, :hidden]
    grad_w_down = (
        own_hidden[:, hidden:].reshape(-1, chunks, D).transpose(1, 0, 2).reshape(-1, D)
    )
    grad_b_up = column_sum(grad_upward)
    _, norm_back = jax.vjp(normalize, residual, gain_two, shift_two)
    grad_resid, grad_gain_two, grad_shift_two = norm_back(through(grad_upward, full_up))
    grad_resid = grad_y.astype(F32) + grad_resid
    grad_branch = grad_resid.astype(B16)
    grad_w_out = scatter_steps(weight_grad(mixed, grad_branch))
    grad_b_out = column_sum(grad_branch)
    grad_mixed = through(grad_branch, full_out).astype(B16)
    grad_joined = jnp.concatenate(attend_backward(joined, grad_mixed, lse, biases), 1)
    grad_qkv = weight_grad(normed_one, grad_joined)
    grad_b_qv = jnp.concatenate(
        [column_sum(grad_joined[:, :D]), column_sum(grad_joined[:, 2 * D :])]
    )
    _, norm_back_one = jax.vjp(normalize, flat_x, gain_one, shift_one)
    grad_input, grad_gain_one, grad_shift_one = norm_back_one(through(grad_joined, full_qkv))
    dx_prompt, dx_cont = return_rows(grad_resid + grad_input, F32)

    small = (
        grad_gain_one, grad_shift_one, grad_b_qv, grad_b_out,
        grad_gain_two, grad_shift_two, grad_b_up, grad_b_down,
    )
    own_first = scatter_steps(jnp.concatenate([grad_qkv, pack_vectors(small, B16)], 1))
    grad_w_qkv = own_first[:, : 3 * D]
    pieces = unpack_vectors(own_first[:, 3 * D :], sizes)
    return (
        y_prompt, y_cont, dx_prompt, dx_cont,
        pieces[0], pieces[1], grad_w_qkv, pieces[2], grad_w_out, pieces[3],
        pieces[4], pieces[5], grad_w_up, pieces[6], grad_w_down, pieces[7],
    )


def solution(mesh):
    sizes = dict(mesh.shape)
    whole = sizes["fsdp"] == MICRO == NCONT and sizes["dp"] & (sizes["dp"] - 1) == 0
    return jax.shard_map(
        whole_layer if whole else spread_layer,
        mesh=mesh,
        in_specs=(
            P(None, "dp", "fsdp", None),
            P(None, "dp", "fsdp", None, None),
            P(None, "dp", "fsdp", None),
            P(None, "dp", "fsdp", None, None),
            P(("dp", "fsdp")),
            P(("dp", "fsdp")),
            P(("dp", "fsdp"), None),
            P(("dp", "fsdp")),
            P(("dp", "fsdp"), None),
            P(("dp", "fsdp")),
            P(("dp", "fsdp")),
            P(("dp", "fsdp")),
            P(("dp", "fsdp"), None),
            P(("dp", "fsdp")),
            P(("dp", "fsdp"), None),
            P(("dp", "fsdp")),
        ),
        out_specs=(
            P(None, "dp", "fsdp", None),
            P(None, "dp", "fsdp", None, None),
            P(None, "dp", "fsdp", None),
            P(None, "dp", "fsdp", None, None),
            P(("dp", "fsdp")),
            P(("dp", "fsdp")),
            P(("dp", "fsdp"), None),
            P(("dp", "fsdp")),
            P(("dp", "fsdp"), None),
            P(("dp", "fsdp")),
            P(("dp", "fsdp")),
            P(("dp", "fsdp")),
            P(("dp", "fsdp"), None),
            P(("dp", "fsdp")),
            P(("dp", "fsdp"), None),
            P(("dp", "fsdp")),
        ),
        check_vma=False,
    )
```

```python
from functools import partial

import jax
import jax.numpy as jnp
from jax import lax
from jax.experimental import pallas as pl
from jax.experimental.pallas import tpu as pltpu
from jax.sharding import PartitionSpec as P


D = 768
HEADS = 12
HEAD_DIM = 64
PROMPT = 960
CONT = 64
MICRO = 2


EPS = 1e-05
NEG = -1e30


def normalize(values, gain, shift):
    center = values - jnp.mean(values, -1, keepdims=True)
    spread = jnp.mean(center * center, -1, keepdims=True)
    return center * lax.rsqrt(spread + EPS) * gain + shift


def later_sum(values):
    return jnp.flip(jnp.cumsum(jnp.flip(values, 1), 1), 1) - values


def attend_group(inputs_g, causal, score_scale):
    query_g, key_g, value_g, penalty_g = inputs_g
    rows_here = query_g.shape[0]
    heads_q = query_g.reshape(rows_here, HEADS, HEAD_DIM)
    heads_k = key_g.reshape(-1, HEADS, HEAD_DIM)
    heads_v = value_g.reshape(-1, HEADS, HEAD_DIM)
    scores = (
        jnp.einsum("rhd,khd->hrk", heads_q, heads_k, preferred_element_type=jnp.float32)
        * score_scale
    )
    logits = jnp.where(causal[None], scores - penalty_g[None], NEG)
    highest = jnp.max(logits, -1, keepdims=True)
    raised = jnp.exp(logits - highest)
    totals = jnp.sum(raised, -1, keepdims=True)
    weights_b = (raised / totals).astype(jnp.bfloat16)
    mixture = jnp.einsum("hrk,khd->rhd", weights_b, heads_v, preferred_element_type=jnp.float32)
    return (
        mixture.reshape(rows_here, -1).astype(jnp.bfloat16),
        (highest + jnp.log(totals))[..., 0],
    )


def attend_back(inputs_g, causal, score_scale):
    query_g, key_g, value_g, penalty_g, grad_mix, log_totals = inputs_g
    rows_here = query_g.shape[0]
    heads_q = query_g.reshape(rows_here, HEADS, HEAD_DIM)
    heads_k = key_g.reshape(-1, HEADS, HEAD_DIM)
    heads_v = value_g.reshape(-1, HEADS, HEAD_DIM)
    heads_g = grad_mix.reshape(rows_here, HEADS, HEAD_DIM)
    scores = (
        jnp.einsum("rhd,khd->hrk", heads_q, heads_k, preferred_element_type=jnp.float32)
        * score_scale
    )
    logits = jnp.where(causal[None], scores - penalty_g[None], NEG)
    softmax_w = jnp.exp(logits - log_totals[..., None])
    grad_soft = jnp.einsum("rhd,khd->hrk", heads_g, heads_v, preferred_element_type=jnp.float32)
    inner_sum = jnp.sum(softmax_w * grad_soft, -1, keepdims=True)
    grad_logit = softmax_w * (grad_soft - inner_sum)
    grad_value = jnp.einsum(
        "hrk,rhd->khd", softmax_w.astype(jnp.bfloat16), heads_g, preferred_element_type=jnp.float32
    )
    grad_penalty = -jnp.sum(grad_logit, 0)
    rest_b = grad_logit[1:].astype(jnp.bfloat16)
    grad_query = (
        jnp.einsum("hrk,khd->rhd", rest_b, heads_k[:, 1:], preferred_element_type=jnp.float32)
        * score_scale
    )
    grad_key = (
        jnp.einsum("hrk,rhd->khd", rest_b, heads_q[:, 1:], preferred_element_type=jnp.float32)
        * score_scale
    )
    return (
        grad_value.reshape(-1, D),
        grad_query.reshape(rows_here, -1),
        grad_key.reshape(grad_key.shape[0], -1),
        grad_logit[0],
        grad_penalty,
    )


def spread_layer(
    x_prompt,
    x_cont,
    dy_prompt,
    dy_cont,
    ln1_gain,
    ln1_bias,
    w_qkv,
    b_qv,
    w_out,
    b_out,
    ln2_gain,
    ln2_bias,
    w_up,
    b_up,
    w_down,
    b_down,
):
    shards = (
        ln1_gain,
        ln1_bias,
        w_qkv,
        b_qv,
        w_out,
        b_out,
        ln2_gain,
        ln2_bias,
        w_up,
        b_up,
        w_down,
        b_down,
    )
    groups_here = x_prompt.shape[1]
    prompt_rows = x_prompt.shape[2]
    fsdp_count = lax.axis_size("fsdp")
    fsdp_place = lax.axis_index("fsdp")
    key_count = PROMPT + CONT
    score_scale = HEAD_DIM ** (-0.5)
    select_gain = 4.0 / (PROMPT + CONT)
    query_pos = jnp.concatenate(
        [
            fsdp_place * prompt_rows + jnp.arange(prompt_rows, dtype=jnp.int32),
            PROMPT + jnp.arange(CONT, dtype=jnp.int32),
        ]
    )
    key_pos = jnp.arange(key_count, dtype=jnp.int32)
    causal = key_pos[None, :] <= query_pos[:, None]
    chosen = (key_pos[None, :] < query_pos[:, None]) & (key_pos[None, :] > 0)
    lower_mask = (jnp.arange(fsdp_count, dtype=jnp.int32) < fsdp_place).astype(jnp.float32)
    pad_zeros = jnp.zeros((groups_here, CONT), jnp.float32)
    forward_attend = partial(attend_group, causal=causal, score_scale=score_scale)
    backward_attend = partial(attend_back, causal=causal, score_scale=score_scale)
    totals = tuple(
        (
            jnp.zeros(
                (single.shape[0] * lax.axis_size(("dp", "fsdp")),) + single.shape[1:], jnp.float32
            )
            for single in shards
        )
    )
    outputs_yp, outputs_yc, outputs_dxp, outputs_dxc = ([], [], [], [])
    for batch_index in range(MICRO):
        gathered = (
            lax.all_gather(shards[0], ("dp", "fsdp"), axis=0, tiled=True),
            lax.all_gather(shards[1], ("dp", "fsdp"), axis=0, tiled=True),
            lax.all_gather(shards[2], ("dp", "fsdp"), axis=0, tiled=True),
            lax.all_gather(shards[3], ("dp", "fsdp"), axis=0, tiled=True),
            lax.all_gather(shards[4], ("dp", "fsdp"), axis=0, tiled=True),
            lax.all_gather(shards[5], ("dp", "fsdp"), axis=0, tiled=True),
            lax.all_gather(shards[6], ("dp", "fsdp"), axis=0, tiled=True),
            lax.all_gather(shards[7], ("dp", "fsdp"), axis=0, tiled=True),
            lax.all_gather(shards[8], ("dp", "fsdp"), axis=0, tiled=True),
            lax.all_gather(shards[9], ("dp", "fsdp"), axis=0, tiled=True),
            lax.all_gather(shards[10], ("dp", "fsdp"), axis=0, tiled=True),
            lax.all_gather(shards[11], ("dp", "fsdp"), axis=0, tiled=True),
        )
        inputs_x = jnp.concatenate([x_prompt[batch_index], x_cont[batch_index][:, 0]], 1).astype(
            jnp.float32
        )
        local_rows = inputs_x.shape[1]
        flat_x = inputs_x.reshape(-1, D)
        normed_one = normalize(
            flat_x, gathered[0].astype(jnp.float32), gathered[1].astype(jnp.float32)
        ).astype(jnp.bfloat16)
        joined = jnp.dot(normed_one, gathered[2], preferred_element_type=jnp.float32)
        bias_qv = gathered[3].astype(jnp.float32)
        queries = (
            (joined[:, :D] + bias_qv[:D]).astype(jnp.bfloat16).reshape(groups_here, local_rows, D)
        )
        keys_own = joined[:, D : 2 * D].astype(jnp.bfloat16).reshape(groups_here, local_rows, D)
        values_own = (
            (joined[:, 2 * D :] + bias_qv[D:])
            .astype(jnp.bfloat16)
            .reshape(groups_here, local_rows, D)
        )
        prompt_pair = jnp.concatenate([keys_own[:, :prompt_rows], values_own[:, :prompt_rows]], 2)
        whole_kv = lax.all_gather(prompt_pair, "fsdp", axis=1, tiled=True)
        keys_all = jnp.concatenate([whole_kv[..., :D], keys_own[:, prompt_rows:]], 1)
        values_all = jnp.concatenate([whole_kv[..., D:], values_own[:, prompt_rows:]], 1)
        score_zero = (
            jnp.einsum(
                "grd,gkd->grk",
                queries[..., :HEAD_DIM],
                keys_all[..., :HEAD_DIM],
                preferred_element_type=jnp.float32,
            )
            * score_scale
        )
        select = jnp.where(chosen[None], jnp.maximum(score_zero, 0.0), 0.0)
        own_part = jnp.sum(select[:, :prompt_rows, :PROMPT], 1)
        all_parts = lax.all_gather(own_part[None], "fsdp", axis=0, tiled=True)
        prefix = jnp.sum(all_parts * lower_mask[:, None, None], 0)
        whole_sum = jnp.sum(all_parts, 0)
        select_p = select[:, :prompt_rows]
        select_c = select[:, prompt_rows:]
        penalty = select_gain * jnp.concatenate(
            [
                jnp.concatenate([prefix, pad_zeros], 1)[:, None]
                + (jnp.cumsum(select_p, 1) - select_p),
                jnp.concatenate([whole_sum, pad_zeros], 1)[:, None]
                + (jnp.cumsum(select_c, 1) - select_c),
            ],
            1,
        )
        mixture, log_totals = lax.map(forward_attend, (queries, keys_all, values_all, penalty))
        mixed_flat = mixture.reshape(-1, D)
        residual = flat_x + (
            jnp.dot(mixed_flat, gathered[4], preferred_element_type=jnp.float32)
            + gathered[5].astype(jnp.float32)
        )
        normed_two = normalize(
            residual, gathered[6].astype(jnp.float32), gathered[7].astype(jnp.float32)
        ).astype(jnp.bfloat16)
        upward = jnp.dot(normed_two, gathered[8], preferred_element_type=jnp.float32) + gathered[
            9
        ].astype(jnp.float32)
        active, gelu_back = jax.vjp(partial(jax.nn.gelu, approximate=True), upward)
        active_b = active.astype(jnp.bfloat16)
        output = residual + (
            jnp.dot(active_b, gathered[10], preferred_element_type=jnp.float32)
            + gathered[11].astype(jnp.float32)
        )
        output_b = output.astype(jnp.bfloat16).reshape(groups_here, local_rows, D)
        outputs_yp.append(output_b[:, :prompt_rows])
        outputs_yc.append(output_b[:, prompt_rows:][:, None])
        back_set = (
            lax.all_gather(shards[0], ("dp", "fsdp"), axis=0, tiled=True),
            lax.all_gather(shards[1], ("dp", "fsdp"), axis=0, tiled=True),
            lax.all_gather(shards[2], ("dp", "fsdp"), axis=0, tiled=True),
            lax.all_gather(shards[3], ("dp", "fsdp"), axis=0, tiled=True),
            lax.all_gather(shards[4], ("dp", "fsdp"), axis=0, tiled=True),
            lax.all_gather(shards[5], ("dp", "fsdp"), axis=0, tiled=True),
            lax.all_gather(shards[6], ("dp", "fsdp"), axis=0, tiled=True),
            lax.all_gather(shards[7], ("dp", "fsdp"), axis=0, tiled=True),
            lax.all_gather(shards[8], ("dp", "fsdp"), axis=0, tiled=True),
            lax.all_gather(shards[9], ("dp", "fsdp"), axis=0, tiled=True),
            lax.all_gather(shards[10], ("dp", "fsdp"), axis=0, tiled=True),
            lax.all_gather(shards[11], ("dp", "fsdp"), axis=0, tiled=True),
        )
        grad_out_y = jnp.concatenate(
            [dy_prompt[batch_index], dy_cont[batch_index][:, 0]], 1
        ).reshape(-1, D)
        grad_down = jnp.einsum(
            "rf,rd->fd", active_b, grad_out_y, preferred_element_type=jnp.float32
        )
        grad_bdown = jnp.sum(grad_out_y.astype(jnp.float32), 0)
        grad_active = jnp.einsum(
            "rd,fd->rf", grad_out_y, back_set[10], preferred_element_type=jnp.float32
        )
        grad_upward = gelu_back(grad_active)[0].astype(jnp.bfloat16)
        grad_up = jnp.einsum(
            "rd,rf->df", normed_two, grad_upward, preferred_element_type=jnp.float32
        )
        grad_bup = jnp.sum(grad_upward.astype(jnp.float32), 0)
        grad_normed = jnp.einsum(
            "rf,df->rd", grad_upward, back_set[8], preferred_element_type=jnp.float32
        )
        _, norm_back = jax.vjp(
            normalize, residual, back_set[6].astype(jnp.float32), back_set[7].astype(jnp.float32)
        )
        grad_resid, grad_gain_two, grad_shift_two = norm_back(grad_normed)
        grad_resid = grad_out_y.astype(jnp.float32) + grad_resid
        grad_branch = grad_resid.astype(jnp.bfloat16)
        grad_wout = jnp.einsum(
            "rd,re->de", mixed_flat, grad_branch, preferred_element_type=jnp.float32
        )
        grad_bout = jnp.sum(grad_branch.astype(jnp.float32), 0)
        grad_mixed = jnp.einsum(
            "re,de->rd", grad_branch, back_set[4], preferred_element_type=jnp.float32
        )
        grad_mixed = grad_mixed.astype(jnp.bfloat16).reshape(groups_here, local_rows, D)
        back_values, back_queries, back_keys, back_zero, back_penalty = lax.map(
            backward_attend, (queries, keys_all, values_all, penalty, grad_mixed, log_totals)
        )
        prefix_grad = select_gain * jnp.sum(back_penalty[:, :prompt_rows, :PROMPT], 1)
        whole_grad = select_gain * jnp.sum(back_penalty[:, prompt_rows:, :PROMPT], 1)
        spread_back = prefix_grad[None] * lower_mask[:, None, None] + whole_grad[None]
        part_grad = lax.psum_scatter(spread_back, "fsdp", scatter_dimension=0, tiled=True)[0]
        select_back = jnp.concatenate(
            [
                select_gain * later_sum(back_penalty[:, :prompt_rows])
                + jnp.concatenate([part_grad, pad_zeros], 1)[:, None],
                select_gain * later_sum(back_penalty[:, prompt_rows:]),
            ],
            1,
        )
        grad_zero = (
            back_zero + jnp.where(chosen[None] & (score_zero > 0), select_back, 0.0)
        ).astype(jnp.bfloat16)
        query_zero = (
            jnp.einsum(
                "grk,gkd->grd",
                grad_zero,
                keys_all[..., :HEAD_DIM],
                preferred_element_type=jnp.float32,
            )
            * score_scale
        )
        key_zero = (
            jnp.einsum(
                "grk,grd->gkd",
                grad_zero,
                queries[..., :HEAD_DIM],
                preferred_element_type=jnp.float32,
            )
            * score_scale
        )
        grad_queries = jnp.concatenate([query_zero, back_queries], 2)
        grad_keys = jnp.concatenate([key_zero, back_keys], 2)
        prompt_back = jnp.concatenate([grad_keys[:, :PROMPT], back_values[:, :PROMPT]], 2)
        own_back = lax.psum_scatter(
            prompt_back.astype(jnp.bfloat16), "fsdp", scatter_dimension=1, tiled=True
        ).astype(jnp.float32)
        keys_back = jnp.concatenate([own_back[..., :D], grad_keys[:, PROMPT:]], 1)
        values_back = jnp.concatenate([own_back[..., D:], back_values[:, PROMPT:]], 1)
        grad_joined = (
            jnp.concatenate([grad_queries, keys_back, values_back], 2)
            .astype(jnp.bfloat16)
            .reshape(-1, 3 * D)
        )
        grad_wqkv = jnp.einsum(
            "rd,re->de", normed_one, grad_joined, preferred_element_type=jnp.float32
        )
        grad_bqv = jnp.concatenate(
            [
                jnp.sum(grad_joined[:, :D].astype(jnp.float32), 0),
                jnp.sum(grad_joined[:, 2 * D :].astype(jnp.float32), 0),
            ]
        )
        grad_normed_one = jnp.einsum(
            "re,de->rd", grad_joined, back_set[2], preferred_element_type=jnp.float32
        )
        _, norm_back_one = jax.vjp(
            normalize, flat_x, back_set[0].astype(jnp.float32), back_set[1].astype(jnp.float32)
        )
        grad_input, grad_gain_one, grad_shift_one = norm_back_one(grad_normed_one)
        grad_input = (grad_resid + grad_input).reshape(groups_here, local_rows, D)
        outputs_dxp.append(grad_input[:, :prompt_rows])
        outputs_dxc.append(grad_input[:, prompt_rows:][:, None])
        micro_grads = (
            grad_gain_one,
            grad_shift_one,
            grad_wqkv,
            grad_bqv,
            grad_wout,
            grad_bout,
            grad_gain_two,
            grad_shift_two,
            grad_up,
            grad_bup,
            grad_down,
            grad_bdown,
        )
        totals = tuple((first + second for first, second in zip(totals, micro_grads)))
    results = (
        lax.psum_scatter(totals[0], ("dp", "fsdp"), scatter_dimension=0, tiled=True),
        lax.psum_scatter(totals[1], ("dp", "fsdp"), scatter_dimension=0, tiled=True),
        lax.psum_scatter(totals[2], ("dp", "fsdp"), scatter_dimension=0, tiled=True),
        lax.psum_scatter(totals[3], ("dp", "fsdp"), scatter_dimension=0, tiled=True),
        lax.psum_scatter(totals[4], ("dp", "fsdp"), scatter_dimension=0, tiled=True),
        lax.psum_scatter(totals[5], ("dp", "fsdp"), scatter_dimension=0, tiled=True),
        lax.psum_scatter(totals[6], ("dp", "fsdp"), scatter_dimension=0, tiled=True),
        lax.psum_scatter(totals[7], ("dp", "fsdp"), scatter_dimension=0, tiled=True),
        lax.psum_scatter(totals[8], ("dp", "fsdp"), scatter_dimension=0, tiled=True),
        lax.psum_scatter(totals[9], ("dp", "fsdp"), scatter_dimension=0, tiled=True),
        lax.psum_scatter(totals[10], ("dp", "fsdp"), scatter_dimension=0, tiled=True),
        lax.psum_scatter(totals[11], ("dp", "fsdp"), scatter_dimension=0, tiled=True),
    )
    return (
        jnp.stack(outputs_yp),
        jnp.stack(outputs_yc),
        jnp.stack(outputs_dxp),
        jnp.stack(outputs_dxc),
        results[0],
        results[1],
        results[2],
        results[3],
        results[4],
        results[5],
        results[6],
        results[7],
        results[8],
        results[9],
        results[10],
        results[11],
    )


NCONT = 2
ROWS = PROMPT + NCONT * CONT
SEQ = PROMPT + CONT
SCALE = HEAD_DIM ** (-0.5)
SELECT_GAIN = 4.0 / SEQ
PAIR = 2 * HEAD_DIM
BLOCKS = ((0, 256, 256), (256, 256, 512), (512, 256, 768), (768, 256, 1024), (1024, 64, ROWS))
TAIL = PROMPT - 768
F32 = jnp.float32
B16 = jnp.bfloat16


def mm(a, b):
    return lax.dot_general(a, b, (((1,), (0,)), ((), ())), preferred_element_type=F32)


def mm_nt(a, b):
    return lax.dot_general(a, b, (((1,), (1,)), ((), ())), preferred_element_type=F32)


def masked_half(values, half):
    lane = lax.broadcasted_iota(jnp.int32, values.shape, 1)
    return jnp.where(lane // HEAD_DIM == half, values, 0.0).astype(B16)


def block_masks(place):
    first, rows, keys = BLOCKS[place]
    key_id = lax.broadcasted_iota(jnp.int32, (keys, rows), 0)
    row_id = first + lax.broadcasted_iota(jnp.int32, (keys, rows), 1)
    visible = key_id <= row_id
    if first >= SEQ:
        visible = visible & ((key_id < PROMPT) | (key_id >= SEQ))
    chosen = visible & (key_id < row_id) & (key_id > 0)
    return visible, chosen


def split_mm(values, ones):
    high = values.astype(B16)
    low = (values - high.astype(F32)).astype(B16)
    return mm(high, ones) + mm(low, ones)


def triangle(rows, later):
    a = lax.broadcasted_iota(jnp.int32, (rows, rows), 0)
    b = lax.broadcasted_iota(jnp.int32, (rows, rows), 1)
    return jnp.where((a > b) if later else (a < b), 1.0, 0.0).astype(B16)


def forward_kernel(q_ref, k_ref, v_ref, o_ref, lse_ref, b0, b1, b2, b3, b4, vt_ref, ot_ref):
    bias_refs = (b0, b1, b2, b3, b4)
    head = pl.program_id(0)
    half = head % 2
    queries = masked_half(q_ref[...].astype(F32) * SCALE, half)

    @pl.when(head == 0)
    def _():
        carry = None
        for place, (first, rows, keys) in enumerate(BLOCKS):
            scores = mm_nt(k_ref[:keys], queries[first : first + rows])
            visible, chosen = block_masks(place)
            select = jnp.where(chosen, jnp.maximum(scores, 0.0), 0.0)
            penalty = split_mm(select, triangle(rows, False))
            if carry is not None:
                grown = jnp.zeros((keys - carry.shape[0], 1), F32)
                penalty = penalty + jnp.concatenate([carry, grown], 0)
            bias_refs[place][...] = jnp.where(visible, -SELECT_GAIN * penalty, NEG)
            if first + rows == SEQ:
                lane = lax.broadcasted_iota(jnp.int32, select.shape, 1)
                select = jnp.where(lane < TAIL, select, 0.0)
            if place + 1 < len(BLOCKS):
                total = jnp.sum(select, 1, keepdims=True)
                if carry is not None:
                    total = total + jnp.concatenate([carry, grown], 0)
                carry = total

    @pl.when(half == 0)
    def _():
        vt_ref[...] = v_ref[...].astype(F32).T.astype(B16)

    own = pl.ds(pl.multiple_of(half * HEAD_DIM, HEAD_DIM), HEAD_DIM)
    for place, (first, rows, keys) in enumerate(BLOCKS):
        logits = mm_nt(k_ref[:keys], queries[first : first + rows]) + bias_refs[place][...]
        highest = jnp.max(logits, 0, keepdims=True)
        raised = jnp.exp(logits - highest)
        total = jnp.sum(raised, 0, keepdims=True)
        mixed = mm(vt_ref[own, :keys], raised.astype(B16))
        ot_ref[own, first : first + rows] = mixed * (1.0 / total)
        lse_ref[0, :, first : first + rows] = highest + jnp.log(total)

    @pl.when(half == 1)
    def _():
        o_ref[...] = ot_ref[...].T.astype(B16)


def backward_kernel(
    q_ref, k_ref, v_ref, g_ref, lse_ref, b0, b1, b2, b3, b4,
    dq_ref, dk_ref, dv_ref,
    kt_ref, dqt_ref, dk_acc, dv_acc, p0, p1, p2, p3, p4,
):
    bias_refs = (b0, b1, b2, b3, b4)
    pen_refs = (p0, p1, p2, p3, p4)
    head = HEADS - 1 - pl.program_id(0)
    half = head % 2
    queries = masked_half(q_ref[...].astype(F32) * SCALE, half)
    grads = masked_half(g_ref[...].astype(F32), half)
    own = pl.ds(pl.multiple_of(half * HEAD_DIM, HEAD_DIM), HEAD_DIM)

    @pl.when(head == HEADS - 1)
    def _():
        for pen in pen_refs:
            pen[...] = jnp.zeros_like(pen)

    @pl.when(half == 1)
    def _():
        kt_ref[...] = k_ref[...].astype(F32).T.astype(B16)
        dk_acc[...] = jnp.zeros_like(dk_acc)
        dv_acc[...] = jnp.zeros_like(dv_acc)

    def softmax_grad(place):
        first, rows, keys = BLOCKS[place]
        scores = mm_nt(k_ref[:keys], queries[first : first + rows])
        shares = jnp.exp(scores + bias_refs[place][...] - lse_ref[0, :, first : first + rows])
        back = mm_nt(v_ref[:keys], grads[first : first + rows])
        inner = jnp.sum(shares * back, 0, keepdims=True)
        dv_acc[:keys] += mm(shares.astype(B16), grads[first : first + rows])
        return scores, shares * (back - inner)

    def score_grad(place, grad):
        first, rows, keys = BLOCKS[place]
        grad = grad.astype(B16)
        dqt_ref[own, first : first + rows] = mm(kt_ref[own, :keys], grad)
        dk_acc[:keys] += mm(grad, queries[first : first + rows])

    @pl.when(head != 0)
    def _():
        for place in range(len(BLOCKS)):
            _, grad = softmax_grad(place)
            pen_refs[place][...] += grad
            score_grad(place, grad)

    @pl.when(head == 0)
    def _():
        carry = None
        for place in reversed(range(len(BLOCKS))):
            first, rows, keys = BLOCKS[place]
            scores, grad = softmax_grad(place)
            whole = pen_refs[place][...] + grad
            later = split_mm(whole, triangle(rows, True))
            total = jnp.sum(whole, 1, keepdims=True)
            if carry is not None:
                if first + rows == SEQ:
                    lane = lax.broadcasted_iota(jnp.int32, (keys, rows), 1)
                    later = later + jnp.where(lane < TAIL, carry[:keys], 0.0)
                else:
                    later = later + carry[:keys]
                total = total + carry[:keys]
            carry = total
            _, chosen = block_masks(place)
            grad = grad + jnp.where(chosen & (scores > 0.0), -SELECT_GAIN * later, 0.0)
            score_grad(place, grad)

    @pl.when(half == 0)
    def _():
        dq_ref[...] = (dqt_ref[...].T * SCALE).astype(B16)
        dk_ref[...] = dk_acc[...].astype(B16)
        dv_ref[...] = dv_acc[...].astype(B16)


def pair_spec(index):
    return pl.BlockSpec((ROWS, PAIR), index)


def whole_specs():
    return [pl.BlockSpec((keys, rows), lambda i: (0, 0)) for _, rows, keys in BLOCKS]


PAIRS = HEADS // 2


def attend_forward(joined):
    return pl.pallas_call(
        forward_kernel,
        grid=(HEADS,),
        in_specs=[
            pair_spec(lambda i: (0, i // 2)),
            pair_spec(lambda i: (0, PAIRS + i // 2)),
            pair_spec(lambda i: (0, 2 * PAIRS + i // 2)),
        ],
        out_specs=[
            pair_spec(lambda i: (0, i // 2)),
            pl.BlockSpec((1, 1, ROWS), lambda i: (i, 0, 0)),
            *whole_specs(),
        ],
        out_shape=[
            jax.ShapeDtypeStruct((ROWS, D), B16),
            jax.ShapeDtypeStruct((HEADS, 1, ROWS), F32),
            *(jax.ShapeDtypeStruct((keys, rows), F32) for _, rows, keys in BLOCKS),
        ],
        scratch_shapes=[pltpu.VMEM((PAIR, ROWS), B16), pltpu.VMEM((PAIR, ROWS), F32)],
        name="attend_forward",
    )(joined, joined, joined)


def attend_backward(joined, grad_mixed, lse, biases):
    last = PAIRS - 1
    return pl.pallas_call(
        backward_kernel,
        grid=(HEADS,),
        in_specs=[
            pair_spec(lambda i: (0, last - i // 2)),
            pair_spec(lambda i: (0, PAIRS + last - i // 2)),
            pair_spec(lambda i: (0, 2 * PAIRS + last - i // 2)),
            pair_spec(lambda i: (0, last - i // 2)),
            pl.BlockSpec((1, 1, ROWS), lambda i: (HEADS - 1 - i, 0, 0)),
            *whole_specs(),
        ],
        out_specs=[pair_spec(lambda i: (0, last - i // 2)) for _ in range(3)],
        out_shape=[jax.ShapeDtypeStruct((ROWS, D), B16) for _ in range(3)],
        scratch_shapes=[
            pltpu.VMEM((PAIR, ROWS), B16),
            pltpu.VMEM((PAIR, ROWS), F32),
            pltpu.VMEM((ROWS, PAIR), F32),
            pltpu.VMEM((ROWS, PAIR), F32),
            *(pltpu.VMEM((keys, rows), F32) for _, rows, keys in BLOCKS),
        ],
        name="attend_backward",
    )(joined, joined, joined, grad_mixed, lse, *biases)


EVERY = ("dp", "fsdp")
CORE = 2
PLANE = (0, 1, 4, 5)


def device_count():
    return lax.axis_size("dp") * lax.axis_size("fsdp")


def depth():
    return device_count() // 8


def place_of():
    number = lax.axis_index("dp")
    return number // 4, number // 2 % 2, number % 2, lax.axis_index("fsdp")


def swap(value, mask):
    return lax.ppermute(value, EVERY, [(i, i ^ mask) for i in range(device_count())])


def arrange(pieces, own):
    pieces = list(pieces)
    bit = 1
    while bit < len(pieces):
        odd = (own // bit) % 2 == 1
        pieces = [jnp.where(odd, pieces[k ^ bit], pieces[k]) for k in range(len(pieces))]
        bit *= 2
    return pieces


def gather_steps(shard):
    z, x, core, y = place_of()
    column = [shard] + [swap(shard, 8 * k) for k in range(1, depth())]
    value = jnp.stack(arrange(column, z))
    plane = [value] + [swap(value, mask) for mask in PLANE[1:]]
    plane = arrange(plane, 2 * x + y)
    value = jnp.stack([jnp.stack(plane[:2], 1), jnp.stack(plane[2:], 1)], 1)
    value = jnp.stack(arrange([value, swap(value, CORE)], core), 2)
    return value.reshape(-1, shard.shape[1])


def take(value, index, axis):
    return lax.dynamic_index_in_dim(value, index, axis, keepdims=False)


def add_up(pieces):
    total = pieces[0].astype(F32)
    for piece in pieces[1:]:
        total = total + piece.astype(F32)
    return total


def scatter_steps(grad):
    return scatter_chips(scatter_core(grad))


def scatter_core(grad):
    core = place_of()[2]
    rows = grad.shape[0] // device_count()
    value = grad.reshape(depth(), 2, 2, 2, rows, grad.shape[1])
    other = swap(take(value, 1 - core, 2), CORE)
    return take(value, core, 2) + other


def scatter_chips(value):
    z, x, _, y = place_of()
    plane = [
        take(take(value, x ^ (mask // 4), 1), y ^ (mask % 2), 1) for mask in PLANE
    ]
    others = [swap(piece, mask) for piece, mask in zip(plane[1:], PLANE[1:])]
    value = add_up(plane[:1] + others).astype(B16)
    column = [take(value, z ^ k, 0) for k in range(depth())]
    others = [swap(column[k], 8 * k) for k in range(1, depth())]
    return add_up(column[:1] + others)


def pack_vectors(vectors, kind):
    rows = D // device_count()
    flat = jnp.concatenate([v.reshape(-1, v.shape[0] // vectors[0].shape[0] * rows) for v in vectors], 1)
    flat = flat.astype(kind).reshape(-1, 3, flat.shape[1] // 3)
    flat = jnp.pad(flat, ((0, 0), (0, rows - 3), (0, 128 - flat.shape[2])))
    return flat.reshape(-1, 128)


def unpack_vectors(columns, sizes):
    rows = D // device_count()
    width = sum(sizes) // 3
    flat = columns.reshape(-1, rows, 128)[:, :3, :width].reshape(-1, 3 * width)
    out, start = [], 0
    for size in sizes:
        out.append(flat[:, start : start + size].reshape(-1).astype(F32))
        start += size
    return out


def gelu_pair(upward):
    rate = (2.0 / jnp.pi) ** 0.5
    square = upward * upward
    bend = jnp.tanh(rate * (upward + 0.044715 * (square * upward)))
    gate = 0.5 * (1.0 + bend)
    slope = gate + 0.5 * upward * (1.0 - bend * bend) * (rate * (1.0 + 3 * 0.044715 * square))
    return (upward * gate).astype(B16), slope.astype(B16)


def normalize_back(values, gain, grad):
    center = values - jnp.mean(values, -1, keepdims=True)
    rate = lax.rsqrt(jnp.mean(center * center, -1, keepdims=True) + EPS)
    unit = center * rate
    scaled = grad * gain
    inner = jnp.mean(scaled * unit, -1, keepdims=True)
    back = rate * (scaled - jnp.mean(scaled, -1, keepdims=True) - unit * inner)
    return back, jnp.sum(grad * unit, 0), jnp.sum(grad, 0)


def pick(first, second, when):
    return jnp.where(when, first, second)


def trade_rows(prompt, cont):
    place = lax.axis_index("fsdp")
    low = place == 0
    swap_pairs = [(0, 1), (1, 0)]
    mine = [pick(t[0], t[1], low).reshape(-1, D) for t in (prompt, cont)]
    away = [pick(t[1], t[0], low).reshape(-1, D) for t in (prompt, cont)]
    came = lax.ppermute(jnp.concatenate(away, 0), "fsdp", swap_pairs)
    half = mine[0].shape[0]
    parts = (came[:half], came[half:])
    return jnp.concatenate(
        [
            pick(mine[0], parts[0], low),
            pick(parts[0], mine[0], low),
            pick(mine[1], parts[1], low),
            pick(parts[1], mine[1], low),
        ],
        0,
    )


def return_rows(whole, kind):
    place = lax.axis_index("fsdp")
    low = place == 0
    half = PROMPT // 2
    parts = (
        (whole[:half], whole[PROMPT:SEQ]),
        (whole[half:PROMPT], whole[SEQ:]),
    )
    mine = [pick(parts[0][i], parts[1][i], low) for i in range(2)]
    away = [pick(parts[1][i], parts[0][i], low) for i in range(2)]
    came = lax.ppermute(jnp.concatenate(away, 0).astype(B16), "fsdp", [(0, 1), (1, 0)])
    came = (came[:half], came[half:])
    out = []
    for i in range(2):
        own, other = mine[i].astype(kind), came[i].astype(kind)
        out.append(jnp.stack([pick(own, other, low), pick(other, own, low)]))
    return out[0][:, None], out[1][:, None, None]


def whole_layer(*args):
    return whole_steps(*args)


def whole_steps(
    x_prompt, x_cont, dy_prompt, dy_cont,
    ln1_gain, ln1_bias, w_qkv, b_qv, w_out, b_out,
    ln2_gain, ln2_bias, w_up, b_up, w_down, b_down,
):
    devices = device_count()
    vectors = (ln1_gain, ln1_bias, b_qv, b_out, ln2_gain, ln2_bias, b_up, b_down)
    sizes = [v.shape[0] for v in vectors]
    chunks = w_down.shape[0] // w_qkv.shape[0]
    rows = w_qkv.shape[0]
    full_rest = lax.all_gather(
        jnp.concatenate([w_out, *(w_up[:, i * D : (i + 1) * D] for i in range(chunks)), w_down], 0),
        EVERY,
        axis=0,
    )
    full_first = gather_steps(jnp.concatenate([w_qkv, pack_vectors(vectors, B16)], 1))
    full_qkv = full_first[:, : 3 * D]
    (
        gain_one, shift_one, bias_qv, bias_out, gain_two, shift_two, bias_up, bias_down,
    ) = unpack_vectors(full_first[:, 3 * D :], sizes)
    hidden = w_up.shape[1]
    full_out = full_rest[:, :rows].reshape(D, D)
    full_up = jnp.concatenate(
        [full_rest[:, rows * i : rows * (i + 1)].reshape(D, D) for i in range(1, chunks + 1)], 1
    )
    full_down = full_rest[:, rows * (chunks + 1) :].reshape(hidden, D)

    flat_x = trade_rows(x_prompt, x_cont).astype(F32)
    normed_one = normalize(flat_x, gain_one, shift_one).astype(B16)
    bias_joined = jnp.concatenate([bias_qv[:D], jnp.zeros((D,), F32), bias_qv[D:]])
    joined = (
        jnp.dot(normed_one, full_qkv, preferred_element_type=F32) + bias_joined
    ).astype(B16)
    joined, dy_prompt, dy_cont = lax.optimization_barrier((joined, dy_prompt, dy_cont))
    grad_y = trade_rows(dy_prompt, dy_cont)
    mixed, lse, *biases = attend_forward(joined)
    residual = flat_x + (jnp.dot(mixed, full_out, preferred_element_type=F32) + bias_out)
    normed_two = normalize(residual, gain_two, shift_two).astype(B16)
    upward = jnp.dot(normed_two, full_up, preferred_element_type=F32) + bias_up
    active, slope = lax.optimization_barrier(gelu_pair(upward))

    def weight_grad(left, right):
        return jnp.einsum("rd,re->de", left, right, preferred_element_type=F32).astype(B16)

    def through(grad, weight):
        return jnp.einsum("re,de->rd", grad, weight, preferred_element_type=F32)

    def column_sum(values):
        return jnp.sum(values.astype(F32), 0)

    grad_upward = (through(grad_y, full_down) * slope.astype(F32)).astype(B16)
    grad_down = weight_grad(active, grad_y)
    grad_up = weight_grad(normed_two, grad_upward)
    packed_grads = jnp.concatenate(
        [
            *(grad_up[:, i * D : (i + 1) * D].reshape(devices, rows, D) for i in range(chunks)),
            grad_down.reshape(devices, -1, D),
        ],
        1,
    )
    packed_grads, active, grad_upward = lax.optimization_barrier(
        (packed_grads, active, grad_upward)
    )
    own_hidden = lax.psum_scatter(packed_grads, EVERY, scatter_dimension=0).astype(F32)
    grad_w_up = jnp.concatenate(
        [own_hidden[i * rows : (i + 1) * rows] for i in range(chunks)], 1
    )
    grad_w_down = own_hidden[chunks * rows :]
    output = residual + (jnp.dot(active, full_down, preferred_element_type=F32) + bias_down)
    y_prompt, y_cont = return_rows(output.astype(B16), B16)

    grad_b_down = column_sum(grad_y)
    grad_b_up = column_sum(grad_upward)
    grad_resid, grad_gain_two, grad_shift_two = normalize_back(
        residual, gain_two, through(grad_upward, full_up)
    )
    grad_resid = grad_y.astype(F32) + grad_resid
    grad_branch = grad_resid.astype(B16)
    grad_w_out = scatter_steps(weight_grad(mixed, grad_branch))
    grad_b_out = column_sum(grad_branch)
    grad_mixed = through(grad_branch, full_out).astype(B16)
    grad_joined = jnp.concatenate(attend_backward(joined, grad_mixed, lse, biases), 1)
    grad_qkv = weight_grad(normed_one, grad_joined)
    grad_qkv, grad_joined = lax.optimization_barrier((grad_qkv, grad_joined))
    grad_b_qv = jnp.concatenate(
        [column_sum(grad_joined[:, :D]), column_sum(grad_joined[:, 2 * D :])]
    )
    first = scatter_core(grad_qkv)
    back_one = through(grad_joined, full_qkv)
    first, back_one = lax.optimization_barrier((first, back_one))
    grad_input, grad_gain_one, grad_shift_one = normalize_back(flat_x, gain_one, back_one)
    dx_prompt, dx_cont = return_rows(grad_resid + grad_input, F32)

    small = (
        grad_gain_one, grad_shift_one, grad_b_qv, grad_b_out,
        grad_gain_two, grad_shift_two, grad_b_up, grad_b_down,
    )
    own_first = scatter_chips(first)
    own_vectors = scatter_steps(pack_vectors(small, B16))
    grad_w_qkv = own_first
    pieces = unpack_vectors(own_vectors, sizes)
    return (
        y_prompt, y_cont, dx_prompt, dx_cont,
        pieces[0], pieces[1], grad_w_qkv, pieces[2], grad_w_out, pieces[3],
        pieces[4], pieces[5], grad_w_up, pieces[6], grad_w_down, pieces[7],
    )


def solution(mesh):
    sizes = dict(mesh.shape)
    whole = sizes["fsdp"] == MICRO == NCONT and sizes["dp"] & (sizes["dp"] - 1) == 0
    return jax.shard_map(
        whole_layer if whole else spread_layer,
        mesh=mesh,
        in_specs=(
            P(None, "dp", "fsdp", None),
            P(None, "dp", "fsdp", None, None),
            P(None, "dp", "fsdp", None),
            P(None, "dp", "fsdp", None, None),
            P(("dp", "fsdp")),
            P(("dp", "fsdp")),
            P(("dp", "fsdp"), None),
            P(("dp", "fsdp")),
            P(("dp", "fsdp"), None),
            P(("dp", "fsdp")),
            P(("dp", "fsdp")),
            P(("dp", "fsdp")),
            P(("dp", "fsdp"), None),
            P(("dp", "fsdp")),
            P(("dp", "fsdp"), None),
            P(("dp", "fsdp")),
        ),
        out_specs=(
            P(None, "dp", "fsdp", None),
            P(None, "dp", "fsdp", None, None),
            P(None, "dp", "fsdp", None),
            P(None, "dp", "fsdp", None, None),
            P(("dp", "fsdp")),
            P(("dp", "fsdp")),
            P(("dp", "fsdp"), None),
            P(("dp", "fsdp")),
            P(("dp", "fsdp"), None),
            P(("dp", "fsdp")),
            P(("dp", "fsdp")),
            P(("dp", "fsdp")),
            P(("dp", "fsdp"), None),
            P(("dp", "fsdp")),
            P(("dp", "fsdp"), None),
            P(("dp", "fsdp")),
        ),
        check_vma=False,
    )
```

```python
from functools import partial

import jax
import jax.numpy as jnp
from jax import lax
from jax.experimental import pallas as pl
from jax.experimental.pallas import tpu as pltpu
from jax.sharding import PartitionSpec as P


D = 768
HEADS = 12
HEAD_DIM = 64
PROMPT = 960
CONT = 64
MICRO = 2


EPS = 1e-05
NEG = -1e30


def normalize(values, gain, shift):
    center = values - jnp.mean(values, -1, keepdims=True)
    spread = jnp.mean(center * center, -1, keepdims=True)
    return center * lax.rsqrt(spread + EPS) * gain + shift


def later_sum(values):
    return jnp.flip(jnp.cumsum(jnp.flip(values, 1), 1), 1) - values


def attend_group(inputs_g, causal, score_scale):
    query_g, key_g, value_g, penalty_g = inputs_g
    rows_here = query_g.shape[0]
    heads_q = query_g.reshape(rows_here, HEADS, HEAD_DIM)
    heads_k = key_g.reshape(-1, HEADS, HEAD_DIM)
    heads_v = value_g.reshape(-1, HEADS, HEAD_DIM)
    scores = (
        jnp.einsum("rhd,khd->hrk", heads_q, heads_k, preferred_element_type=jnp.float32)
        * score_scale
    )
    logits = jnp.where(causal[None], scores - penalty_g[None], NEG)
    highest = jnp.max(logits, -1, keepdims=True)
    raised = jnp.exp(logits - highest)
    totals = jnp.sum(raised, -1, keepdims=True)
    weights_b = (raised / totals).astype(jnp.bfloat16)
    mixture = jnp.einsum("hrk,khd->rhd", weights_b, heads_v, preferred_element_type=jnp.float32)
    return (
        mixture.reshape(rows_here, -1).astype(jnp.bfloat16),
        (highest + jnp.log(totals))[..., 0],
    )


def attend_back(inputs_g, causal, score_scale):
    query_g, key_g, value_g, penalty_g, grad_mix, log_totals = inputs_g
    rows_here = query_g.shape[0]
    heads_q = query_g.reshape(rows_here, HEADS, HEAD_DIM)
    heads_k = key_g.reshape(-1, HEADS, HEAD_DIM)
    heads_v = value_g.reshape(-1, HEADS, HEAD_DIM)
    heads_g = grad_mix.reshape(rows_here, HEADS, HEAD_DIM)
    scores = (
        jnp.einsum("rhd,khd->hrk", heads_q, heads_k, preferred_element_type=jnp.float32)
        * score_scale
    )
    logits = jnp.where(causal[None], scores - penalty_g[None], NEG)
    softmax_w = jnp.exp(logits - log_totals[..., None])
    grad_soft = jnp.einsum("rhd,khd->hrk", heads_g, heads_v, preferred_element_type=jnp.float32)
    inner_sum = jnp.sum(softmax_w * grad_soft, -1, keepdims=True)
    grad_logit = softmax_w * (grad_soft - inner_sum)
    grad_value = jnp.einsum(
        "hrk,rhd->khd", softmax_w.astype(jnp.bfloat16), heads_g, preferred_element_type=jnp.float32
    )
    grad_penalty = -jnp.sum(grad_logit, 0)
    rest_b = grad_logit[1:].astype(jnp.bfloat16)
    grad_query = (
        jnp.einsum("hrk,khd->rhd", rest_b, heads_k[:, 1:], preferred_element_type=jnp.float32)
        * score_scale
    )
    grad_key = (
        jnp.einsum("hrk,rhd->khd", rest_b, heads_q[:, 1:], preferred_element_type=jnp.float32)
        * score_scale
    )
    return (
        grad_value.reshape(-1, D),
        grad_query.reshape(rows_here, -1),
        grad_key.reshape(grad_key.shape[0], -1),
        grad_logit[0],
        grad_penalty,
    )


def spread_layer(
    x_prompt,
    x_cont,
    dy_prompt,
    dy_cont,
    ln1_gain,
    ln1_bias,
    w_qkv,
    b_qv,
    w_out,
    b_out,
    ln2_gain,
    ln2_bias,
    w_up,
    b_up,
    w_down,
    b_down,
):
    shards = (
        ln1_gain,
        ln1_bias,
        w_qkv,
        b_qv,
        w_out,
        b_out,
        ln2_gain,
        ln2_bias,
        w_up,
        b_up,
        w_down,
        b_down,
    )
    groups_here = x_prompt.shape[1]
    prompt_rows = x_prompt.shape[2]
    fsdp_count = lax.axis_size("fsdp")
    fsdp_place = lax.axis_index("fsdp")
    key_count = PROMPT + CONT
    score_scale = HEAD_DIM ** (-0.5)
    select_gain = 4.0 / (PROMPT + CONT)
    query_pos = jnp.concatenate(
        [
            fsdp_place * prompt_rows + jnp.arange(prompt_rows, dtype=jnp.int32),
            PROMPT + jnp.arange(CONT, dtype=jnp.int32),
        ]
    )
    key_pos = jnp.arange(key_count, dtype=jnp.int32)
    causal = key_pos[None, :] <= query_pos[:, None]
    chosen = (key_pos[None, :] < query_pos[:, None]) & (key_pos[None, :] > 0)
    lower_mask = (jnp.arange(fsdp_count, dtype=jnp.int32) < fsdp_place).astype(jnp.float32)
    pad_zeros = jnp.zeros((groups_here, CONT), jnp.float32)
    forward_attend = partial(attend_group, causal=causal, score_scale=score_scale)
    backward_attend = partial(attend_back, causal=causal, score_scale=score_scale)
    totals = tuple(
        (
            jnp.zeros(
                (single.shape[0] * lax.axis_size(("dp", "fsdp")),) + single.shape[1:], jnp.float32
            )
            for single in shards
        )
    )
    outputs_yp, outputs_yc, outputs_dxp, outputs_dxc = ([], [], [], [])
    for batch_index in range(MICRO):
        gathered = (
            lax.all_gather(shards[0], ("dp", "fsdp"), axis=0, tiled=True),
            lax.all_gather(shards[1], ("dp", "fsdp"), axis=0, tiled=True),
            lax.all_gather(shards[2], ("dp", "fsdp"), axis=0, tiled=True),
            lax.all_gather(shards[3], ("dp", "fsdp"), axis=0, tiled=True),
            lax.all_gather(shards[4], ("dp", "fsdp"), axis=0, tiled=True),
            lax.all_gather(shards[5], ("dp", "fsdp"), axis=0, tiled=True),
            lax.all_gather(shards[6], ("dp", "fsdp"), axis=0, tiled=True),
            lax.all_gather(shards[7], ("dp", "fsdp"), axis=0, tiled=True),
            lax.all_gather(shards[8], ("dp", "fsdp"), axis=0, tiled=True),
            lax.all_gather(shards[9], ("dp", "fsdp"), axis=0, tiled=True),
            lax.all_gather(shards[10], ("dp", "fsdp"), axis=0, tiled=True),
            lax.all_gather(shards[11], ("dp", "fsdp"), axis=0, tiled=True),
        )
        inputs_x = jnp.concatenate([x_prompt[batch_index], x_cont[batch_index][:, 0]], 1).astype(
            jnp.float32
        )
        local_rows = inputs_x.shape[1]
        flat_x = inputs_x.reshape(-1, D)
        normed_one = normalize(
            flat_x, gathered[0].astype(jnp.float32), gathered[1].astype(jnp.float32)
        ).astype(jnp.bfloat16)
        joined = jnp.dot(normed_one, gathered[2], preferred_element_type=jnp.float32)
        bias_qv = gathered[3].astype(jnp.float32)
        queries = (
            (joined[:, :D] + bias_qv[:D]).astype(jnp.bfloat16).reshape(groups_here, local_rows, D)
        )
        keys_own = joined[:, D : 2 * D].astype(jnp.bfloat16).reshape(groups_here, local_rows, D)
        values_own = (
            (joined[:, 2 * D :] + bias_qv[D:])
            .astype(jnp.bfloat16)
            .reshape(groups_here, local_rows, D)
        )
        prompt_pair = jnp.concatenate([keys_own[:, :prompt_rows], values_own[:, :prompt_rows]], 2)
        whole_kv = lax.all_gather(prompt_pair, "fsdp", axis=1, tiled=True)
        keys_all = jnp.concatenate([whole_kv[..., :D], keys_own[:, prompt_rows:]], 1)
        values_all = jnp.concatenate([whole_kv[..., D:], values_own[:, prompt_rows:]], 1)
        score_zero = (
            jnp.einsum(
                "grd,gkd->grk",
                queries[..., :HEAD_DIM],
                keys_all[..., :HEAD_DIM],
                preferred_element_type=jnp.float32,
            )
            * score_scale
        )
        select = jnp.where(chosen[None], jnp.maximum(score_zero, 0.0), 0.0)
        own_part = jnp.sum(select[:, :prompt_rows, :PROMPT], 1)
        all_parts = lax.all_gather(own_part[None], "fsdp", axis=0, tiled=True)
        prefix = jnp.sum(all_parts * lower_mask[:, None, None], 0)
        whole_sum = jnp.sum(all_parts, 0)
        select_p = select[:, :prompt_rows]
        select_c = select[:, prompt_rows:]
        penalty = select_gain * jnp.concatenate(
            [
                jnp.concatenate([prefix, pad_zeros], 1)[:, None]
                + (jnp.cumsum(select_p, 1) - select_p),
                jnp.concatenate([whole_sum, pad_zeros], 1)[:, None]
                + (jnp.cumsum(select_c, 1) - select_c),
            ],
            1,
        )
        mixture, log_totals = lax.map(forward_attend, (queries, keys_all, values_all, penalty))
        mixed_flat = mixture.reshape(-1, D)
        residual = flat_x + (
            jnp.dot(mixed_flat, gathered[4], preferred_element_type=jnp.float32)
            + gathered[5].astype(jnp.float32)
        )
        normed_two = normalize(
            residual, gathered[6].astype(jnp.float32), gathered[7].astype(jnp.float32)
        ).astype(jnp.bfloat16)
        upward = jnp.dot(normed_two, gathered[8], preferred_element_type=jnp.float32) + gathered[
            9
        ].astype(jnp.float32)
        active, gelu_back = jax.vjp(partial(jax.nn.gelu, approximate=True), upward)
        active_b = active.astype(jnp.bfloat16)
        output = residual + (
            jnp.dot(active_b, gathered[10], preferred_element_type=jnp.float32)
            + gathered[11].astype(jnp.float32)
        )
        output_b = output.astype(jnp.bfloat16).reshape(groups_here, local_rows, D)
        outputs_yp.append(output_b[:, :prompt_rows])
        outputs_yc.append(output_b[:, prompt_rows:][:, None])
        back_set = (
            lax.all_gather(shards[0], ("dp", "fsdp"), axis=0, tiled=True),
            lax.all_gather(shards[1], ("dp", "fsdp"), axis=0, tiled=True),
            lax.all_gather(shards[2], ("dp", "fsdp"), axis=0, tiled=True),
            lax.all_gather(shards[3], ("dp", "fsdp"), axis=0, tiled=True),
            lax.all_gather(shards[4], ("dp", "fsdp"), axis=0, tiled=True),
            lax.all_gather(shards[5], ("dp", "fsdp"), axis=0, tiled=True),
            lax.all_gather(shards[6], ("dp", "fsdp"), axis=0, tiled=True),
            lax.all_gather(shards[7], ("dp", "fsdp"), axis=0, tiled=True),
            lax.all_gather(shards[8], ("dp", "fsdp"), axis=0, tiled=True),
            lax.all_gather(shards[9], ("dp", "fsdp"), axis=0, tiled=True),
            lax.all_gather(shards[10], ("dp", "fsdp"), axis=0, tiled=True),
            lax.all_gather(shards[11], ("dp", "fsdp"), axis=0, tiled=True),
        )
        grad_out_y = jnp.concatenate(
            [dy_prompt[batch_index], dy_cont[batch_index][:, 0]], 1
        ).reshape(-1, D)
        grad_down = jnp.einsum(
            "rf,rd->fd", active_b, grad_out_y, preferred_element_type=jnp.float32
        )
        grad_bdown = jnp.sum(grad_out_y.astype(jnp.float32), 0)
        grad_active = jnp.einsum(
            "rd,fd->rf", grad_out_y, back_set[10], preferred_element_type=jnp.float32
        )
        grad_upward = gelu_back(grad_active)[0].astype(jnp.bfloat16)
        grad_up = jnp.einsum(
            "rd,rf->df", normed_two, grad_upward, preferred_element_type=jnp.float32
        )
        grad_bup = jnp.sum(grad_upward.astype(jnp.float32), 0)
        grad_normed = jnp.einsum(
            "rf,df->rd", grad_upward, back_set[8], preferred_element_type=jnp.float32
        )
        _, norm_back = jax.vjp(
            normalize, residual, back_set[6].astype(jnp.float32), back_set[7].astype(jnp.float32)
        )
        grad_resid, grad_gain_two, grad_shift_two = norm_back(grad_normed)
        grad_resid = grad_out_y.astype(jnp.float32) + grad_resid
        grad_branch = grad_resid.astype(jnp.bfloat16)
        grad_wout = jnp.einsum(
            "rd,re->de", mixed_flat, grad_branch, preferred_element_type=jnp.float32
        )
        grad_bout = jnp.sum(grad_branch.astype(jnp.float32), 0)
        grad_mixed = jnp.einsum(
            "re,de->rd", grad_branch, back_set[4], preferred_element_type=jnp.float32
        )
        grad_mixed = grad_mixed.astype(jnp.bfloat16).reshape(groups_here, local_rows, D)
        back_values, back_queries, back_keys, back_zero, back_penalty = lax.map(
            backward_attend, (queries, keys_all, values_all, penalty, grad_mixed, log_totals)
        )
        prefix_grad = select_gain * jnp.sum(back_penalty[:, :prompt_rows, :PROMPT], 1)
        whole_grad = select_gain * jnp.sum(back_penalty[:, prompt_rows:, :PROMPT], 1)
        spread_back = prefix_grad[None] * lower_mask[:, None, None] + whole_grad[None]
        part_grad = lax.psum_scatter(spread_back, "fsdp", scatter_dimension=0, tiled=True)[0]
        select_back = jnp.concatenate(
            [
                select_gain * later_sum(back_penalty[:, :prompt_rows])
                + jnp.concatenate([part_grad, pad_zeros], 1)[:, None],
                select_gain * later_sum(back_penalty[:, prompt_rows:]),
            ],
            1,
        )
        grad_zero = (
            back_zero + jnp.where(chosen[None] & (score_zero > 0), select_back, 0.0)
        ).astype(jnp.bfloat16)
        query_zero = (
            jnp.einsum(
                "grk,gkd->grd",
                grad_zero,
                keys_all[..., :HEAD_DIM],
                preferred_element_type=jnp.float32,
            )
            * score_scale
        )
        key_zero = (
            jnp.einsum(
                "grk,grd->gkd",
                grad_zero,
                queries[..., :HEAD_DIM],
                preferred_element_type=jnp.float32,
            )
            * score_scale
        )
        grad_queries = jnp.concatenate([query_zero, back_queries], 2)
        grad_keys = jnp.concatenate([key_zero, back_keys], 2)
        prompt_back = jnp.concatenate([grad_keys[:, :PROMPT], back_values[:, :PROMPT]], 2)
        own_back = lax.psum_scatter(
            prompt_back.astype(jnp.bfloat16), "fsdp", scatter_dimension=1, tiled=True
        ).astype(jnp.float32)
        keys_back = jnp.concatenate([own_back[..., :D], grad_keys[:, PROMPT:]], 1)
        values_back = jnp.concatenate([own_back[..., D:], back_values[:, PROMPT:]], 1)
        grad_joined = (
            jnp.concatenate([grad_queries, keys_back, values_back], 2)
            .astype(jnp.bfloat16)
            .reshape(-1, 3 * D)
        )
        grad_wqkv = jnp.einsum(
            "rd,re->de", normed_one, grad_joined, preferred_element_type=jnp.float32
        )
        grad_bqv = jnp.concatenate(
            [
                jnp.sum(grad_joined[:, :D].astype(jnp.float32), 0),
                jnp.sum(grad_joined[:, 2 * D :].astype(jnp.float32), 0),
            ]
        )
        grad_normed_one = jnp.einsum(
            "re,de->rd", grad_joined, back_set[2], preferred_element_type=jnp.float32
        )
        _, norm_back_one = jax.vjp(
            normalize, flat_x, back_set[0].astype(jnp.float32), back_set[1].astype(jnp.float32)
        )
        grad_input, grad_gain_one, grad_shift_one = norm_back_one(grad_normed_one)
        grad_input = (grad_resid + grad_input).reshape(groups_here, local_rows, D)
        outputs_dxp.append(grad_input[:, :prompt_rows])
        outputs_dxc.append(grad_input[:, prompt_rows:][:, None])
        micro_grads = (
            grad_gain_one,
            grad_shift_one,
            grad_wqkv,
            grad_bqv,
            grad_wout,
            grad_bout,
            grad_gain_two,
            grad_shift_two,
            grad_up,
            grad_bup,
            grad_down,
            grad_bdown,
        )
        totals = tuple((first + second for first, second in zip(totals, micro_grads)))
    results = (
        lax.psum_scatter(totals[0], ("dp", "fsdp"), scatter_dimension=0, tiled=True),
        lax.psum_scatter(totals[1], ("dp", "fsdp"), scatter_dimension=0, tiled=True),
        lax.psum_scatter(totals[2], ("dp", "fsdp"), scatter_dimension=0, tiled=True),
        lax.psum_scatter(totals[3], ("dp", "fsdp"), scatter_dimension=0, tiled=True),
        lax.psum_scatter(totals[4], ("dp", "fsdp"), scatter_dimension=0, tiled=True),
        lax.psum_scatter(totals[5], ("dp", "fsdp"), scatter_dimension=0, tiled=True),
        lax.psum_scatter(totals[6], ("dp", "fsdp"), scatter_dimension=0, tiled=True),
        lax.psum_scatter(totals[7], ("dp", "fsdp"), scatter_dimension=0, tiled=True),
        lax.psum_scatter(totals[8], ("dp", "fsdp"), scatter_dimension=0, tiled=True),
        lax.psum_scatter(totals[9], ("dp", "fsdp"), scatter_dimension=0, tiled=True),
        lax.psum_scatter(totals[10], ("dp", "fsdp"), scatter_dimension=0, tiled=True),
        lax.psum_scatter(totals[11], ("dp", "fsdp"), scatter_dimension=0, tiled=True),
    )
    return (
        jnp.stack(outputs_yp),
        jnp.stack(outputs_yc),
        jnp.stack(outputs_dxp),
        jnp.stack(outputs_dxc),
        results[0],
        results[1],
        results[2],
        results[3],
        results[4],
        results[5],
        results[6],
        results[7],
        results[8],
        results[9],
        results[10],
        results[11],
    )


NCONT = 2
ROWS = PROMPT + NCONT * CONT
SEQ = PROMPT + CONT
SCALE = HEAD_DIM ** (-0.5)
SELECT_GAIN = 4.0 / SEQ
PAIR = 2 * HEAD_DIM
BLOCKS = ((0, 256, 256), (256, 256, 512), (512, 256, 768), (768, 256, 1024), (1024, 64, ROWS))
TAIL = PROMPT - 768
F32 = jnp.float32
B16 = jnp.bfloat16


def mm(a, b):
    return lax.dot_general(a, b, (((1,), (0,)), ((), ())), preferred_element_type=F32)


def mm_nt(a, b):
    return lax.dot_general(a, b, (((1,), (1,)), ((), ())), preferred_element_type=F32)


def masked_half(values, half):
    lane = lax.broadcasted_iota(jnp.int32, values.shape, 1)
    return jnp.where(lane // HEAD_DIM == half, values, 0.0).astype(B16)


def block_masks(place):
    first, rows, keys = BLOCKS[place]
    key_id = lax.broadcasted_iota(jnp.int32, (keys, rows), 0)
    row_id = first + lax.broadcasted_iota(jnp.int32, (keys, rows), 1)
    visible = key_id <= row_id
    if first >= SEQ:
        visible = visible & ((key_id < PROMPT) | (key_id >= SEQ))
    chosen = visible & (key_id < row_id) & (key_id > 0)
    return visible, chosen


def split_mm(values, ones):
    high = values.astype(B16)
    low = (values - high.astype(F32)).astype(B16)
    return mm(high, ones) + mm(low, ones)


def triangle(rows, later):
    a = lax.broadcasted_iota(jnp.int32, (rows, rows), 0)
    b = lax.broadcasted_iota(jnp.int32, (rows, rows), 1)
    return jnp.where((a > b) if later else (a < b), 1.0, 0.0).astype(B16)


def forward_kernel(q_ref, k_ref, v_ref, o_ref, lse_ref, b0, b1, b2, b3, b4, vt_ref, ot_ref):
    bias_refs = (b0, b1, b2, b3, b4)
    head = pl.program_id(0)
    half = head % 2
    queries = masked_half(q_ref[...].astype(F32) * SCALE, half)

    @pl.when(head == 0)
    def _():
        carry = None
        for place, (first, rows, keys) in enumerate(BLOCKS):
            scores = mm_nt(k_ref[:keys], queries[first : first + rows])
            visible, chosen = block_masks(place)
            select = jnp.where(chosen, jnp.maximum(scores, 0.0), 0.0)
            penalty = split_mm(select, triangle(rows, False))
            if carry is not None:
                grown = jnp.zeros((keys - carry.shape[0], 1), F32)
                penalty = penalty + jnp.concatenate([carry, grown], 0)
            bias_refs[place][...] = jnp.where(visible, -SELECT_GAIN * penalty, NEG)
            if first + rows == SEQ:
                lane = lax.broadcasted_iota(jnp.int32, select.shape, 1)
                select = jnp.where(lane < TAIL, select, 0.0)
            if place + 1 < len(BLOCKS):
                total = jnp.sum(select, 1, keepdims=True)
                if carry is not None:
                    total = total + jnp.concatenate([carry, grown], 0)
                carry = total

    @pl.when(half == 0)
    def _():
        vt_ref[...] = v_ref[...].astype(F32).T.astype(B16)

    own = pl.ds(pl.multiple_of(half * HEAD_DIM, HEAD_DIM), HEAD_DIM)
    for place, (first, rows, keys) in enumerate(BLOCKS):
        logits = mm_nt(k_ref[:keys], queries[first : first + rows]) + bias_refs[place][...]
        highest = jnp.max(logits, 0, keepdims=True)
        raised = jnp.exp(logits - highest)
        total = jnp.sum(raised, 0, keepdims=True)
        mixed = mm(vt_ref[own, :keys], raised.astype(B16))
        ot_ref[own, first : first + rows] = mixed * (1.0 / total)
        lse_ref[0, :, first : first + rows] = highest + jnp.log(total)

    @pl.when(half == 1)
    def _():
        o_ref[...] = ot_ref[...].T.astype(B16)


def backward_kernel(
    q_ref, k_ref, v_ref, g_ref, lse_ref, b0, b1, b2, b3, b4,
    joined_ref,
    kt_ref, dqt_ref, dk_acc, dv_acc, p0, p1, p2, p3, p4, stage_ref, sems,
):
    bias_refs = (b0, b1, b2, b3, b4)
    pen_refs = (p0, p1, p2, p3, p4)
    head = HEADS - 1 - pl.program_id(0)
    half = head % 2
    queries = masked_half(q_ref[...].astype(F32) * SCALE, half)
    grads = masked_half(g_ref[...].astype(F32), half)
    own = pl.ds(pl.multiple_of(half * HEAD_DIM, HEAD_DIM), HEAD_DIM)

    @pl.when(head == HEADS - 1)
    def _():
        for pen in pen_refs:
            pen[...] = jnp.zeros_like(pen)

    @pl.when(half == 1)
    def _():
        kt_ref[...] = k_ref[...].astype(F32).T.astype(B16)
        dk_acc[...] = jnp.zeros_like(dk_acc)
        dv_acc[...] = jnp.zeros_like(dv_acc)

    def softmax_grad(place):
        first, rows, keys = BLOCKS[place]
        scores = mm_nt(k_ref[:keys], queries[first : first + rows])
        shares = jnp.exp(scores + bias_refs[place][...] - lse_ref[0, :, first : first + rows])
        back = mm_nt(v_ref[:keys], grads[first : first + rows])
        inner = jnp.sum(shares * back, 0, keepdims=True)
        dv_acc[:keys] += mm(shares.astype(B16), grads[first : first + rows])
        return scores, shares * (back - inner)

    def score_grad(place, grad):
        first, rows, keys = BLOCKS[place]
        grad = grad.astype(B16)
        dqt_ref[own, first : first + rows] = mm(kt_ref[own, :keys], grad)
        dk_acc[:keys] += mm(grad, queries[first : first + rows])

    @pl.when(head != 0)
    def _():
        for place in range(len(BLOCKS)):
            _, grad = softmax_grad(place)
            pen_refs[place][...] += grad
            score_grad(place, grad)

    @pl.when(head == 0)
    def _():
        carry = None
        for place in reversed(range(len(BLOCKS))):
            first, rows, keys = BLOCKS[place]
            scores, grad = softmax_grad(place)
            whole = pen_refs[place][...] + grad
            later = split_mm(whole, triangle(rows, True))
            total = jnp.sum(whole, 1, keepdims=True)
            if carry is not None:
                if first + rows == SEQ:
                    lane = lax.broadcasted_iota(jnp.int32, (keys, rows), 1)
                    later = later + jnp.where(lane < TAIL, carry[:keys], 0.0)
                else:
                    later = later + carry[:keys]
                total = total + carry[:keys]
            carry = total
            _, chosen = block_masks(place)
            grad = grad + jnp.where(chosen & (scores > 0.0), -SELECT_GAIN * later, 0.0)
            score_grad(place, grad)

    def copies(pair):
        return [
            pltpu.make_async_copy(
                stage_ref.at[part],
                joined_ref.at[:, pl.ds(pl.multiple_of(part * D + pair * PAIR, PAIR), PAIR)],
                sems.at[part],
            )
            for part in range(3)
        ]

    @pl.when((half == 0) & (head != HEADS - 2))
    def _():
        for copy in copies(head // 2 + 1):
            copy.wait()

    @pl.when(half == 0)
    def _():
        stage_ref[0] = (dqt_ref[...].T * SCALE).astype(B16)
        stage_ref[1] = dk_acc[...].astype(B16)
        stage_ref[2] = dv_acc[...].astype(B16)
        for copy in copies(head // 2):
            copy.start()

    @pl.when(head == 0)
    def _():
        for copy in copies(0):
            copy.wait()


def pair_spec(index):
    return pl.BlockSpec((ROWS, PAIR), index)


def whole_specs():
    return [pl.BlockSpec((keys, rows), lambda i: (0, 0)) for _, rows, keys in BLOCKS]


PAIRS = HEADS // 2


def attend_forward(joined):
    return pl.pallas_call(
        forward_kernel,
        grid=(HEADS,),
        in_specs=[
            pair_spec(lambda i: (0, i // 2)),
            pair_spec(lambda i: (0, PAIRS + i // 2)),
            pair_spec(lambda i: (0, 2 * PAIRS + i // 2)),
        ],
        out_specs=[
            pair_spec(lambda i: (0, i // 2)),
            pl.BlockSpec((1, 1, ROWS), lambda i: (i, 0, 0)),
            *whole_specs(),
        ],
        out_shape=[
            jax.ShapeDtypeStruct((ROWS, D), B16),
            jax.ShapeDtypeStruct((HEADS, 1, ROWS), F32),
            *(jax.ShapeDtypeStruct((keys, rows), F32) for _, rows, keys in BLOCKS),
        ],
        scratch_shapes=[pltpu.VMEM((PAIR, ROWS), B16), pltpu.VMEM((PAIR, ROWS), F32)],
        name="attend_forward",
    )(joined, joined, joined)


def attend_backward(joined, grad_mixed, lse, biases):
    last = PAIRS - 1
    return pl.pallas_call(
        backward_kernel,
        grid=(HEADS,),
        in_specs=[
            pair_spec(lambda i: (0, last - i // 2)),
            pair_spec(lambda i: (0, PAIRS + last - i // 2)),
            pair_spec(lambda i: (0, 2 * PAIRS + last - i // 2)),
            pair_spec(lambda i: (0, last - i // 2)),
            pl.BlockSpec((1, 1, ROWS), lambda i: (HEADS - 1 - i, 0, 0)),
            *whole_specs(),
        ],
        out_specs=pl.BlockSpec(memory_space=pl.ANY),
        out_shape=jax.ShapeDtypeStruct((ROWS, 3 * D), B16),
        scratch_shapes=[
            pltpu.VMEM((PAIR, ROWS), B16),
            pltpu.VMEM((PAIR, ROWS), F32),
            pltpu.VMEM((ROWS, PAIR), F32),
            pltpu.VMEM((ROWS, PAIR), F32),
            *(pltpu.VMEM((keys, rows), F32) for _, rows, keys in BLOCKS),
            pltpu.VMEM((3, ROWS, PAIR), B16),
            pltpu.SemaphoreType.DMA((3,)),
        ],
        name="attend_backward",
    )(joined, joined, joined, grad_mixed, lse, *biases)


EVERY = ("dp", "fsdp")
CORE = 2
PLANE = (0, 1, 4, 5)


def device_count():
    return lax.axis_size("dp") * lax.axis_size("fsdp")


def depth():
    return device_count() // 8


def place_of():
    number = lax.axis_index("dp")
    return number // 4, number // 2 % 2, number % 2, lax.axis_index("fsdp")


def swap(value, mask):
    return lax.ppermute(value, EVERY, [(i, i ^ mask) for i in range(device_count())])


def arrange(pieces, own):
    pieces = list(pieces)
    bit = 1
    while bit < len(pieces):
        odd = (own // bit) % 2 == 1
        pieces = [jnp.where(odd, pieces[k ^ bit], pieces[k]) for k in range(len(pieces))]
        bit *= 2
    return pieces


def gather_steps(shard, held):
    z, x, core, y = place_of()
    column = [shard] + [swap(shard, 8 * k) for k in range(1, depth())]
    *column, held = lax.optimization_barrier((*column, held))
    value = jnp.stack(arrange(column, z))
    plane = [value] + [swap(value, mask) for mask in PLANE[1:]]
    plane = arrange(plane, 2 * x + y)
    value = jnp.stack([jnp.stack(plane[:2], 1), jnp.stack(plane[2:], 1)], 1)
    value = jnp.stack(arrange([value, swap(value, CORE)], core), 2)
    return value.reshape(-1, shard.shape[1]), held


def take(value, index, axis):
    return lax.dynamic_index_in_dim(value, index, axis, keepdims=False)


def add_up(pieces):
    total = pieces[0].astype(F32)
    for piece in pieces[1:]:
        total = total + piece.astype(F32)
    return total


def scatter_steps(grad):
    return scatter_chips(scatter_core(grad))


def scatter_core(grad):
    core = place_of()[2]
    rows = grad.shape[0] // device_count()
    value = grad.reshape(depth(), 2, 2, 2, rows, grad.shape[1])
    other = swap(take(value, 1 - core, 2), CORE)
    return take(value, core, 2) + other


def scatter_chips(value):
    z, x, _, y = place_of()
    plane = [
        take(take(value, x ^ (mask // 4), 1), y ^ (mask % 2), 1) for mask in PLANE
    ]
    others = [swap(piece, mask) for piece, mask in zip(plane[1:], PLANE[1:])]
    value = add_up(plane[:1] + others).astype(B16)
    column = [take(value, z ^ k, 0) for k in range(depth())]
    others = [swap(column[k], 8 * k) for k in range(1, depth())]
    return add_up(column[:1] + others)


def pack_vectors(vectors, kind):
    rows = D // device_count()
    flat = jnp.concatenate([v.reshape(-1, v.shape[0] // vectors[0].shape[0] * rows) for v in vectors], 1)
    flat = flat.astype(kind).reshape(-1, 3, flat.shape[1] // 3)
    flat = jnp.pad(flat, ((0, 0), (0, rows - 3), (0, 128 - flat.shape[2])))
    return flat.reshape(-1, 128)


def unpack_vectors(columns, sizes):
    rows = D // device_count()
    width = sum(sizes) // 3
    flat = columns.reshape(-1, rows, 128)[:, :3, :width].reshape(-1, 3 * width)
    out, start = [], 0
    for size in sizes:
        out.append(flat[:, start : start + size].reshape(-1).astype(F32))
        start += size
    return out


def gelu_pair(upward):
    rate = (2.0 / jnp.pi) ** 0.5
    square = upward * upward
    bend = jnp.tanh(rate * (upward + 0.044715 * (square * upward)))
    gate = 0.5 * (1.0 + bend)
    slope = gate + 0.5 * upward * (1.0 - bend * bend) * (rate * (1.0 + 3 * 0.044715 * square))
    return (upward * gate).astype(B16), slope.astype(B16)


def normalize_back(values, gain, grad):
    center = values - jnp.mean(values, -1, keepdims=True)
    rate = lax.rsqrt(jnp.mean(center * center, -1, keepdims=True) + EPS)
    unit = center * rate
    scaled = grad * gain
    inner = jnp.mean(scaled * unit, -1, keepdims=True)
    back = rate * (scaled - jnp.mean(scaled, -1, keepdims=True) - unit * inner)
    return back, jnp.sum(grad * unit, 0), jnp.sum(grad, 0)


def pick(first, second, when):
    return jnp.where(when, first, second)


def trade_rows(prompt, cont):
    place = lax.axis_index("fsdp")
    low = place == 0
    swap_pairs = [(0, 1), (1, 0)]
    mine = [pick(t[0], t[1], low).reshape(-1, D) for t in (prompt, cont)]
    away = [pick(t[1], t[0], low).reshape(-1, D) for t in (prompt, cont)]
    came = lax.ppermute(jnp.concatenate(away, 0), "fsdp", swap_pairs)
    half = mine[0].shape[0]
    parts = (came[:half], came[half:])
    return jnp.concatenate(
        [
            pick(mine[0], parts[0], low),
            pick(parts[0], mine[0], low),
            pick(mine[1], parts[1], low),
            pick(parts[1], mine[1], low),
        ],
        0,
    )


def return_rows(whole, kind):
    place = lax.axis_index("fsdp")
    low = place == 0
    half = PROMPT // 2
    parts = (
        (whole[:half], whole[PROMPT:SEQ]),
        (whole[half:PROMPT], whole[SEQ:]),
    )
    mine = [pick(parts[0][i], parts[1][i], low) for i in range(2)]
    away = [pick(parts[1][i], parts[0][i], low) for i in range(2)]
    came = lax.ppermute(jnp.concatenate(away, 0).astype(B16), "fsdp", [(0, 1), (1, 0)])
    came = (came[:half], came[half:])
    out = []
    for i in range(2):
        own, other = mine[i].astype(kind), came[i].astype(kind)
        out.append(jnp.stack([pick(own, other, low), pick(other, own, low)]))
    return out[0][:, None], out[1][:, None, None]


def whole_layer(*args):
    return whole_steps(*args)


def whole_steps(
    x_prompt, x_cont, dy_prompt, dy_cont,
    ln1_gain, ln1_bias, w_qkv, b_qv, w_out, b_out,
    ln2_gain, ln2_bias, w_up, b_up, w_down, b_down,
):
    devices = device_count()
    vectors = (ln1_gain, ln1_bias, b_qv, b_out, ln2_gain, ln2_bias, b_up, b_down)
    sizes = [v.shape[0] for v in vectors]
    chunks = w_down.shape[0] // w_qkv.shape[0]
    rows = w_qkv.shape[0]
    flat_x = trade_rows(x_prompt, x_cont).astype(F32)
    rest = jnp.concatenate(
        [w_out, *(w_up[:, i * D : (i + 1) * D] for i in range(chunks)), w_down], 0
    )
    full_first, rest = gather_steps(jnp.concatenate([w_qkv, pack_vectors(vectors, B16)], 1), rest)
    full_rest = lax.all_gather(rest, EVERY, axis=0)
    full_qkv = full_first[:, : 3 * D]
    (
        gain_one, shift_one, bias_qv, bias_out, gain_two, shift_two, bias_up, bias_down,
    ) = unpack_vectors(full_first[:, 3 * D :], sizes)
    hidden = w_up.shape[1]
    full_out = full_rest[:, :rows].reshape(D, D)
    full_up = jnp.concatenate(
        [full_rest[:, rows * i : rows * (i + 1)].reshape(D, D) for i in range(1, chunks + 1)], 1
    )
    full_down = full_rest[:, rows * (chunks + 1) :].reshape(hidden, D)

    normed_one = normalize(flat_x, gain_one, shift_one).astype(B16)
    bias_joined = jnp.concatenate([bias_qv[:D], jnp.zeros((D,), F32), bias_qv[D:]])
    joined = (
        jnp.dot(normed_one, full_qkv, preferred_element_type=F32) + bias_joined
    ).astype(B16)
    joined, dy_prompt, dy_cont = lax.optimization_barrier((joined, dy_prompt, dy_cont))
    grad_y = trade_rows(dy_prompt, dy_cont)
    mixed, lse, *biases = attend_forward(joined)
    residual = flat_x + (jnp.dot(mixed, full_out, preferred_element_type=F32) + bias_out)
    normed_two = normalize(residual, gain_two, shift_two).astype(B16)
    upward = jnp.dot(normed_two, full_up, preferred_element_type=F32) + bias_up
    active, slope = lax.optimization_barrier(gelu_pair(upward))

    def weight_grad(left, right):
        return jnp.einsum("rd,re->de", left, right, preferred_element_type=F32).astype(B16)

    def through(grad, weight):
        return jnp.einsum("re,de->rd", grad, weight, preferred_element_type=F32)

    def column_sum(values):
        return jnp.sum(values.astype(F32), 0)

    grad_upward = (through(grad_y, full_down) * slope.astype(F32)).astype(B16)
    grad_down = weight_grad(active, grad_y)
    grad_up = weight_grad(normed_two, grad_upward)
    packed_grads = jnp.concatenate(
        [
            *(grad_up[:, i * D : (i + 1) * D].reshape(devices, rows, D) for i in range(chunks)),
            grad_down.reshape(devices, -1, D),
        ],
        1,
    )
    packed_grads, active, grad_upward = lax.optimization_barrier(
        (packed_grads, active, grad_upward)
    )
    own_hidden = lax.psum_scatter(packed_grads, EVERY, scatter_dimension=0).astype(F32)
    grad_w_up = jnp.concatenate(
        [own_hidden[i * rows : (i + 1) * rows] for i in range(chunks)], 1
    )
    grad_w_down = own_hidden[chunks * rows :]
    output = residual + (jnp.dot(active, full_down, preferred_element_type=F32) + bias_down)
    y_prompt, y_cont = return_rows(output.astype(B16), B16)

    grad_b_down = column_sum(grad_y)
    grad_b_up = column_sum(grad_upward)
    grad_resid, grad_gain_two, grad_shift_two = normalize_back(
        residual, gain_two, through(grad_upward, full_up)
    )
    grad_resid = grad_y.astype(F32) + grad_resid
    grad_branch = grad_resid.astype(B16)
    grad_w_out = scatter_steps(weight_grad(mixed, grad_branch))
    grad_b_out = column_sum(grad_branch)
    grad_mixed = through(grad_branch, full_out).astype(B16)
    grad_joined = attend_backward(joined, grad_mixed, lse, biases)
    grad_qkv = weight_grad(normed_one, grad_joined)
    grad_qkv, grad_joined = lax.optimization_barrier((grad_qkv, grad_joined))
    grad_b_qv = jnp.concatenate(
        [column_sum(grad_joined[:, :D]), column_sum(grad_joined[:, 2 * D :])]
    )
    first = scatter_core(grad_qkv)
    back_one = through(grad_joined, full_qkv)
    first, back_one = lax.optimization_barrier((first, back_one))
    grad_input, grad_gain_one, grad_shift_one = normalize_back(flat_x, gain_one, back_one)
    dx_prompt, dx_cont = return_rows(grad_resid + grad_input, F32)

    small = (
        grad_gain_one, grad_shift_one, grad_b_qv, grad_b_out,
        grad_gain_two, grad_shift_two, grad_b_up, grad_b_down,
    )
    own_first = scatter_chips(first)
    own_vectors = scatter_steps(pack_vectors(small, B16))
    grad_w_qkv = own_first
    pieces = unpack_vectors(own_vectors, sizes)
    return (
        y_prompt, y_cont, dx_prompt, dx_cont,
        pieces[0], pieces[1], grad_w_qkv, pieces[2], grad_w_out, pieces[3],
        pieces[4], pieces[5], grad_w_up, pieces[6], grad_w_down, pieces[7],
    )


def solution(mesh):
    sizes = dict(mesh.shape)
    whole = sizes["fsdp"] == MICRO == NCONT and sizes["dp"] & (sizes["dp"] - 1) == 0
    return jax.shard_map(
        whole_layer if whole else spread_layer,
        mesh=mesh,
        in_specs=(
            P(None, "dp", "fsdp", None),
            P(None, "dp", "fsdp", None, None),
            P(None, "dp", "fsdp", None),
            P(None, "dp", "fsdp", None, None),
            P(("dp", "fsdp")),
            P(("dp", "fsdp")),
            P(("dp", "fsdp"), None),
            P(("dp", "fsdp")),
            P(("dp", "fsdp"), None),
            P(("dp", "fsdp")),
            P(("dp", "fsdp")),
            P(("dp", "fsdp")),
            P(("dp", "fsdp"), None),
            P(("dp", "fsdp")),
            P(("dp", "fsdp"), None),
            P(("dp", "fsdp")),
        ),
        out_specs=(
            P(None, "dp", "fsdp", None),
            P(None, "dp", "fsdp", None, None),
            P(None, "dp", "fsdp", None),
            P(None, "dp", "fsdp", None, None),
            P(("dp", "fsdp")),
            P(("dp", "fsdp")),
            P(("dp", "fsdp"), None),
            P(("dp", "fsdp")),
            P(("dp", "fsdp"), None),
            P(("dp", "fsdp")),
            P(("dp", "fsdp")),
            P(("dp", "fsdp")),
            P(("dp", "fsdp"), None),
            P(("dp", "fsdp")),
            P(("dp", "fsdp"), None),
            P(("dp", "fsdp")),
        ),
        check_vma=False,
    )
```

```python
from functools import partial

import jax
import jax.numpy as jnp
from jax import lax
from jax.experimental import pallas as pl
from jax.experimental.pallas import tpu as pltpu
from jax.sharding import PartitionSpec as P


D = 768
HEADS = 12
HEAD_DIM = 64
PROMPT = 960
CONT = 64
MICRO = 2


EPS = 1e-05
NEG = -1e30


def normalize(values, gain, shift):
    center = values - jnp.mean(values, -1, keepdims=True)
    spread = jnp.mean(center * center, -1, keepdims=True)
    return center * lax.rsqrt(spread + EPS) * gain + shift


def later_sum(values):
    return jnp.flip(jnp.cumsum(jnp.flip(values, 1), 1), 1) - values


def attend_group(inputs_g, causal, score_scale):
    query_g, key_g, value_g, penalty_g = inputs_g
    rows_here = query_g.shape[0]
    heads_q = query_g.reshape(rows_here, HEADS, HEAD_DIM)
    heads_k = key_g.reshape(-1, HEADS, HEAD_DIM)
    heads_v = value_g.reshape(-1, HEADS, HEAD_DIM)
    scores = (
        jnp.einsum("rhd,khd->hrk", heads_q, heads_k, preferred_element_type=jnp.float32)
        * score_scale
    )
    logits = jnp.where(causal[None], scores - penalty_g[None], NEG)
    highest = jnp.max(logits, -1, keepdims=True)
    raised = jnp.exp(logits - highest)
    totals = jnp.sum(raised, -1, keepdims=True)
    weights_b = (raised / totals).astype(jnp.bfloat16)
    mixture = jnp.einsum("hrk,khd->rhd", weights_b, heads_v, preferred_element_type=jnp.float32)
    return (
        mixture.reshape(rows_here, -1).astype(jnp.bfloat16),
        (highest + jnp.log(totals))[..., 0],
    )


def attend_back(inputs_g, causal, score_scale):
    query_g, key_g, value_g, penalty_g, grad_mix, log_totals = inputs_g
    rows_here = query_g.shape[0]
    heads_q = query_g.reshape(rows_here, HEADS, HEAD_DIM)
    heads_k = key_g.reshape(-1, HEADS, HEAD_DIM)
    heads_v = value_g.reshape(-1, HEADS, HEAD_DIM)
    heads_g = grad_mix.reshape(rows_here, HEADS, HEAD_DIM)
    scores = (
        jnp.einsum("rhd,khd->hrk", heads_q, heads_k, preferred_element_type=jnp.float32)
        * score_scale
    )
    logits = jnp.where(causal[None], scores - penalty_g[None], NEG)
    softmax_w = jnp.exp(logits - log_totals[..., None])
    grad_soft = jnp.einsum("rhd,khd->hrk", heads_g, heads_v, preferred_element_type=jnp.float32)
    inner_sum = jnp.sum(softmax_w * grad_soft, -1, keepdims=True)
    grad_logit = softmax_w * (grad_soft - inner_sum)
    grad_value = jnp.einsum(
        "hrk,rhd->khd", softmax_w.astype(jnp.bfloat16), heads_g, preferred_element_type=jnp.float32
    )
    grad_penalty = -jnp.sum(grad_logit, 0)
    rest_b = grad_logit[1:].astype(jnp.bfloat16)
    grad_query = (
        jnp.einsum("hrk,khd->rhd", rest_b, heads_k[:, 1:], preferred_element_type=jnp.float32)
        * score_scale
    )
    grad_key = (
        jnp.einsum("hrk,rhd->khd", rest_b, heads_q[:, 1:], preferred_element_type=jnp.float32)
        * score_scale
    )
    return (
        grad_value.reshape(-1, D),
        grad_query.reshape(rows_here, -1),
        grad_key.reshape(grad_key.shape[0], -1),
        grad_logit[0],
        grad_penalty,
    )


def spread_layer(
    x_prompt,
    x_cont,
    dy_prompt,
    dy_cont,
    ln1_gain,
    ln1_bias,
    w_qkv,
    b_qv,
    w_out,
    b_out,
    ln2_gain,
    ln2_bias,
    w_up,
    b_up,
    w_down,
    b_down,
):
    shards = (
        ln1_gain,
        ln1_bias,
        w_qkv,
        b_qv,
        w_out,
        b_out,
        ln2_gain,
        ln2_bias,
        w_up,
        b_up,
        w_down,
        b_down,
    )
    groups_here = x_prompt.shape[1]
    prompt_rows = x_prompt.shape[2]
    fsdp_count = lax.axis_size("fsdp")
    fsdp_place = lax.axis_index("fsdp")
    key_count = PROMPT + CONT
    score_scale = HEAD_DIM ** (-0.5)
    select_gain = 4.0 / (PROMPT + CONT)
    query_pos = jnp.concatenate(
        [
            fsdp_place * prompt_rows + jnp.arange(prompt_rows, dtype=jnp.int32),
            PROMPT + jnp.arange(CONT, dtype=jnp.int32),
        ]
    )
    key_pos = jnp.arange(key_count, dtype=jnp.int32)
    causal = key_pos[None, :] <= query_pos[:, None]
    chosen = (key_pos[None, :] < query_pos[:, None]) & (key_pos[None, :] > 0)
    lower_mask = (jnp.arange(fsdp_count, dtype=jnp.int32) < fsdp_place).astype(jnp.float32)
    pad_zeros = jnp.zeros((groups_here, CONT), jnp.float32)
    forward_attend = partial(attend_group, causal=causal, score_scale=score_scale)
    backward_attend = partial(attend_back, causal=causal, score_scale=score_scale)
    totals = tuple(
        (
            jnp.zeros(
                (single.shape[0] * lax.axis_size(("dp", "fsdp")),) + single.shape[1:], jnp.float32
            )
            for single in shards
        )
    )
    outputs_yp, outputs_yc, outputs_dxp, outputs_dxc = ([], [], [], [])
    for batch_index in range(MICRO):
        gathered = (
            lax.all_gather(shards[0], ("dp", "fsdp"), axis=0, tiled=True),
            lax.all_gather(shards[1], ("dp", "fsdp"), axis=0, tiled=True),
            lax.all_gather(shards[2], ("dp", "fsdp"), axis=0, tiled=True),
            lax.all_gather(shards[3], ("dp", "fsdp"), axis=0, tiled=True),
            lax.all_gather(shards[4], ("dp", "fsdp"), axis=0, tiled=True),
            lax.all_gather(shards[5], ("dp", "fsdp"), axis=0, tiled=True),
            lax.all_gather(shards[6], ("dp", "fsdp"), axis=0, tiled=True),
            lax.all_gather(shards[7], ("dp", "fsdp"), axis=0, tiled=True),
            lax.all_gather(shards[8], ("dp", "fsdp"), axis=0, tiled=True),
            lax.all_gather(shards[9], ("dp", "fsdp"), axis=0, tiled=True),
            lax.all_gather(shards[10], ("dp", "fsdp"), axis=0, tiled=True),
            lax.all_gather(shards[11], ("dp", "fsdp"), axis=0, tiled=True),
        )
        inputs_x = jnp.concatenate([x_prompt[batch_index], x_cont[batch_index][:, 0]], 1).astype(
            jnp.float32
        )
        local_rows = inputs_x.shape[1]
        flat_x = inputs_x.reshape(-1, D)
        normed_one = normalize(
            flat_x, gathered[0].astype(jnp.float32), gathered[1].astype(jnp.float32)
        ).astype(jnp.bfloat16)
        joined = jnp.dot(normed_one, gathered[2], preferred_element_type=jnp.float32)
        bias_qv = gathered[3].astype(jnp.float32)
        queries = (
            (joined[:, :D] + bias_qv[:D]).astype(jnp.bfloat16).reshape(groups_here, local_rows, D)
        )
        keys_own = joined[:, D : 2 * D].astype(jnp.bfloat16).reshape(groups_here, local_rows, D)
        values_own = (
            (joined[:, 2 * D :] + bias_qv[D:])
            .astype(jnp.bfloat16)
            .reshape(groups_here, local_rows, D)
        )
        prompt_pair = jnp.concatenate([keys_own[:, :prompt_rows], values_own[:, :prompt_rows]], 2)
        whole_kv = lax.all_gather(prompt_pair, "fsdp", axis=1, tiled=True)
        keys_all = jnp.concatenate([whole_kv[..., :D], keys_own[:, prompt_rows:]], 1)
        values_all = jnp.concatenate([whole_kv[..., D:], values_own[:, prompt_rows:]], 1)
        score_zero = (
            jnp.einsum(
                "grd,gkd->grk",
                queries[..., :HEAD_DIM],
                keys_all[..., :HEAD_DIM],
                preferred_element_type=jnp.float32,
            )
            * score_scale
        )
        select = jnp.where(chosen[None], jnp.maximum(score_zero, 0.0), 0.0)
        own_part = jnp.sum(select[:, :prompt_rows, :PROMPT], 1)
        all_parts = lax.all_gather(own_part[None], "fsdp", axis=0, tiled=True)
        prefix = jnp.sum(all_parts * lower_mask[:, None, None], 0)
        whole_sum = jnp.sum(all_parts, 0)
        select_p = select[:, :prompt_rows]
        select_c = select[:, prompt_rows:]
        penalty = select_gain * jnp.concatenate(
            [
                jnp.concatenate([prefix, pad_zeros], 1)[:, None]
                + (jnp.cumsum(select_p, 1) - select_p),
                jnp.concatenate([whole_sum, pad_zeros], 1)[:, None]
                + (jnp.cumsum(select_c, 1) - select_c),
            ],
            1,
        )
        mixture, log_totals = lax.map(forward_attend, (queries, keys_all, values_all, penalty))
        mixed_flat = mixture.reshape(-1, D)
        residual = flat_x + (
            jnp.dot(mixed_flat, gathered[4], preferred_element_type=jnp.float32)
            + gathered[5].astype(jnp.float32)
        )
        normed_two = normalize(
            residual, gathered[6].astype(jnp.float32), gathered[7].astype(jnp.float32)
        ).astype(jnp.bfloat16)
        upward = jnp.dot(normed_two, gathered[8], preferred_element_type=jnp.float32) + gathered[
            9
        ].astype(jnp.float32)
        active, gelu_back = jax.vjp(partial(jax.nn.gelu, approximate=True), upward)
        active_b = active.astype(jnp.bfloat16)
        output = residual + (
            jnp.dot(active_b, gathered[10], preferred_element_type=jnp.float32)
            + gathered[11].astype(jnp.float32)
        )
        output_b = output.astype(jnp.bfloat16).reshape(groups_here, local_rows, D)
        outputs_yp.append(output_b[:, :prompt_rows])
        outputs_yc.append(output_b[:, prompt_rows:][:, None])
        back_set = (
            lax.all_gather(shards[0], ("dp", "fsdp"), axis=0, tiled=True),
            lax.all_gather(shards[1], ("dp", "fsdp"), axis=0, tiled=True),
            lax.all_gather(shards[2], ("dp", "fsdp"), axis=0, tiled=True),
            lax.all_gather(shards[3], ("dp", "fsdp"), axis=0, tiled=True),
            lax.all_gather(shards[4], ("dp", "fsdp"), axis=0, tiled=True),
            lax.all_gather(shards[5], ("dp", "fsdp"), axis=0, tiled=True),
            lax.all_gather(shards[6], ("dp", "fsdp"), axis=0, tiled=True),
            lax.all_gather(shards[7], ("dp", "fsdp"), axis=0, tiled=True),
            lax.all_gather(shards[8], ("dp", "fsdp"), axis=0, tiled=True),
            lax.all_gather(shards[9], ("dp", "fsdp"), axis=0, tiled=True),
            lax.all_gather(shards[10], ("dp", "fsdp"), axis=0, tiled=True),
            lax.all_gather(shards[11], ("dp", "fsdp"), axis=0, tiled=True),
        )
        grad_out_y = jnp.concatenate(
            [dy_prompt[batch_index], dy_cont[batch_index][:, 0]], 1
        ).reshape(-1, D)
        grad_down = jnp.einsum(
            "rf,rd->fd", active_b, grad_out_y, preferred_element_type=jnp.float32
        )
        grad_bdown = jnp.sum(grad_out_y.astype(jnp.float32), 0)
        grad_active = jnp.einsum(
            "rd,fd->rf", grad_out_y, back_set[10], preferred_element_type=jnp.float32
        )
        grad_upward = gelu_back(grad_active)[0].astype(jnp.bfloat16)
        grad_up = jnp.einsum(
            "rd,rf->df", normed_two, grad_upward, preferred_element_type=jnp.float32
        )
        grad_bup = jnp.sum(grad_upward.astype(jnp.float32), 0)
        grad_normed = jnp.einsum(
            "rf,df->rd", grad_upward, back_set[8], preferred_element_type=jnp.float32
        )
        _, norm_back = jax.vjp(
            normalize, residual, back_set[6].astype(jnp.float32), back_set[7].astype(jnp.float32)
        )
        grad_resid, grad_gain_two, grad_shift_two = norm_back(grad_normed)
        grad_resid = grad_out_y.astype(jnp.float32) + grad_resid
        grad_branch = grad_resid.astype(jnp.bfloat16)
        grad_wout = jnp.einsum(
            "rd,re->de", mixed_flat, grad_branch, preferred_element_type=jnp.float32
        )
        grad_bout = jnp.sum(grad_branch.astype(jnp.float32), 0)
        grad_mixed = jnp.einsum(
            "re,de->rd", grad_branch, back_set[4], preferred_element_type=jnp.float32
        )
        grad_mixed = grad_mixed.astype(jnp.bfloat16).reshape(groups_here, local_rows, D)
        back_values, back_queries, back_keys, back_zero, back_penalty = lax.map(
            backward_attend, (queries, keys_all, values_all, penalty, grad_mixed, log_totals)
        )
        prefix_grad = select_gain * jnp.sum(back_penalty[:, :prompt_rows, :PROMPT], 1)
        whole_grad = select_gain * jnp.sum(back_penalty[:, prompt_rows:, :PROMPT], 1)
        spread_back = prefix_grad[None] * lower_mask[:, None, None] + whole_grad[None]
        part_grad = lax.psum_scatter(spread_back, "fsdp", scatter_dimension=0, tiled=True)[0]
        select_back = jnp.concatenate(
            [
                select_gain * later_sum(back_penalty[:, :prompt_rows])
                + jnp.concatenate([part_grad, pad_zeros], 1)[:, None],
                select_gain * later_sum(back_penalty[:, prompt_rows:]),
            ],
            1,
        )
        grad_zero = (
            back_zero + jnp.where(chosen[None] & (score_zero > 0), select_back, 0.0)
        ).astype(jnp.bfloat16)
        query_zero = (
            jnp.einsum(
                "grk,gkd->grd",
                grad_zero,
                keys_all[..., :HEAD_DIM],
                preferred_element_type=jnp.float32,
            )
            * score_scale
        )
        key_zero = (
            jnp.einsum(
                "grk,grd->gkd",
                grad_zero,
                queries[..., :HEAD_DIM],
                preferred_element_type=jnp.float32,
            )
            * score_scale
        )
        grad_queries = jnp.concatenate([query_zero, back_queries], 2)
        grad_keys = jnp.concatenate([key_zero, back_keys], 2)
        prompt_back = jnp.concatenate([grad_keys[:, :PROMPT], back_values[:, :PROMPT]], 2)
        own_back = lax.psum_scatter(
            prompt_back.astype(jnp.bfloat16), "fsdp", scatter_dimension=1, tiled=True
        ).astype(jnp.float32)
        keys_back = jnp.concatenate([own_back[..., :D], grad_keys[:, PROMPT:]], 1)
        values_back = jnp.concatenate([own_back[..., D:], back_values[:, PROMPT:]], 1)
        grad_joined = (
            jnp.concatenate([grad_queries, keys_back, values_back], 2)
            .astype(jnp.bfloat16)
            .reshape(-1, 3 * D)
        )
        grad_wqkv = jnp.einsum(
            "rd,re->de", normed_one, grad_joined, preferred_element_type=jnp.float32
        )
        grad_bqv = jnp.concatenate(
            [
                jnp.sum(grad_joined[:, :D].astype(jnp.float32), 0),
                jnp.sum(grad_joined[:, 2 * D :].astype(jnp.float32), 0),
            ]
        )
        grad_normed_one = jnp.einsum(
            "re,de->rd", grad_joined, back_set[2], preferred_element_type=jnp.float32
        )
        _, norm_back_one = jax.vjp(
            normalize, flat_x, back_set[0].astype(jnp.float32), back_set[1].astype(jnp.float32)
        )
        grad_input, grad_gain_one, grad_shift_one = norm_back_one(grad_normed_one)
        grad_input = (grad_resid + grad_input).reshape(groups_here, local_rows, D)
        outputs_dxp.append(grad_input[:, :prompt_rows])
        outputs_dxc.append(grad_input[:, prompt_rows:][:, None])
        micro_grads = (
            grad_gain_one,
            grad_shift_one,
            grad_wqkv,
            grad_bqv,
            grad_wout,
            grad_bout,
            grad_gain_two,
            grad_shift_two,
            grad_up,
            grad_bup,
            grad_down,
            grad_bdown,
        )
        totals = tuple((first + second for first, second in zip(totals, micro_grads)))
    results = (
        lax.psum_scatter(totals[0], ("dp", "fsdp"), scatter_dimension=0, tiled=True),
        lax.psum_scatter(totals[1], ("dp", "fsdp"), scatter_dimension=0, tiled=True),
        lax.psum_scatter(totals[2], ("dp", "fsdp"), scatter_dimension=0, tiled=True),
        lax.psum_scatter(totals[3], ("dp", "fsdp"), scatter_dimension=0, tiled=True),
        lax.psum_scatter(totals[4], ("dp", "fsdp"), scatter_dimension=0, tiled=True),
        lax.psum_scatter(totals[5], ("dp", "fsdp"), scatter_dimension=0, tiled=True),
        lax.psum_scatter(totals[6], ("dp", "fsdp"), scatter_dimension=0, tiled=True),
        lax.psum_scatter(totals[7], ("dp", "fsdp"), scatter_dimension=0, tiled=True),
        lax.psum_scatter(totals[8], ("dp", "fsdp"), scatter_dimension=0, tiled=True),
        lax.psum_scatter(totals[9], ("dp", "fsdp"), scatter_dimension=0, tiled=True),
        lax.psum_scatter(totals[10], ("dp", "fsdp"), scatter_dimension=0, tiled=True),
        lax.psum_scatter(totals[11], ("dp", "fsdp"), scatter_dimension=0, tiled=True),
    )
    return (
        jnp.stack(outputs_yp),
        jnp.stack(outputs_yc),
        jnp.stack(outputs_dxp),
        jnp.stack(outputs_dxc),
        results[0],
        results[1],
        results[2],
        results[3],
        results[4],
        results[5],
        results[6],
        results[7],
        results[8],
        results[9],
        results[10],
        results[11],
    )


NCONT = 2
ROWS = PROMPT + NCONT * CONT
SEQ = PROMPT + CONT
SCALE = HEAD_DIM ** (-0.5)
SELECT_GAIN = 4.0 / SEQ
PAIR = 2 * HEAD_DIM
BLOCKS = ((0, 256, 256), (256, 256, 512), (512, 256, 768), (768, 256, 1024), (1024, 64, ROWS))
TAIL = PROMPT - 768
F32 = jnp.float32
B16 = jnp.bfloat16


def mm(a, b):
    return lax.dot_general(a, b, (((1,), (0,)), ((), ())), preferred_element_type=F32)


def mm_nt(a, b):
    return lax.dot_general(a, b, (((1,), (1,)), ((), ())), preferred_element_type=F32)


def masked_half(values, half):
    lane = lax.broadcasted_iota(jnp.int32, values.shape, 1)
    return jnp.where(lane // HEAD_DIM == half, values, 0.0).astype(B16)


def block_masks(place):
    first, rows, keys = BLOCKS[place]
    key_id = lax.broadcasted_iota(jnp.int32, (keys, rows), 0)
    row_id = first + lax.broadcasted_iota(jnp.int32, (keys, rows), 1)
    visible = key_id <= row_id
    if first >= SEQ:
        visible = visible & ((key_id < PROMPT) | (key_id >= SEQ))
    chosen = visible & (key_id < row_id) & (key_id > 0)
    return visible, chosen


def split_mm(values, ones):
    high = values.astype(B16)
    low = (values - high.astype(F32)).astype(B16)
    return mm(high, ones) + mm(low, ones)


def triangle(rows, later):
    a = lax.broadcasted_iota(jnp.int32, (rows, rows), 0)
    b = lax.broadcasted_iota(jnp.int32, (rows, rows), 1)
    return jnp.where((a > b) if later else (a < b), 1.0, 0.0).astype(B16)


def forward_kernel(q_ref, k_ref, v_ref, o_ref, lse_ref, b0, b1, b2, b3, b4, vt_ref, ot_ref):
    bias_refs = (b0, b1, b2, b3, b4)
    head = pl.program_id(0)
    half = head % 2
    queries = masked_half(q_ref[...].astype(F32) * SCALE, half)

    @pl.when(head == 0)
    def _():
        carry = None
        for place, (first, rows, keys) in enumerate(BLOCKS):
            scores = mm_nt(k_ref[:keys], queries[first : first + rows])
            visible, chosen = block_masks(place)
            select = jnp.where(chosen, jnp.maximum(scores, 0.0), 0.0)
            penalty = split_mm(select, triangle(rows, False))
            if carry is not None:
                grown = jnp.zeros((keys - carry.shape[0], 1), F32)
                penalty = penalty + jnp.concatenate([carry, grown], 0)
            bias_refs[place][...] = jnp.where(visible, -SELECT_GAIN * penalty, NEG)
            if first + rows == SEQ:
                lane = lax.broadcasted_iota(jnp.int32, select.shape, 1)
                select = jnp.where(lane < TAIL, select, 0.0)
            if place + 1 < len(BLOCKS):
                total = jnp.sum(select, 1, keepdims=True)
                if carry is not None:
                    total = total + jnp.concatenate([carry, grown], 0)
                carry = total

    @pl.when(half == 0)
    def _():
        vt_ref[...] = v_ref[...].astype(F32).T.astype(B16)

    own = pl.ds(pl.multiple_of(half * HEAD_DIM, HEAD_DIM), HEAD_DIM)
    for place, (first, rows, keys) in enumerate(BLOCKS):
        logits = mm_nt(k_ref[:keys], queries[first : first + rows]) + bias_refs[place][...]
        highest = jnp.max(logits, 0, keepdims=True)
        raised = jnp.exp(logits - highest)
        total = jnp.sum(raised, 0, keepdims=True)
        mixed = mm(vt_ref[own, :keys], raised.astype(B16))
        ot_ref[own, first : first + rows] = mixed * (1.0 / total)
        lse_ref[0, :, first : first + rows] = highest + jnp.log(total)

    @pl.when(half == 1)
    def _():
        o_ref[...] = ot_ref[...].T.astype(B16)


def backward_kernel(
    q_ref, k_ref, v_ref, g_ref, lse_ref, b0, b1, b2, b3, b4,
    joined_ref,
    kt_ref, dqt_ref, dk_acc, dv_acc, p0, p1, p2, p3, p4, stage_ref, sems,
):
    bias_refs = (b0, b1, b2, b3, b4)
    pen_refs = (p0, p1, p2, p3, p4)
    head = HEADS - 1 - pl.program_id(0)
    half = head % 2
    queries = masked_half(q_ref[...].astype(F32) * SCALE, half)
    grads = masked_half(g_ref[...].astype(F32), half)
    own = pl.ds(pl.multiple_of(half * HEAD_DIM, HEAD_DIM), HEAD_DIM)

    @pl.when(head == HEADS - 1)
    def _():
        for pen in pen_refs:
            pen[...] = jnp.zeros_like(pen)

    @pl.when(half == 1)
    def _():
        kt_ref[...] = k_ref[...].astype(F32).T.astype(B16)
        dk_acc[...] = jnp.zeros_like(dk_acc)
        dv_acc[...] = jnp.zeros_like(dv_acc)

    def softmax_grad(place):
        first, rows, keys = BLOCKS[place]
        scores = mm_nt(k_ref[:keys], queries[first : first + rows])
        shares = jnp.exp(scores + bias_refs[place][...] - lse_ref[0, :, first : first + rows])
        back = mm_nt(v_ref[:keys], grads[first : first + rows])
        inner = jnp.sum(shares * back, 0, keepdims=True)
        dv_acc[:keys] += mm(shares.astype(B16), grads[first : first + rows])
        return scores, shares * (back - inner)

    def score_grad(place, grad):
        first, rows, keys = BLOCKS[place]
        grad = grad.astype(B16)
        dqt_ref[own, first : first + rows] = mm(kt_ref[own, :keys], grad)
        dk_acc[:keys] += mm(grad, queries[first : first + rows])

    @pl.when(head != 0)
    def _():
        for place in range(len(BLOCKS)):
            _, grad = softmax_grad(place)
            pen_refs[place][...] += grad
            score_grad(place, grad)

    @pl.when(head == 0)
    def _():
        carry = None
        for place in reversed(range(len(BLOCKS))):
            first, rows, keys = BLOCKS[place]
            scores, grad = softmax_grad(place)
            whole = pen_refs[place][...] + grad
            later = split_mm(whole, triangle(rows, True))
            total = jnp.sum(whole, 1, keepdims=True)
            if carry is not None:
                if first + rows == SEQ:
                    lane = lax.broadcasted_iota(jnp.int32, (keys, rows), 1)
                    later = later + jnp.where(lane < TAIL, carry[:keys], 0.0)
                else:
                    later = later + carry[:keys]
                total = total + carry[:keys]
            carry = total
            _, chosen = block_masks(place)
            grad = grad + jnp.where(chosen & (scores > 0.0), -SELECT_GAIN * later, 0.0)
            score_grad(place, grad)

    def copies(pair):
        return [
            pltpu.make_async_copy(
                stage_ref.at[part],
                joined_ref.at[:, pl.ds(pl.multiple_of(part * D + pair * PAIR, PAIR), PAIR)],
                sems.at[part],
            )
            for part in range(3)
        ]

    @pl.when((half == 0) & (head != HEADS - 2))
    def _():
        for copy in copies(head // 2 + 1):
            copy.wait()

    @pl.when(half == 0)
    def _():
        stage_ref[0] = (dqt_ref[...].T * SCALE).astype(B16)
        stage_ref[1] = dk_acc[...].astype(B16)
        stage_ref[2] = dv_acc[...].astype(B16)
        for copy in copies(head // 2):
            copy.start()

    @pl.when(head == 0)
    def _():
        for copy in copies(0):
            copy.wait()


def pair_spec(index):
    return pl.BlockSpec((ROWS, PAIR), index)


def whole_specs():
    return [pl.BlockSpec((keys, rows), lambda i: (0, 0)) for _, rows, keys in BLOCKS]


PAIRS = HEADS // 2


def attend_forward(joined):
    return pl.pallas_call(
        forward_kernel,
        grid=(HEADS,),
        in_specs=[
            pair_spec(lambda i: (0, i // 2)),
            pair_spec(lambda i: (0, PAIRS + i // 2)),
            pair_spec(lambda i: (0, 2 * PAIRS + i // 2)),
        ],
        out_specs=[
            pair_spec(lambda i: (0, i // 2)),
            pl.BlockSpec((1, 1, ROWS), lambda i: (i, 0, 0)),
            *whole_specs(),
        ],
        out_shape=[
            jax.ShapeDtypeStruct((ROWS, D), B16),
            jax.ShapeDtypeStruct((HEADS, 1, ROWS), F32),
            *(jax.ShapeDtypeStruct((keys, rows), F32) for _, rows, keys in BLOCKS),
        ],
        scratch_shapes=[pltpu.VMEM((PAIR, ROWS), B16), pltpu.VMEM((PAIR, ROWS), F32)],
        name="attend_forward",
    )(joined, joined, joined)


def attend_backward(joined, grad_mixed, lse, biases):
    last = PAIRS - 1
    return pl.pallas_call(
        backward_kernel,
        grid=(HEADS,),
        in_specs=[
            pair_spec(lambda i: (0, last - i // 2)),
            pair_spec(lambda i: (0, PAIRS + last - i // 2)),
            pair_spec(lambda i: (0, 2 * PAIRS + last - i // 2)),
            pair_spec(lambda i: (0, last - i // 2)),
            pl.BlockSpec((1, 1, ROWS), lambda i: (HEADS - 1 - i, 0, 0)),
            *whole_specs(),
        ],
        out_specs=pl.BlockSpec(memory_space=pl.ANY),
        out_shape=jax.ShapeDtypeStruct((ROWS, 3 * D), B16),
        scratch_shapes=[
            pltpu.VMEM((PAIR, ROWS), B16),
            pltpu.VMEM((PAIR, ROWS), F32),
            pltpu.VMEM((ROWS, PAIR), F32),
            pltpu.VMEM((ROWS, PAIR), F32),
            *(pltpu.VMEM((keys, rows), F32) for _, rows, keys in BLOCKS),
            pltpu.VMEM((3, ROWS, PAIR), B16),
            pltpu.SemaphoreType.DMA((3,)),
        ],
        name="attend_backward",
    )(joined, joined, joined, grad_mixed, lse, *biases)


EVERY = ("dp", "fsdp")
CORE = 2
PLANE = (0, 1, 4, 5)


def device_count():
    return lax.axis_size("dp") * lax.axis_size("fsdp")


def depth():
    return device_count() // 8


def place_of():
    number = lax.axis_index("dp")
    return number // 4, number // 2 % 2, number % 2, lax.axis_index("fsdp")


def swap(value, mask):
    return lax.ppermute(value, EVERY, [(i, i ^ mask) for i in range(device_count())])


def arrange(pieces, own):
    pieces = list(pieces)
    bit = 1
    while bit < len(pieces):
        odd = (own // bit) % 2 == 1
        pieces = [jnp.where(odd, pieces[k ^ bit], pieces[k]) for k in range(len(pieces))]
        bit *= 2
    return pieces


def gather_steps(shard, held):
    z, x, core, y = place_of()
    column = [shard] + [swap(shard, 8 * k) for k in range(1, depth())]
    *column, held = lax.optimization_barrier((*column, held))
    value = jnp.stack(arrange(column, z))
    plane = [value] + [swap(value, mask) for mask in PLANE[1:]]
    plane = arrange(plane, 2 * x + y)
    value = jnp.stack([jnp.stack(plane[:2], 1), jnp.stack(plane[2:], 1)], 1)
    value = jnp.stack(arrange([value, swap(value, CORE)], core), 2)
    return value.reshape(-1, shard.shape[1]), held


def take(value, index, axis):
    return lax.dynamic_index_in_dim(value, index, axis, keepdims=False)


def add_up(pieces):
    total = pieces[0].astype(F32)
    for piece in pieces[1:]:
        total = total + piece.astype(F32)
    return total


def scatter_steps(grad):
    return scatter_chips(scatter_core(grad))


def scatter_core(grad):
    core = place_of()[2]
    rows = grad.shape[0] // device_count()
    value = grad.reshape(depth(), 2, 2, 2, rows, grad.shape[1])
    other = swap(take(value, 1 - core, 2), CORE)
    return take(value, core, 2) + other


def scatter_chips(value):
    z, x, _, y = place_of()
    plane = [
        take(take(value, x ^ (mask // 4), 1), y ^ (mask % 2), 1) for mask in PLANE
    ]
    others = [swap(piece, mask) for piece, mask in zip(plane[1:], PLANE[1:])]
    value = add_up(plane[:1] + others).astype(B16)
    column = [take(value, z ^ k, 0) for k in range(depth())]
    others = [swap(column[k], 8 * k) for k in range(1, depth())]
    return add_up(column[:1] + others)


def pack_vectors(vectors, kind):
    rows = D // device_count()
    flat = jnp.concatenate([v.reshape(-1, v.shape[0] // vectors[0].shape[0] * rows) for v in vectors], 1)
    flat = flat.astype(kind).reshape(-1, 3, flat.shape[1] // 3)
    flat = jnp.pad(flat, ((0, 0), (0, rows - 3), (0, 128 - flat.shape[2])))
    return flat.reshape(-1, 128)


def unpack_vectors(columns, sizes):
    rows = D // device_count()
    width = sum(sizes) // 3
    flat = columns.reshape(-1, rows, 128)[:, :3, :width].reshape(-1, 3 * width)
    out, start = [], 0
    for size in sizes:
        out.append(flat[:, start : start + size].reshape(-1).astype(F32))
        start += size
    return out


def gelu_pair(upward):
    rate = (2.0 / jnp.pi) ** 0.5
    square = upward * upward
    bend = jnp.tanh(upward * (rate + (rate * 0.044715) * square))
    gate = 0.5 + 0.5 * bend
    slope = gate + upward * (1.0 - bend * bend) * (
        0.5 * rate + (1.5 * 0.044715 * rate) * square
    )
    return (upward * gate).astype(B16), slope.astype(B16)


def normalize_back(values, gain, grad):
    center = values - jnp.mean(values, -1, keepdims=True)
    rate = lax.rsqrt(jnp.mean(center * center, -1, keepdims=True) + EPS)
    unit = center * rate
    scaled = grad * gain
    inner = jnp.mean(scaled * unit, -1, keepdims=True)
    back = rate * (scaled - jnp.mean(scaled, -1, keepdims=True) - unit * inner)
    return back, jnp.sum(grad * unit, 0), jnp.sum(grad, 0)


def pick(first, second, when):
    return jnp.where(when, first, second)


def trade_rows(prompt, cont):
    place = lax.axis_index("fsdp")
    low = place == 0
    swap_pairs = [(0, 1), (1, 0)]
    mine = [pick(t[0], t[1], low).reshape(-1, D) for t in (prompt, cont)]
    away = [pick(t[1], t[0], low).reshape(-1, D) for t in (prompt, cont)]
    came = lax.ppermute(jnp.concatenate(away, 0), "fsdp", swap_pairs)
    half = mine[0].shape[0]
    parts = (came[:half], came[half:])
    return jnp.concatenate(
        [
            pick(mine[0], parts[0], low),
            pick(parts[0], mine[0], low),
            pick(mine[1], parts[1], low),
            pick(parts[1], mine[1], low),
        ],
        0,
    )


def return_rows(whole, kind):
    place = lax.axis_index("fsdp")
    low = place == 0
    half = PROMPT // 2
    parts = (
        (whole[:half], whole[PROMPT:SEQ]),
        (whole[half:PROMPT], whole[SEQ:]),
    )
    mine = [pick(parts[0][i], parts[1][i], low) for i in range(2)]
    away = [pick(parts[1][i], parts[0][i], low) for i in range(2)]
    came = lax.ppermute(jnp.concatenate(away, 0).astype(B16), "fsdp", [(0, 1), (1, 0)])
    came = (came[:half], came[half:])
    out = []
    for i in range(2):
        own, other = mine[i].astype(kind), came[i].astype(kind)
        out.append(jnp.stack([pick(own, other, low), pick(other, own, low)]))
    return out[0][:, None], out[1][:, None, None]


def whole_layer(*args):
    return whole_steps(*args)


def whole_steps(
    x_prompt, x_cont, dy_prompt, dy_cont,
    ln1_gain, ln1_bias, w_qkv, b_qv, w_out, b_out,
    ln2_gain, ln2_bias, w_up, b_up, w_down, b_down,
):
    devices = device_count()
    vectors = (ln1_gain, ln1_bias, b_qv, b_out, ln2_gain, ln2_bias, b_up, b_down)
    sizes = [v.shape[0] for v in vectors]
    chunks = w_down.shape[0] // w_qkv.shape[0]
    rows = w_qkv.shape[0]
    flat_x = trade_rows(x_prompt, x_cont).astype(F32)
    rest = jnp.concatenate(
        [w_out, *(w_up[:, i * D : (i + 1) * D] for i in range(chunks)), w_down], 0
    )
    full_first, rest = gather_steps(jnp.concatenate([w_qkv, pack_vectors(vectors, B16)], 1), rest)
    full_rest = lax.all_gather(rest, EVERY, axis=0)
    full_qkv = full_first[:, : 3 * D]
    (
        gain_one, shift_one, bias_qv, bias_out, gain_two, shift_two, bias_up, bias_down,
    ) = unpack_vectors(full_first[:, 3 * D :], sizes)
    hidden = w_up.shape[1]
    full_out = full_rest[:, :rows].reshape(D, D)
    full_up = jnp.concatenate(
        [full_rest[:, rows * i : rows * (i + 1)].reshape(D, D) for i in range(1, chunks + 1)], 1
    )
    full_down = full_rest[:, rows * (chunks + 1) :].reshape(hidden, D)

    normed_one = normalize(flat_x, gain_one, shift_one).astype(B16)
    bias_joined = jnp.concatenate([bias_qv[:D], jnp.zeros((D,), F32), bias_qv[D:]])
    joined = (
        jnp.dot(normed_one, full_qkv, preferred_element_type=F32) + bias_joined
    ).astype(B16)
    joined, dy_prompt, dy_cont = lax.optimization_barrier((joined, dy_prompt, dy_cont))
    grad_y = trade_rows(dy_prompt, dy_cont)
    mixed, lse, *biases = attend_forward(joined)
    residual = flat_x + (jnp.dot(mixed, full_out, preferred_element_type=F32) + bias_out)
    normed_two = normalize(residual, gain_two, shift_two).astype(B16)
    upward = jnp.dot(normed_two, full_up, preferred_element_type=F32) + bias_up
    active, slope = lax.optimization_barrier(gelu_pair(upward))

    def weight_grad(left, right):
        return jnp.einsum("rd,re->de", left, right, preferred_element_type=F32).astype(B16)

    def through(grad, weight):
        return jnp.einsum("re,de->rd", grad, weight, preferred_element_type=F32)

    def column_sum(values):
        return jnp.sum(values.astype(F32), 0)

    grad_upward = (through(grad_y, full_down) * slope.astype(F32)).astype(B16)
    grad_down = weight_grad(active, grad_y)
    grad_up = weight_grad(normed_two, grad_upward)
    packed_grads = jnp.concatenate(
        [
            *(grad_up[:, i * D : (i + 1) * D].reshape(devices, rows, D) for i in range(chunks)),
            grad_down.reshape(devices, -1, D),
        ],
        1,
    )
    packed_grads, active, grad_upward = lax.optimization_barrier(
        (packed_grads, active, grad_upward)
    )
    own_hidden = lax.psum_scatter(packed_grads, EVERY, scatter_dimension=0).astype(F32)
    grad_w_up = jnp.concatenate(
        [own_hidden[i * rows : (i + 1) * rows] for i in range(chunks)], 1
    )
    grad_w_down = own_hidden[chunks * rows :]
    output = residual + (jnp.dot(active, full_down, preferred_element_type=F32) + bias_down)
    y_prompt, y_cont = return_rows(output.astype(B16), B16)

    grad_b_down = column_sum(grad_y)
    grad_b_up = column_sum(grad_upward)
    grad_resid, grad_gain_two, grad_shift_two = normalize_back(
        residual, gain_two, through(grad_upward, full_up)
    )
    grad_resid = grad_y.astype(F32) + grad_resid
    grad_branch = grad_resid.astype(B16)
    grad_w_out = scatter_steps(weight_grad(mixed, grad_branch))
    grad_b_out = column_sum(grad_branch)
    grad_mixed = through(grad_branch, full_out).astype(B16)
    grad_joined = attend_backward(joined, grad_mixed, lse, biases)
    grad_b_qv = jnp.concatenate(
        [column_sum(grad_joined[:, :D]), column_sum(grad_joined[:, 2 * D :])]
    )
    grad_input, grad_gain_one, grad_shift_one = normalize_back(
        flat_x, gain_one, through(grad_joined, full_qkv)
    )
    grad_x = grad_resid + grad_input
    dx_prompt, dx_cont = return_rows(grad_x, F32)
    small = (
        grad_gain_one, grad_shift_one, grad_b_qv, grad_b_out,
        grad_gain_two, grad_shift_two, grad_b_up, grad_b_down,
    )
    small, grad_x, grad_joined = lax.optimization_barrier(
        (pack_vectors(small, B16), grad_x, grad_joined)
    )
    grad_qkv = weight_grad(normed_one, grad_joined)
    own_first = scatter_steps(jnp.concatenate([grad_qkv, small], 1))
    grad_w_qkv = own_first[:, : 3 * D]
    own_vectors = own_first[:, 3 * D :]
    pieces = unpack_vectors(own_vectors, sizes)
    return (
        y_prompt, y_cont, dx_prompt, dx_cont,
        pieces[0], pieces[1], grad_w_qkv, pieces[2], grad_w_out, pieces[3],
        pieces[4], pieces[5], grad_w_up, pieces[6], grad_w_down, pieces[7],
    )


def solution(mesh):
    sizes = dict(mesh.shape)
    whole = sizes["fsdp"] == MICRO == NCONT and sizes["dp"] & (sizes["dp"] - 1) == 0
    return jax.shard_map(
        whole_layer if whole else spread_layer,
        mesh=mesh,
        in_specs=(
            P(None, "dp", "fsdp", None),
            P(None, "dp", "fsdp", None, None),
            P(None, "dp", "fsdp", None),
            P(None, "dp", "fsdp", None, None),
            P(("dp", "fsdp")),
            P(("dp", "fsdp")),
            P(("dp", "fsdp"), None),
            P(("dp", "fsdp")),
            P(("dp", "fsdp"), None),
            P(("dp", "fsdp")),
            P(("dp", "fsdp")),
            P(("dp", "fsdp")),
            P(("dp", "fsdp"), None),
            P(("dp", "fsdp")),
            P(("dp", "fsdp"), None),
            P(("dp", "fsdp")),
        ),
        out_specs=(
            P(None, "dp", "fsdp", None),
            P(None, "dp", "fsdp", None, None),
            P(None, "dp", "fsdp", None),
            P(None, "dp", "fsdp", None, None),
            P(("dp", "fsdp")),
            P(("dp", "fsdp")),
            P(("dp", "fsdp"), None),
            P(("dp", "fsdp")),
            P(("dp", "fsdp"), None),
            P(("dp", "fsdp")),
            P(("dp", "fsdp")),
            P(("dp", "fsdp")),
            P(("dp", "fsdp"), None),
            P(("dp", "fsdp")),
            P(("dp", "fsdp"), None),
            P(("dp", "fsdp")),
        ),
        check_vma=False,
    )
```

```python
from functools import partial

import jax
import jax.numpy as jnp
from jax import lax
from jax.experimental import pallas as pl
from jax.experimental.pallas import tpu as pltpu
from jax.sharding import PartitionSpec as P


D = 768
HEADS = 12
HEAD_DIM = 64
PROMPT = 960
CONT = 64
MICRO = 2


EPS = 1e-05
NEG = -1e30


def normalize(values, gain, shift):
    center = values - jnp.mean(values, -1, keepdims=True)
    spread = jnp.mean(center * center, -1, keepdims=True)
    return center * lax.rsqrt(spread + EPS) * gain + shift


def later_sum(values):
    return jnp.flip(jnp.cumsum(jnp.flip(values, 1), 1), 1) - values


def attend_group(inputs_g, causal, score_scale):
    query_g, key_g, value_g, penalty_g = inputs_g
    rows_here = query_g.shape[0]
    heads_q = query_g.reshape(rows_here, HEADS, HEAD_DIM)
    heads_k = key_g.reshape(-1, HEADS, HEAD_DIM)
    heads_v = value_g.reshape(-1, HEADS, HEAD_DIM)
    scores = (
        jnp.einsum("rhd,khd->hrk", heads_q, heads_k, preferred_element_type=jnp.float32)
        * score_scale
    )
    logits = jnp.where(causal[None], scores - penalty_g[None], NEG)
    highest = jnp.max(logits, -1, keepdims=True)
    raised = jnp.exp(logits - highest)
    totals = jnp.sum(raised, -1, keepdims=True)
    weights_b = (raised / totals).astype(jnp.bfloat16)
    mixture = jnp.einsum("hrk,khd->rhd", weights_b, heads_v, preferred_element_type=jnp.float32)
    return (
        mixture.reshape(rows_here, -1).astype(jnp.bfloat16),
        (highest + jnp.log(totals))[..., 0],
    )


def attend_back(inputs_g, causal, score_scale):
    query_g, key_g, value_g, penalty_g, grad_mix, log_totals = inputs_g
    rows_here = query_g.shape[0]
    heads_q = query_g.reshape(rows_here, HEADS, HEAD_DIM)
    heads_k = key_g.reshape(-1, HEADS, HEAD_DIM)
    heads_v = value_g.reshape(-1, HEADS, HEAD_DIM)
    heads_g = grad_mix.reshape(rows_here, HEADS, HEAD_DIM)
    scores = (
        jnp.einsum("rhd,khd->hrk", heads_q, heads_k, preferred_element_type=jnp.float32)
        * score_scale
    )
    logits = jnp.where(causal[None], scores - penalty_g[None], NEG)
    softmax_w = jnp.exp(logits - log_totals[..., None])
    grad_soft = jnp.einsum("rhd,khd->hrk", heads_g, heads_v, preferred_element_type=jnp.float32)
    inner_sum = jnp.sum(softmax_w * grad_soft, -1, keepdims=True)
    grad_logit = softmax_w * (grad_soft - inner_sum)
    grad_value = jnp.einsum(
        "hrk,rhd->khd", softmax_w.astype(jnp.bfloat16), heads_g, preferred_element_type=jnp.float32
    )
    grad_penalty = -jnp.sum(grad_logit, 0)
    rest_b = grad_logit[1:].astype(jnp.bfloat16)
    grad_query = (
        jnp.einsum("hrk,khd->rhd", rest_b, heads_k[:, 1:], preferred_element_type=jnp.float32)
        * score_scale
    )
    grad_key = (
        jnp.einsum("hrk,rhd->khd", rest_b, heads_q[:, 1:], preferred_element_type=jnp.float32)
        * score_scale
    )
    return (
        grad_value.reshape(-1, D),
        grad_query.reshape(rows_here, -1),
        grad_key.reshape(grad_key.shape[0], -1),
        grad_logit[0],
        grad_penalty,
    )


def spread_layer(
    x_prompt,
    x_cont,
    dy_prompt,
    dy_cont,
    ln1_gain,
    ln1_bias,
    w_qkv,
    b_qv,
    w_out,
    b_out,
    ln2_gain,
    ln2_bias,
    w_up,
    b_up,
    w_down,
    b_down,
):
    shards = (
        ln1_gain,
        ln1_bias,
        w_qkv,
        b_qv,
        w_out,
        b_out,
        ln2_gain,
        ln2_bias,
        w_up,
        b_up,
        w_down,
        b_down,
    )
    groups_here = x_prompt.shape[1]
    prompt_rows = x_prompt.shape[2]
    fsdp_count = lax.axis_size("fsdp")
    fsdp_place = lax.axis_index("fsdp")
    key_count = PROMPT + CONT
    score_scale = HEAD_DIM ** (-0.5)
    select_gain = 4.0 / (PROMPT + CONT)
    query_pos = jnp.concatenate(
        [
            fsdp_place * prompt_rows + jnp.arange(prompt_rows, dtype=jnp.int32),
            PROMPT + jnp.arange(CONT, dtype=jnp.int32),
        ]
    )
    key_pos = jnp.arange(key_count, dtype=jnp.int32)
    causal = key_pos[None, :] <= query_pos[:, None]
    chosen = (key_pos[None, :] < query_pos[:, None]) & (key_pos[None, :] > 0)
    lower_mask = (jnp.arange(fsdp_count, dtype=jnp.int32) < fsdp_place).astype(jnp.float32)
    pad_zeros = jnp.zeros((groups_here, CONT), jnp.float32)
    forward_attend = partial(attend_group, causal=causal, score_scale=score_scale)
    backward_attend = partial(attend_back, causal=causal, score_scale=score_scale)
    totals = tuple(
        (
            jnp.zeros(
                (single.shape[0] * lax.axis_size(("dp", "fsdp")),) + single.shape[1:], jnp.float32
            )
            for single in shards
        )
    )
    outputs_yp, outputs_yc, outputs_dxp, outputs_dxc = ([], [], [], [])
    for batch_index in range(MICRO):
        gathered = (
            lax.all_gather(shards[0], ("dp", "fsdp"), axis=0, tiled=True),
            lax.all_gather(shards[1], ("dp", "fsdp"), axis=0, tiled=True),
            lax.all_gather(shards[2], ("dp", "fsdp"), axis=0, tiled=True),
            lax.all_gather(shards[3], ("dp", "fsdp"), axis=0, tiled=True),
            lax.all_gather(shards[4], ("dp", "fsdp"), axis=0, tiled=True),
            lax.all_gather(shards[5], ("dp", "fsdp"), axis=0, tiled=True),
            lax.all_gather(shards[6], ("dp", "fsdp"), axis=0, tiled=True),
            lax.all_gather(shards[7], ("dp", "fsdp"), axis=0, tiled=True),
            lax.all_gather(shards[8], ("dp", "fsdp"), axis=0, tiled=True),
            lax.all_gather(shards[9], ("dp", "fsdp"), axis=0, tiled=True),
            lax.all_gather(shards[10], ("dp", "fsdp"), axis=0, tiled=True),
            lax.all_gather(shards[11], ("dp", "fsdp"), axis=0, tiled=True),
        )
        inputs_x = jnp.concatenate([x_prompt[batch_index], x_cont[batch_index][:, 0]], 1).astype(
            jnp.float32
        )
        local_rows = inputs_x.shape[1]
        flat_x = inputs_x.reshape(-1, D)
        normed_one = normalize(
            flat_x, gathered[0].astype(jnp.float32), gathered[1].astype(jnp.float32)
        ).astype(jnp.bfloat16)
        joined = jnp.dot(normed_one, gathered[2], preferred_element_type=jnp.float32)
        bias_qv = gathered[3].astype(jnp.float32)
        queries = (
            (joined[:, :D] + bias_qv[:D]).astype(jnp.bfloat16).reshape(groups_here, local_rows, D)
        )
        keys_own = joined[:, D : 2 * D].astype(jnp.bfloat16).reshape(groups_here, local_rows, D)
        values_own = (
            (joined[:, 2 * D :] + bias_qv[D:])
            .astype(jnp.bfloat16)
            .reshape(groups_here, local_rows, D)
        )
        prompt_pair = jnp.concatenate([keys_own[:, :prompt_rows], values_own[:, :prompt_rows]], 2)
        whole_kv = lax.all_gather(prompt_pair, "fsdp", axis=1, tiled=True)
        keys_all = jnp.concatenate([whole_kv[..., :D], keys_own[:, prompt_rows:]], 1)
        values_all = jnp.concatenate([whole_kv[..., D:], values_own[:, prompt_rows:]], 1)
        score_zero = (
            jnp.einsum(
                "grd,gkd->grk",
                queries[..., :HEAD_DIM],
                keys_all[..., :HEAD_DIM],
                preferred_element_type=jnp.float32,
            )
            * score_scale
        )
        select = jnp.where(chosen[None], jnp.maximum(score_zero, 0.0), 0.0)
        own_part = jnp.sum(select[:, :prompt_rows, :PROMPT], 1)
        all_parts = lax.all_gather(own_part[None], "fsdp", axis=0, tiled=True)
        prefix = jnp.sum(all_parts * lower_mask[:, None, None], 0)
        whole_sum = jnp.sum(all_parts, 0)
        select_p = select[:, :prompt_rows]
        select_c = select[:, prompt_rows:]
        penalty = select_gain * jnp.concatenate(
            [
                jnp.concatenate([prefix, pad_zeros], 1)[:, None]
                + (jnp.cumsum(select_p, 1) - select_p),
                jnp.concatenate([whole_sum, pad_zeros], 1)[:, None]
                + (jnp.cumsum(select_c, 1) - select_c),
            ],
            1,
        )
        mixture, log_totals = lax.map(forward_attend, (queries, keys_all, values_all, penalty))
        mixed_flat = mixture.reshape(-1, D)
        residual = flat_x + (
            jnp.dot(mixed_flat, gathered[4], preferred_element_type=jnp.float32)
            + gathered[5].astype(jnp.float32)
        )
        normed_two = normalize(
            residual, gathered[6].astype(jnp.float32), gathered[7].astype(jnp.float32)
        ).astype(jnp.bfloat16)
        upward = jnp.dot(normed_two, gathered[8], preferred_element_type=jnp.float32) + gathered[
            9
        ].astype(jnp.float32)
        active, gelu_back = jax.vjp(partial(jax.nn.gelu, approximate=True), upward)
        active_b = active.astype(jnp.bfloat16)
        output = residual + (
            jnp.dot(active_b, gathered[10], preferred_element_type=jnp.float32)
            + gathered[11].astype(jnp.float32)
        )
        output_b = output.astype(jnp.bfloat16).reshape(groups_here, local_rows, D)
        outputs_yp.append(output_b[:, :prompt_rows])
        outputs_yc.append(output_b[:, prompt_rows:][:, None])
        back_set = (
            lax.all_gather(shards[0], ("dp", "fsdp"), axis=0, tiled=True),
            lax.all_gather(shards[1], ("dp", "fsdp"), axis=0, tiled=True),
            lax.all_gather(shards[2], ("dp", "fsdp"), axis=0, tiled=True),
            lax.all_gather(shards[3], ("dp", "fsdp"), axis=0, tiled=True),
            lax.all_gather(shards[4], ("dp", "fsdp"), axis=0, tiled=True),
            lax.all_gather(shards[5], ("dp", "fsdp"), axis=0, tiled=True),
            lax.all_gather(shards[6], ("dp", "fsdp"), axis=0, tiled=True),
            lax.all_gather(shards[7], ("dp", "fsdp"), axis=0, tiled=True),
            lax.all_gather(shards[8], ("dp", "fsdp"), axis=0, tiled=True),
            lax.all_gather(shards[9], ("dp", "fsdp"), axis=0, tiled=True),
            lax.all_gather(shards[10], ("dp", "fsdp"), axis=0, tiled=True),
            lax.all_gather(shards[11], ("dp", "fsdp"), axis=0, tiled=True),
        )
        grad_out_y = jnp.concatenate(
            [dy_prompt[batch_index], dy_cont[batch_index][:, 0]], 1
        ).reshape(-1, D)
        grad_down = jnp.einsum(
            "rf,rd->fd", active_b, grad_out_y, preferred_element_type=jnp.float32
        )
        grad_bdown = jnp.sum(grad_out_y.astype(jnp.float32), 0)
        grad_active = jnp.einsum(
            "rd,fd->rf", grad_out_y, back_set[10], preferred_element_type=jnp.float32
        )
        grad_upward = gelu_back(grad_active)[0].astype(jnp.bfloat16)
        grad_up = jnp.einsum(
            "rd,rf->df", normed_two, grad_upward, preferred_element_type=jnp.float32
        )
        grad_bup = jnp.sum(grad_upward.astype(jnp.float32), 0)
        grad_normed = jnp.einsum(
            "rf,df->rd", grad_upward, back_set[8], preferred_element_type=jnp.float32
        )
        _, norm_back = jax.vjp(
            normalize, residual, back_set[6].astype(jnp.float32), back_set[7].astype(jnp.float32)
        )
        grad_resid, grad_gain_two, grad_shift_two = norm_back(grad_normed)
        grad_resid = grad_out_y.astype(jnp.float32) + grad_resid
        grad_branch = grad_resid.astype(jnp.bfloat16)
        grad_wout = jnp.einsum(
            "rd,re->de", mixed_flat, grad_branch, preferred_element_type=jnp.float32
        )
        grad_bout = jnp.sum(grad_branch.astype(jnp.float32), 0)
        grad_mixed = jnp.einsum(
            "re,de->rd", grad_branch, back_set[4], preferred_element_type=jnp.float32
        )
        grad_mixed = grad_mixed.astype(jnp.bfloat16).reshape(groups_here, local_rows, D)
        back_values, back_queries, back_keys, back_zero, back_penalty = lax.map(
            backward_attend, (queries, keys_all, values_all, penalty, grad_mixed, log_totals)
        )
        prefix_grad = select_gain * jnp.sum(back_penalty[:, :prompt_rows, :PROMPT], 1)
        whole_grad = select_gain * jnp.sum(back_penalty[:, prompt_rows:, :PROMPT], 1)
        spread_back = prefix_grad[None] * lower_mask[:, None, None] + whole_grad[None]
        part_grad = lax.psum_scatter(spread_back, "fsdp", scatter_dimension=0, tiled=True)[0]
        select_back = jnp.concatenate(
            [
                select_gain * later_sum(back_penalty[:, :prompt_rows])
                + jnp.concatenate([part_grad, pad_zeros], 1)[:, None],
                select_gain * later_sum(back_penalty[:, prompt_rows:]),
            ],
            1,
        )
        grad_zero = (
            back_zero + jnp.where(chosen[None] & (score_zero > 0), select_back, 0.0)
        ).astype(jnp.bfloat16)
        query_zero = (
            jnp.einsum(
                "grk,gkd->grd",
                grad_zero,
                keys_all[..., :HEAD_DIM],
                preferred_element_type=jnp.float32,
            )
            * score_scale
        )
        key_zero = (
            jnp.einsum(
                "grk,grd->gkd",
                grad_zero,
                queries[..., :HEAD_DIM],
                preferred_element_type=jnp.float32,
            )
            * score_scale
        )
        grad_queries = jnp.concatenate([query_zero, back_queries], 2)
        grad_keys = jnp.concatenate([key_zero, back_keys], 2)
        prompt_back = jnp.concatenate([grad_keys[:, :PROMPT], back_values[:, :PROMPT]], 2)
        own_back = lax.psum_scatter(
            prompt_back.astype(jnp.bfloat16), "fsdp", scatter_dimension=1, tiled=True
        ).astype(jnp.float32)
        keys_back = jnp.concatenate([own_back[..., :D], grad_keys[:, PROMPT:]], 1)
        values_back = jnp.concatenate([own_back[..., D:], back_values[:, PROMPT:]], 1)
        grad_joined = (
            jnp.concatenate([grad_queries, keys_back, values_back], 2)
            .astype(jnp.bfloat16)
            .reshape(-1, 3 * D)
        )
        grad_wqkv = jnp.einsum(
            "rd,re->de", normed_one, grad_joined, preferred_element_type=jnp.float32
        )
        grad_bqv = jnp.concatenate(
            [
                jnp.sum(grad_joined[:, :D].astype(jnp.float32), 0),
                jnp.sum(grad_joined[:, 2 * D :].astype(jnp.float32), 0),
            ]
        )
        grad_normed_one = jnp.einsum(
            "re,de->rd", grad_joined, back_set[2], preferred_element_type=jnp.float32
        )
        _, norm_back_one = jax.vjp(
            normalize, flat_x, back_set[0].astype(jnp.float32), back_set[1].astype(jnp.float32)
        )
        grad_input, grad_gain_one, grad_shift_one = norm_back_one(grad_normed_one)
        grad_input = (grad_resid + grad_input).reshape(groups_here, local_rows, D)
        outputs_dxp.append(grad_input[:, :prompt_rows])
        outputs_dxc.append(grad_input[:, prompt_rows:][:, None])
        micro_grads = (
            grad_gain_one,
            grad_shift_one,
            grad_wqkv,
            grad_bqv,
            grad_wout,
            grad_bout,
            grad_gain_two,
            grad_shift_two,
            grad_up,
            grad_bup,
            grad_down,
            grad_bdown,
        )
        totals = tuple((first + second for first, second in zip(totals, micro_grads)))
    results = (
        lax.psum_scatter(totals[0], ("dp", "fsdp"), scatter_dimension=0, tiled=True),
        lax.psum_scatter(totals[1], ("dp", "fsdp"), scatter_dimension=0, tiled=True),
        lax.psum_scatter(totals[2], ("dp", "fsdp"), scatter_dimension=0, tiled=True),
        lax.psum_scatter(totals[3], ("dp", "fsdp"), scatter_dimension=0, tiled=True),
        lax.psum_scatter(totals[4], ("dp", "fsdp"), scatter_dimension=0, tiled=True),
        lax.psum_scatter(totals[5], ("dp", "fsdp"), scatter_dimension=0, tiled=True),
        lax.psum_scatter(totals[6], ("dp", "fsdp"), scatter_dimension=0, tiled=True),
        lax.psum_scatter(totals[7], ("dp", "fsdp"), scatter_dimension=0, tiled=True),
        lax.psum_scatter(totals[8], ("dp", "fsdp"), scatter_dimension=0, tiled=True),
        lax.psum_scatter(totals[9], ("dp", "fsdp"), scatter_dimension=0, tiled=True),
        lax.psum_scatter(totals[10], ("dp", "fsdp"), scatter_dimension=0, tiled=True),
        lax.psum_scatter(totals[11], ("dp", "fsdp"), scatter_dimension=0, tiled=True),
    )
    return (
        jnp.stack(outputs_yp),
        jnp.stack(outputs_yc),
        jnp.stack(outputs_dxp),
        jnp.stack(outputs_dxc),
        results[0],
        results[1],
        results[2],
        results[3],
        results[4],
        results[5],
        results[6],
        results[7],
        results[8],
        results[9],
        results[10],
        results[11],
    )


NCONT = 2
ROWS = PROMPT + NCONT * CONT
SEQ = PROMPT + CONT
SCALE = HEAD_DIM ** (-0.5)
SELECT_GAIN = 4.0 / SEQ
PAIR = 2 * HEAD_DIM
BLOCKS = ((0, 256, 256), (256, 256, 512), (512, 256, 768), (768, 256, 1024), (1024, 64, ROWS))
TAIL = PROMPT - 768
F32 = jnp.float32
B16 = jnp.bfloat16


def mm(a, b):
    return lax.dot_general(a, b, (((1,), (0,)), ((), ())), preferred_element_type=F32)


def mm_nt(a, b):
    return lax.dot_general(a, b, (((1,), (1,)), ((), ())), preferred_element_type=F32)


def masked_half(values, half):
    lane = lax.broadcasted_iota(jnp.int32, values.shape, 1)
    return jnp.where(lane // HEAD_DIM == half, values, 0.0).astype(B16)


def block_masks(place, low=0, high=None):
    first, rows, keys = BLOCKS[place]
    shape = ((high or keys) - low, rows)
    key_id = low + lax.broadcasted_iota(jnp.int32, shape, 0)
    row_id = first + lax.broadcasted_iota(jnp.int32, shape, 1)
    visible = key_id <= row_id
    if first >= SEQ:
        visible = visible & ((key_id < PROMPT) | (key_id >= SEQ))
    chosen = visible & (key_id < row_id) & (key_id > 0)
    return visible, chosen


def split_mm(values, ones):
    high = values.astype(B16)
    low = (values - high.astype(F32)).astype(B16)
    return mm(high, ones) + mm(low, ones)


def triangle(rows, later):
    a = lax.broadcasted_iota(jnp.int32, (rows, rows), 0)
    b = lax.broadcasted_iota(jnp.int32, (rows, rows), 1)
    return jnp.where((a > b) if later else (a < b), 1.0, 0.0).astype(B16)


def chunks_of(keys):
    return [(low, min(low + 256, keys)) for low in range(0, keys, 256)]


def forward_kernel(q_ref, k_ref, v_ref, o_ref, lse_ref, b0, b1, b2, b3, b4, vt_ref, ot_ref, logit_ref, share_ref):
    bias_refs = (b0, b1, b2, b3, b4)
    head = pl.program_id(0)
    half = head % 2
    queries = masked_half(q_ref[...].astype(F32) * SCALE, half)

    @pl.when(head == 0)
    def _():
        carry = None
        for place, (first, rows, keys) in enumerate(BLOCKS):
            scores = mm_nt(k_ref[:keys], queries[first : first + rows])
            visible, chosen = block_masks(place)
            select = jnp.where(chosen, jnp.maximum(scores, 0.0), 0.0)
            penalty = split_mm(select, triangle(rows, False))
            if carry is not None:
                grown = jnp.zeros((keys - carry.shape[0], 1), F32)
                penalty = penalty + jnp.concatenate([carry, grown], 0)
            bias_refs[place][...] = jnp.where(visible, -SELECT_GAIN * penalty, NEG)
            if first + rows == SEQ:
                lane = lax.broadcasted_iota(jnp.int32, select.shape, 1)
                select = jnp.where(lane < TAIL, select, 0.0)
            if place + 1 < len(BLOCKS):
                total = jnp.sum(select, 1, keepdims=True)
                if carry is not None:
                    total = total + jnp.concatenate([carry, grown], 0)
                carry = total

    @pl.when(half == 0)
    def _():
        vt_ref[...] = v_ref[...].astype(F32).T.astype(B16)

    own = pl.ds(pl.multiple_of(half * HEAD_DIM, HEAD_DIM), HEAD_DIM)
    for place, (first, rows, keys) in enumerate(BLOCKS):
        asked = queries[first : first + rows]
        highest = None
        for low, high in chunks_of(keys):
            logits = mm_nt(k_ref[low:high], asked) + bias_refs[place][low:high]
            logit_ref[low:high, first : first + rows] = logits
            top = jnp.max(logits, 0, keepdims=True)
            highest = top if highest is None else jnp.maximum(highest, top)
        total = 0.0
        for low, high in chunks_of(keys):
            raised = jnp.exp(logit_ref[low:high, first : first + rows] - highest)
            total = total + jnp.sum(raised, 0, keepdims=True)
            share_ref[low:high, first : first + rows] = raised.astype(B16)
        mixed = mm(vt_ref[own, :keys], share_ref[:keys, first : first + rows])
        ot_ref[own, first : first + rows] = mixed * (1.0 / total)
        lse_ref[0, :, first : first + rows] = highest + jnp.log(total)

    @pl.when(half == 1)
    def _():
        o_ref[...] = ot_ref[...].T.astype(B16)


def backward_kernel(
    q_ref, k_ref, v_ref, g_ref, o_ref, lse_ref, b0, b1, b2, b3, b4,
    joined_ref,
    kt_ref, dqt_ref, dk_acc, dv_acc, p0, p1, p2, p3, p4, stage_ref, share_ref, grad_ref, inner_ref, sems,
):
    bias_refs = (b0, b1, b2, b3, b4)
    pen_refs = (p0, p1, p2, p3, p4)
    head = HEADS - 1 - pl.program_id(0)
    half = head % 2
    queries = masked_half(q_ref[...].astype(F32) * SCALE, half)
    grads = masked_half(g_ref[...].astype(F32), half)
    own = pl.ds(pl.multiple_of(half * HEAD_DIM, HEAD_DIM), HEAD_DIM)

    @pl.when(head == HEADS - 1)
    def _():
        for pen in pen_refs:
            pen[...] = jnp.zeros_like(pen)

    @pl.when(half == 1)
    def _():
        kt_ref[...] = k_ref[...].astype(F32).T.astype(B16)
        both = (o_ref[...].astype(F32) * g_ref[...].astype(F32)).T
        inner_ref[0] = jnp.sum(both[:HEAD_DIM], 0, keepdims=True)
        inner_ref[1] = jnp.sum(both[HEAD_DIM:], 0, keepdims=True)
        dk_acc[...] = jnp.zeros_like(dk_acc)
        dv_acc[...] = jnp.zeros_like(dv_acc)

    def tile(place, low, high):
        first, rows, _ = BLOCKS[place]
        scores = mm_nt(k_ref[low:high], queries[first : first + rows])
        shares = jnp.exp(
            scores + bias_refs[place][low:high] - lse_ref[0, :, first : first + rows]
        )
        back = mm_nt(v_ref[low:high], grads[first : first + rows])
        share_ref[low:high, first : first + rows] = shares.astype(B16)
        return scores, shares * (back - inner_ref[half, :, first : first + rows])

    def finish(low, high):
        dv_acc[low:high] += mm(share_ref[low:high, low:], grads[low:])
        dk_acc[low:high] += mm(grad_ref[low:high, low:], queries[low:])

    def finish_queries(place):
        first, rows, keys = BLOCKS[place]
        dqt_ref[own, first : first + rows] = mm(
            kt_ref[own, :keys], grad_ref[:keys, first : first + rows]
        )

    @pl.when(head != 0)
    def _():
        for low, high in chunks_of(ROWS):
            for place, (first, rows, keys) in enumerate(BLOCKS):
                if low < keys:
                    _, grad = tile(place, low, high)
                    pen_refs[place][low:high] += grad
                    grad_ref[low:high, first : first + rows] = grad.astype(B16)
            finish(low, high)
            finish_queries(low // 256)

    @pl.when(head == 0)
    def _():
        for low, high in chunks_of(ROWS):
            carry = None
            for place in reversed(range(len(BLOCKS))):
                first, rows, keys = BLOCKS[place]
                if low >= keys:
                    continue
                scores, grad = tile(place, low, high)
                whole = pen_refs[place][low:high] + grad
                later = split_mm(whole, triangle(rows, True))
                total = jnp.sum(whole, 1, keepdims=True)
                if carry is not None:
                    if first + rows == SEQ:
                        lane = lax.broadcasted_iota(jnp.int32, later.shape, 1)
                        later = later + jnp.where(lane < TAIL, carry, 0.0)
                    else:
                        later = later + carry
                    total = total + carry
                carry = total
                chosen = block_masks(place, low, high)[1]
                grad = grad + jnp.where(chosen & (scores > 0.0), -SELECT_GAIN * later, 0.0)
                grad_ref[low:high, first : first + rows] = grad.astype(B16)
            finish(low, high)
            finish_queries(low // 256)

    def copies(pair):
        return [
            pltpu.make_async_copy(
                stage_ref.at[part],
                joined_ref.at[:, pl.ds(pl.multiple_of(part * D + pair * PAIR, PAIR), PAIR)],
                sems.at[part],
            )
            for part in range(3)
        ]

    @pl.when((half == 0) & (head != HEADS - 2))
    def _():
        for copy in copies(head // 2 + 1):
            copy.wait()

    @pl.when(half == 0)
    def _():
        stage_ref[0] = (dqt_ref[...].T * SCALE).astype(B16)
        stage_ref[1] = dk_acc[...].astype(B16)
        stage_ref[2] = dv_acc[...].astype(B16)
        for copy in copies(head // 2):
            copy.start()

    @pl.when(head == 0)
    def _():
        for copy in copies(0):
            copy.wait()


def pair_spec(index):
    return pl.BlockSpec((ROWS, PAIR), index)


def whole_specs():
    return [pl.BlockSpec((keys, rows), lambda i: (0, 0)) for _, rows, keys in BLOCKS]


PAIRS = HEADS // 2


def attend_forward(joined):
    return pl.pallas_call(
        forward_kernel,
        grid=(HEADS,),
        in_specs=[
            pair_spec(lambda i: (0, i // 2)),
            pair_spec(lambda i: (0, PAIRS + i // 2)),
            pair_spec(lambda i: (0, 2 * PAIRS + i // 2)),
        ],
        out_specs=[
            pair_spec(lambda i: (0, i // 2)),
            pl.BlockSpec((1, 1, ROWS), lambda i: (i, 0, 0)),
            *whole_specs(),
        ],
        out_shape=[
            jax.ShapeDtypeStruct((ROWS, D), B16),
            jax.ShapeDtypeStruct((HEADS, 1, ROWS), F32),
            *(jax.ShapeDtypeStruct((keys, rows), F32) for _, rows, keys in BLOCKS),
        ],
        scratch_shapes=[
            pltpu.VMEM((PAIR, ROWS), B16),
            pltpu.VMEM((PAIR, ROWS), F32),
            pltpu.VMEM((ROWS, ROWS), F32),
            pltpu.VMEM((ROWS, ROWS), B16),
        ],
        name="attend_forward",
    )(joined, joined, joined)


def attend_backward(joined, grad_mixed, mixed, lse, biases):
    last = PAIRS - 1
    return pl.pallas_call(
        backward_kernel,
        grid=(HEADS,),
        in_specs=[
            pair_spec(lambda i: (0, last - i // 2)),
            pair_spec(lambda i: (0, PAIRS + last - i // 2)),
            pair_spec(lambda i: (0, 2 * PAIRS + last - i // 2)),
            pair_spec(lambda i: (0, last - i // 2)),
            pair_spec(lambda i: (0, last - i // 2)),
            pl.BlockSpec((1, 1, ROWS), lambda i: (HEADS - 1 - i, 0, 0)),
            *whole_specs(),
        ],
        out_specs=pl.BlockSpec(memory_space=pl.ANY),
        out_shape=jax.ShapeDtypeStruct((ROWS, 3 * D), B16),
        scratch_shapes=[
            pltpu.VMEM((PAIR, ROWS), B16),
            pltpu.VMEM((PAIR, ROWS), F32),
            pltpu.VMEM((ROWS, PAIR), F32),
            pltpu.VMEM((ROWS, PAIR), F32),
            *(pltpu.VMEM((keys, rows), F32) for _, rows, keys in BLOCKS),
            pltpu.VMEM((3, ROWS, PAIR), B16),
            pltpu.VMEM((ROWS, ROWS), B16),
            pltpu.VMEM((ROWS, ROWS), B16),
            pltpu.VMEM((2, 1, ROWS), F32),
            pltpu.SemaphoreType.DMA((3,)),
        ],
        name="attend_backward",
    )(joined, joined, joined, grad_mixed, mixed, lse, *biases)


EVERY = ("dp", "fsdp")
CORE = 2
PLANE = (0, 1, 4, 5)


def device_count():
    return lax.axis_size("dp") * lax.axis_size("fsdp")


def depth():
    return device_count() // 8


def place_of():
    number = lax.axis_index("dp")
    return number // 4, number // 2 % 2, number % 2, lax.axis_index("fsdp")


def swap(value, mask):
    return lax.ppermute(value, EVERY, [(i, i ^ mask) for i in range(device_count())])


def arrange(pieces, own):
    pieces = list(pieces)
    bit = 1
    while bit < len(pieces):
        odd = (own // bit) % 2 == 1
        pieces = [jnp.where(odd, pieces[k ^ bit], pieces[k]) for k in range(len(pieces))]
        bit *= 2
    return pieces


def gather_steps(shard, held):
    z, x, core, y = place_of()
    column = [shard] + [swap(shard, 8 * k) for k in range(1, depth())]
    *column, held = lax.optimization_barrier((*column, held))
    value = jnp.stack(arrange(column, z))
    plane = [value] + [swap(value, mask) for mask in PLANE[1:]]
    plane = arrange(plane, 2 * x + y)
    value = jnp.stack([jnp.stack(plane[:2], 1), jnp.stack(plane[2:], 1)], 1)
    value = jnp.stack(arrange([value, swap(value, CORE)], core), 2)
    return value.reshape(-1, shard.shape[1]), held


def take(value, index, axis):
    return lax.dynamic_index_in_dim(value, index, axis, keepdims=False)


def add_up(pieces):
    total = pieces[0].astype(F32)
    for piece in pieces[1:]:
        total = total + piece.astype(F32)
    return total


def scatter_core(grad):
    core = place_of()[2]
    rows = grad.shape[0] // device_count()
    value = grad.reshape(depth(), 2, 2, 2, rows, grad.shape[1])
    other = swap(take(value, 1 - core, 2), CORE)
    return take(value, core, 2) + other


def scatter_plane(value):
    _, x, _, y = place_of()
    plane = [
        take(take(value, x ^ (mask // 4), 1), y ^ (mask % 2), 1) for mask in PLANE
    ]
    others = [swap(piece, mask) for piece, mask in zip(plane[1:], PLANE[1:])]
    return plane[:1] + others


def scatter_column(plane):
    z = place_of()[0]
    value = add_up(plane).astype(B16)
    column = [take(value, z ^ k, 0) for k in range(depth())]
    others = [swap(column[k], 8 * k) for k in range(1, depth())]
    return add_up(column[:1] + others)


def pack_vectors(vectors):
    rows = D // device_count()
    padded = [jnp.pad(v, (0, 128 - v.shape[0]))[None] for v in vectors]
    return jnp.pad(jnp.concatenate(padded, 0), ((0, rows - len(vectors)), (0, 0)))


def unpack_vectors(columns, sizes):
    rows = columns.reshape(-1, D // device_count(), 128)
    return [rows[:, i, :size].reshape(-1).astype(F32) for i, size in enumerate(sizes)]


def pack_kernel(*refs):
    out_ref = refs[-1]
    devices = out_ref.shape[0]
    out_ref[...] = jnp.zeros_like(out_ref)
    for i, ref in enumerate(refs[:-1]):
        count = ref.shape[1]
        piece = count // devices
        values = ref[...]
        for j in range(devices):
            out_ref[j, i : i + 1, :piece] = values[:, j * piece : (j + 1) * piece]


def pack_grads(vectors):
    devices = device_count()
    return pl.pallas_call(
        pack_kernel,
        out_shape=jax.ShapeDtypeStruct((devices, D // devices, 128), F32),
        name="pack_grads",
    )(*(v.astype(F32)[None] for v in vectors))


def gelu_pair(upward):
    rate = (2.0 / jnp.pi) ** 0.5
    square = upward * upward
    bend = jnp.tanh(upward * (rate + (rate * 0.044715) * square))
    gate = 0.5 + 0.5 * bend
    slope = gate + upward * (1.0 - bend * bend) * (
        0.5 * rate + (1.5 * 0.044715 * rate) * square
    )
    return (upward * gate).astype(B16), slope.astype(B16)


def normalize_back(values, gain, grad):
    center = values - jnp.mean(values, -1, keepdims=True)
    rate = lax.rsqrt(jnp.mean(center * center, -1, keepdims=True) + EPS)
    unit = center * rate
    scaled = grad * gain
    inner = jnp.mean(scaled * unit, -1, keepdims=True)
    back = rate * (scaled - jnp.mean(scaled, -1, keepdims=True) - unit * inner)
    return back, jnp.sum(grad * unit, 0), jnp.sum(grad, 0)


def pick(first, second, when):
    return jnp.where(when, first, second)


def trade_rows(prompt, cont):
    place = lax.axis_index("fsdp")
    low = place == 0
    swap_pairs = [(0, 1), (1, 0)]
    mine = [pick(t[0], t[1], low).reshape(-1, D) for t in (prompt, cont)]
    away = [pick(t[1], t[0], low).reshape(-1, D) for t in (prompt, cont)]
    came = lax.ppermute(jnp.concatenate(away, 0), "fsdp", swap_pairs)
    half = mine[0].shape[0]
    parts = (came[:half], came[half:])
    return jnp.concatenate(
        [
            pick(mine[0], parts[0], low),
            pick(parts[0], mine[0], low),
            pick(mine[1], parts[1], low),
            pick(parts[1], mine[1], low),
        ],
        0,
    )


def trade_back(whole):
    place = lax.axis_index("fsdp")
    low = place == 0
    half = PROMPT // 2
    parts = (
        (whole[:half], whole[PROMPT:SEQ]),
        (whole[half:PROMPT], whole[SEQ:]),
    )
    mine = [pick(parts[0][i], parts[1][i], low) for i in range(2)]
    away = [pick(parts[1][i], parts[0][i], low) for i in range(2)]
    came = lax.ppermute(jnp.concatenate(away, 0).astype(B16), "fsdp", [(0, 1), (1, 0)])
    return mine, came


def join_rows(mine, came, kind):
    low = lax.axis_index("fsdp") == 0
    came = (came[: PROMPT // 2], came[PROMPT // 2 :])
    out = []
    for i in range(2):
        own, other = mine[i].astype(kind), came[i].astype(kind)
        out.append(jnp.stack([pick(own, other, low), pick(other, own, low)]))
    return out[0][:, None], out[1][:, None, None]


def whole_layer(*args):
    return whole_steps(*args)


def whole_steps(
    x_prompt, x_cont, dy_prompt, dy_cont,
    ln1_gain, ln1_bias, w_qkv, b_qv, w_out, b_out,
    ln2_gain, ln2_bias, w_up, b_up, w_down, b_down,
):
    devices = device_count()
    vectors = (ln1_gain, ln1_bias, b_qv, b_out, ln2_gain, ln2_bias, b_up, b_down)
    sizes = [v.shape[0] for v in vectors]
    chunks = w_down.shape[0] // w_qkv.shape[0]
    rows = w_qkv.shape[0]
    flat_x = trade_rows(x_prompt, x_cont).astype(F32)
    rest = jnp.concatenate(
        [w_out, *(w_up[:, i * D : (i + 1) * D] for i in range(chunks)), w_down], 0
    )
    full_first, rest = gather_steps(
        jnp.concatenate([w_qkv, pack_vectors(vectors)], 1), rest
    )
    full_rest = lax.all_gather(rest, EVERY, axis=0)
    full_qkv = full_first[:, : 3 * D]
    (
        gain_one, shift_one, bias_qv, bias_out, gain_two, shift_two, bias_up, bias_down,
    ) = unpack_vectors(full_first[:, 3 * D :], sizes)
    hidden = w_up.shape[1]
    full_out = full_rest[:, :rows].reshape(D, D)
    full_up = jnp.concatenate(
        [full_rest[:, rows * i : rows * (i + 1)].reshape(D, D) for i in range(1, chunks + 1)], 1
    )
    full_down = full_rest[:, rows * (chunks + 1) :].reshape(hidden, D)

    normed_one = normalize(flat_x, gain_one, shift_one).astype(B16)
    bias_joined = jnp.concatenate([bias_qv[:D], jnp.zeros((D,), F32), bias_qv[D:]])
    joined = (
        jnp.dot(normed_one, full_qkv, preferred_element_type=F32) + bias_joined
    ).astype(B16)
    joined, dy_prompt, dy_cont = lax.optimization_barrier((joined, dy_prompt, dy_cont))
    grad_y = trade_rows(dy_prompt, dy_cont)
    mixed, lse, *biases = attend_forward(joined)
    residual = flat_x + (jnp.dot(mixed, full_out, preferred_element_type=F32) + bias_out)
    normed_two = normalize(residual, gain_two, shift_two).astype(B16)
    upward = jnp.dot(normed_two, full_up, preferred_element_type=F32) + bias_up
    active, slope = lax.optimization_barrier(gelu_pair(upward))

    def weight_grad(left, right):
        return jnp.einsum("rd,re->de", left, right, preferred_element_type=F32).astype(B16)

    def through(grad, weight):
        return jnp.einsum("re,de->rd", grad, weight, preferred_element_type=F32)

    def column_sum(values):
        return jnp.sum(values.astype(F32), 0)

    grad_upward = (through(grad_y, full_down) * slope.astype(F32)).astype(B16)
    grad_down = weight_grad(active, grad_y)
    grad_up = weight_grad(normed_two, grad_upward)
    packed_grads = jnp.concatenate(
        [
            *(grad_up[:, i * D : (i + 1) * D].reshape(devices, rows, D) for i in range(chunks)),
            grad_down.reshape(devices, -1, D),
        ],
        1,
    )
    packed_grads, active, grad_upward = lax.optimization_barrier(
        (packed_grads, active, grad_upward)
    )
    own_hidden = lax.psum_scatter(packed_grads, EVERY, scatter_dimension=0).astype(F32)
    grad_w_up = jnp.concatenate(
        [own_hidden[i * rows : (i + 1) * rows] for i in range(chunks)], 1
    )
    grad_w_down = own_hidden[chunks * rows :]
    output = residual + (jnp.dot(active, full_down, preferred_element_type=F32) + bias_down)
    came_y = trade_back(output.astype(B16))

    grad_b_down = column_sum(grad_y)
    grad_b_up = column_sum(grad_upward)
    grad_resid, grad_gain_two, grad_shift_two = normalize_back(
        residual, gain_two, through(grad_upward, full_up)
    )
    grad_resid = grad_y.astype(F32) + grad_resid
    grad_branch = grad_resid.astype(B16)
    out_plane = scatter_plane(scatter_core(weight_grad(mixed, grad_branch)))
    grad_b_out = column_sum(grad_branch)
    grad_mixed = through(grad_branch, full_out).astype(B16)
    grad_joined = attend_backward(joined, grad_mixed, mixed, lse, biases)
    grad_b_qv = jnp.concatenate(
        [column_sum(grad_joined[:, :D]), column_sum(grad_joined[:, 2 * D :])]
    )
    grad_input, grad_gain_one, grad_shift_one = normalize_back(
        flat_x, gain_one, through(grad_joined, full_qkv)
    )
    grad_x = grad_resid + grad_input
    came_x = trade_back(grad_x)
    small = (
        grad_gain_one, grad_shift_one, grad_b_qv, grad_b_out,
        grad_gain_two, grad_shift_two, grad_b_up, grad_b_down,
    )
    small, grad_x, grad_joined = lax.optimization_barrier(
        (pack_grads(small), grad_x, grad_joined)
    )
    grad_qkv = weight_grad(normed_one, grad_joined)
    first = scatter_core(
        jnp.concatenate([grad_qkv, small.reshape(D, 128).astype(B16)], 1)
    )
    first, came_y, out_plane = lax.optimization_barrier((first, came_y, out_plane))
    plane = scatter_plane(first)
    plane, came_x = lax.optimization_barrier((plane, came_x))
    own_first = scatter_column(plane)
    dx_prompt, dx_cont = join_rows(*came_x, F32)
    grad_w_out = scatter_column(out_plane)
    y_prompt, y_cont = join_rows(*came_y, B16)
    grad_w_qkv = own_first[:, : 3 * D]
    own_vectors = own_first[:, 3 * D :]
    pieces = [own_vectors[i, :size] for i, size in enumerate(sizes)]
    return (
        y_prompt, y_cont, dx_prompt, dx_cont,
        pieces[0], pieces[1], grad_w_qkv, pieces[2], grad_w_out, pieces[3],
        pieces[4], pieces[5], grad_w_up, pieces[6], grad_w_down, pieces[7],
    )


def solution(mesh):
    sizes = dict(mesh.shape)
    whole = sizes["fsdp"] == MICRO == NCONT and sizes["dp"] & (sizes["dp"] - 1) == 0
    return jax.shard_map(
        whole_layer if whole else spread_layer,
        mesh=mesh,
        in_specs=(
            P(None, "dp", "fsdp", None),
            P(None, "dp", "fsdp", None, None),
            P(None, "dp", "fsdp", None),
            P(None, "dp", "fsdp", None, None),
            P(("dp", "fsdp")),
            P(("dp", "fsdp")),
            P(("dp", "fsdp"), None),
            P(("dp", "fsdp")),
            P(("dp", "fsdp"), None),
            P(("dp", "fsdp")),
            P(("dp", "fsdp")),
            P(("dp", "fsdp")),
            P(("dp", "fsdp"), None),
            P(("dp", "fsdp")),
            P(("dp", "fsdp"), None),
            P(("dp", "fsdp")),
        ),
        out_specs=(
            P(None, "dp", "fsdp", None),
            P(None, "dp", "fsdp", None, None),
            P(None, "dp", "fsdp", None),
            P(None, "dp", "fsdp", None, None),
            P(("dp", "fsdp")),
            P(("dp", "fsdp")),
            P(("dp", "fsdp"), None),
            P(("dp", "fsdp")),
            P(("dp", "fsdp"), None),
            P(("dp", "fsdp")),
            P(("dp", "fsdp")),
            P(("dp", "fsdp")),
            P(("dp", "fsdp"), None),
            P(("dp", "fsdp")),
            P(("dp", "fsdp"), None),
            P(("dp", "fsdp")),
        ),
        check_vma=False,
    )
```

```python
from functools import partial

import jax
import jax.numpy as jnp
from jax import lax
from jax.experimental import pallas as pl
from jax.experimental.pallas import tpu as pltpu
from jax.sharding import PartitionSpec as P


D = 768
HEADS = 12
HEAD_DIM = 64
PROMPT = 960
CONT = 64
MICRO = 2


EPS = 1e-05
NEG = -1e30


def normalize(values, gain, shift):
    center = values - jnp.mean(values, -1, keepdims=True)
    spread = jnp.mean(center * center, -1, keepdims=True)
    return center * lax.rsqrt(spread + EPS) * gain + shift


def later_sum(values):
    return jnp.flip(jnp.cumsum(jnp.flip(values, 1), 1), 1) - values


def attend_group(inputs_g, causal, score_scale):
    query_g, key_g, value_g, penalty_g = inputs_g
    rows_here = query_g.shape[0]
    heads_q = query_g.reshape(rows_here, HEADS, HEAD_DIM)
    heads_k = key_g.reshape(-1, HEADS, HEAD_DIM)
    heads_v = value_g.reshape(-1, HEADS, HEAD_DIM)
    scores = (
        jnp.einsum("rhd,khd->hrk", heads_q, heads_k, preferred_element_type=jnp.float32)
        * score_scale
    )
    logits = jnp.where(causal[None], scores - penalty_g[None], NEG)
    highest = jnp.max(logits, -1, keepdims=True)
    raised = jnp.exp(logits - highest)
    totals = jnp.sum(raised, -1, keepdims=True)
    weights_b = (raised / totals).astype(jnp.bfloat16)
    mixture = jnp.einsum("hrk,khd->rhd", weights_b, heads_v, preferred_element_type=jnp.float32)
    return (
        mixture.reshape(rows_here, -1).astype(jnp.bfloat16),
        (highest + jnp.log(totals))[..., 0],
    )


def attend_back(inputs_g, causal, score_scale):
    query_g, key_g, value_g, penalty_g, grad_mix, log_totals = inputs_g
    rows_here = query_g.shape[0]
    heads_q = query_g.reshape(rows_here, HEADS, HEAD_DIM)
    heads_k = key_g.reshape(-1, HEADS, HEAD_DIM)
    heads_v = value_g.reshape(-1, HEADS, HEAD_DIM)
    heads_g = grad_mix.reshape(rows_here, HEADS, HEAD_DIM)
    scores = (
        jnp.einsum("rhd,khd->hrk", heads_q, heads_k, preferred_element_type=jnp.float32)
        * score_scale
    )
    logits = jnp.where(causal[None], scores - penalty_g[None], NEG)
    softmax_w = jnp.exp(logits - log_totals[..., None])
    grad_soft = jnp.einsum("rhd,khd->hrk", heads_g, heads_v, preferred_element_type=jnp.float32)
    inner_sum = jnp.sum(softmax_w * grad_soft, -1, keepdims=True)
    grad_logit = softmax_w * (grad_soft - inner_sum)
    grad_value = jnp.einsum(
        "hrk,rhd->khd", softmax_w.astype(jnp.bfloat16), heads_g, preferred_element_type=jnp.float32
    )
    grad_penalty = -jnp.sum(grad_logit, 0)
    rest_b = grad_logit[1:].astype(jnp.bfloat16)
    grad_query = (
        jnp.einsum("hrk,khd->rhd", rest_b, heads_k[:, 1:], preferred_element_type=jnp.float32)
        * score_scale
    )
    grad_key = (
        jnp.einsum("hrk,rhd->khd", rest_b, heads_q[:, 1:], preferred_element_type=jnp.float32)
        * score_scale
    )
    return (
        grad_value.reshape(-1, D),
        grad_query.reshape(rows_here, -1),
        grad_key.reshape(grad_key.shape[0], -1),
        grad_logit[0],
        grad_penalty,
    )


def spread_layer(
    x_prompt,
    x_cont,
    dy_prompt,
    dy_cont,
    ln1_gain,
    ln1_bias,
    w_qkv,
    b_qv,
    w_out,
    b_out,
    ln2_gain,
    ln2_bias,
    w_up,
    b_up,
    w_down,
    b_down,
):
    shards = (
        ln1_gain,
        ln1_bias,
        w_qkv,
        b_qv,
        w_out,
        b_out,
        ln2_gain,
        ln2_bias,
        w_up,
        b_up,
        w_down,
        b_down,
    )
    groups_here = x_prompt.shape[1]
    prompt_rows = x_prompt.shape[2]
    fsdp_count = lax.axis_size("fsdp")
    fsdp_place = lax.axis_index("fsdp")
    key_count = PROMPT + CONT
    score_scale = HEAD_DIM ** (-0.5)
    select_gain = 4.0 / (PROMPT + CONT)
    query_pos = jnp.concatenate(
        [
            fsdp_place * prompt_rows + jnp.arange(prompt_rows, dtype=jnp.int32),
            PROMPT + jnp.arange(CONT, dtype=jnp.int32),
        ]
    )
    key_pos = jnp.arange(key_count, dtype=jnp.int32)
    causal = key_pos[None, :] <= query_pos[:, None]
    chosen = (key_pos[None, :] < query_pos[:, None]) & (key_pos[None, :] > 0)
    lower_mask = (jnp.arange(fsdp_count, dtype=jnp.int32) < fsdp_place).astype(jnp.float32)
    pad_zeros = jnp.zeros((groups_here, CONT), jnp.float32)
    forward_attend = partial(attend_group, causal=causal, score_scale=score_scale)
    backward_attend = partial(attend_back, causal=causal, score_scale=score_scale)
    totals = tuple(
        (
            jnp.zeros(
                (single.shape[0] * lax.axis_size(("dp", "fsdp")),) + single.shape[1:], jnp.float32
            )
            for single in shards
        )
    )
    outputs_yp, outputs_yc, outputs_dxp, outputs_dxc = ([], [], [], [])
    for batch_index in range(MICRO):
        gathered = (
            lax.all_gather(shards[0], ("dp", "fsdp"), axis=0, tiled=True),
            lax.all_gather(shards[1], ("dp", "fsdp"), axis=0, tiled=True),
            lax.all_gather(shards[2], ("dp", "fsdp"), axis=0, tiled=True),
            lax.all_gather(shards[3], ("dp", "fsdp"), axis=0, tiled=True),
            lax.all_gather(shards[4], ("dp", "fsdp"), axis=0, tiled=True),
            lax.all_gather(shards[5], ("dp", "fsdp"), axis=0, tiled=True),
            lax.all_gather(shards[6], ("dp", "fsdp"), axis=0, tiled=True),
            lax.all_gather(shards[7], ("dp", "fsdp"), axis=0, tiled=True),
            lax.all_gather(shards[8], ("dp", "fsdp"), axis=0, tiled=True),
            lax.all_gather(shards[9], ("dp", "fsdp"), axis=0, tiled=True),
            lax.all_gather(shards[10], ("dp", "fsdp"), axis=0, tiled=True),
            lax.all_gather(shards[11], ("dp", "fsdp"), axis=0, tiled=True),
        )
        inputs_x = jnp.concatenate([x_prompt[batch_index], x_cont[batch_index][:, 0]], 1).astype(
            jnp.float32
        )
        local_rows = inputs_x.shape[1]
        flat_x = inputs_x.reshape(-1, D)
        normed_one = normalize(
            flat_x, gathered[0].astype(jnp.float32), gathered[1].astype(jnp.float32)
        ).astype(jnp.bfloat16)
        joined = jnp.dot(normed_one, gathered[2], preferred_element_type=jnp.float32)
        bias_qv = gathered[3].astype(jnp.float32)
        queries = (
            (joined[:, :D] + bias_qv[:D]).astype(jnp.bfloat16).reshape(groups_here, local_rows, D)
        )
        keys_own = joined[:, D : 2 * D].astype(jnp.bfloat16).reshape(groups_here, local_rows, D)
        values_own = (
            (joined[:, 2 * D :] + bias_qv[D:])
            .astype(jnp.bfloat16)
            .reshape(groups_here, local_rows, D)
        )
        prompt_pair = jnp.concatenate([keys_own[:, :prompt_rows], values_own[:, :prompt_rows]], 2)
        whole_kv = lax.all_gather(prompt_pair, "fsdp", axis=1, tiled=True)
        keys_all = jnp.concatenate([whole_kv[..., :D], keys_own[:, prompt_rows:]], 1)
        values_all = jnp.concatenate([whole_kv[..., D:], values_own[:, prompt_rows:]], 1)
        score_zero = (
            jnp.einsum(
                "grd,gkd->grk",
                queries[..., :HEAD_DIM],
                keys_all[..., :HEAD_DIM],
                preferred_element_type=jnp.float32,
            )
            * score_scale
        )
        select = jnp.where(chosen[None], jnp.maximum(score_zero, 0.0), 0.0)
        own_part = jnp.sum(select[:, :prompt_rows, :PROMPT], 1)
        all_parts = lax.all_gather(own_part[None], "fsdp", axis=0, tiled=True)
        prefix = jnp.sum(all_parts * lower_mask[:, None, None], 0)
        whole_sum = jnp.sum(all_parts, 0)
        select_p = select[:, :prompt_rows]
        select_c = select[:, prompt_rows:]
        penalty = select_gain * jnp.concatenate(
            [
                jnp.concatenate([prefix, pad_zeros], 1)[:, None]
                + (jnp.cumsum(select_p, 1) - select_p),
                jnp.concatenate([whole_sum, pad_zeros], 1)[:, None]
                + (jnp.cumsum(select_c, 1) - select_c),
            ],
            1,
        )
        mixture, log_totals = lax.map(forward_attend, (queries, keys_all, values_all, penalty))
        mixed_flat = mixture.reshape(-1, D)
        residual = flat_x + (
            jnp.dot(mixed_flat, gathered[4], preferred_element_type=jnp.float32)
            + gathered[5].astype(jnp.float32)
        )
        normed_two = normalize(
            residual, gathered[6].astype(jnp.float32), gathered[7].astype(jnp.float32)
        ).astype(jnp.bfloat16)
        upward = jnp.dot(normed_two, gathered[8], preferred_element_type=jnp.float32) + gathered[
            9
        ].astype(jnp.float32)
        active, gelu_back = jax.vjp(partial(jax.nn.gelu, approximate=True), upward)
        active_b = active.astype(jnp.bfloat16)
        output = residual + (
            jnp.dot(active_b, gathered[10], preferred_element_type=jnp.float32)
            + gathered[11].astype(jnp.float32)
        )
        output_b = output.astype(jnp.bfloat16).reshape(groups_here, local_rows, D)
        outputs_yp.append(output_b[:, :prompt_rows])
        outputs_yc.append(output_b[:, prompt_rows:][:, None])
        back_set = (
            lax.all_gather(shards[0], ("dp", "fsdp"), axis=0, tiled=True),
            lax.all_gather(shards[1], ("dp", "fsdp"), axis=0, tiled=True),
            lax.all_gather(shards[2], ("dp", "fsdp"), axis=0, tiled=True),
            lax.all_gather(shards[3], ("dp", "fsdp"), axis=0, tiled=True),
            lax.all_gather(shards[4], ("dp", "fsdp"), axis=0, tiled=True),
            lax.all_gather(shards[5], ("dp", "fsdp"), axis=0, tiled=True),
            lax.all_gather(shards[6], ("dp", "fsdp"), axis=0, tiled=True),
            lax.all_gather(shards[7], ("dp", "fsdp"), axis=0, tiled=True),
            lax.all_gather(shards[8], ("dp", "fsdp"), axis=0, tiled=True),
            lax.all_gather(shards[9], ("dp", "fsdp"), axis=0, tiled=True),
            lax.all_gather(shards[10], ("dp", "fsdp"), axis=0, tiled=True),
            lax.all_gather(shards[11], ("dp", "fsdp"), axis=0, tiled=True),
        )
        grad_out_y = jnp.concatenate(
            [dy_prompt[batch_index], dy_cont[batch_index][:, 0]], 1
        ).reshape(-1, D)
        grad_down = jnp.einsum(
            "rf,rd->fd", active_b, grad_out_y, preferred_element_type=jnp.float32
        )
        grad_bdown = jnp.sum(grad_out_y.astype(jnp.float32), 0)
        grad_active = jnp.einsum(
            "rd,fd->rf", grad_out_y, back_set[10], preferred_element_type=jnp.float32
        )
        grad_upward = gelu_back(grad_active)[0].astype(jnp.bfloat16)
        grad_up = jnp.einsum(
            "rd,rf->df", normed_two, grad_upward, preferred_element_type=jnp.float32
        )
        grad_bup = jnp.sum(grad_upward.astype(jnp.float32), 0)
        grad_normed = jnp.einsum(
            "rf,df->rd", grad_upward, back_set[8], preferred_element_type=jnp.float32
        )
        _, norm_back = jax.vjp(
            normalize, residual, back_set[6].astype(jnp.float32), back_set[7].astype(jnp.float32)
        )
        grad_resid, grad_gain_two, grad_shift_two = norm_back(grad_normed)
        grad_resid = grad_out_y.astype(jnp.float32) + grad_resid
        grad_branch = grad_resid.astype(jnp.bfloat16)
        grad_wout = jnp.einsum(
            "rd,re->de", mixed_flat, grad_branch, preferred_element_type=jnp.float32
        )
        grad_bout = jnp.sum(grad_branch.astype(jnp.float32), 0)
        grad_mixed = jnp.einsum(
            "re,de->rd", grad_branch, back_set[4], preferred_element_type=jnp.float32
        )
        grad_mixed = grad_mixed.astype(jnp.bfloat16).reshape(groups_here, local_rows, D)
        back_values, back_queries, back_keys, back_zero, back_penalty = lax.map(
            backward_attend, (queries, keys_all, values_all, penalty, grad_mixed, log_totals)
        )
        prefix_grad = select_gain * jnp.sum(back_penalty[:, :prompt_rows, :PROMPT], 1)
        whole_grad = select_gain * jnp.sum(back_penalty[:, prompt_rows:, :PROMPT], 1)
        spread_back = prefix_grad[None] * lower_mask[:, None, None] + whole_grad[None]
        part_grad = lax.psum_scatter(spread_back, "fsdp", scatter_dimension=0, tiled=True)[0]
        select_back = jnp.concatenate(
            [
                select_gain * later_sum(back_penalty[:, :prompt_rows])
                + jnp.concatenate([part_grad, pad_zeros], 1)[:, None],
                select_gain * later_sum(back_penalty[:, prompt_rows:]),
            ],
            1,
        )
        grad_zero = (
            back_zero + jnp.where(chosen[None] & (score_zero > 0), select_back, 0.0)
        ).astype(jnp.bfloat16)
        query_zero = (
            jnp.einsum(
                "grk,gkd->grd",
                grad_zero,
                keys_all[..., :HEAD_DIM],
                preferred_element_type=jnp.float32,
            )
            * score_scale
        )
        key_zero = (
            jnp.einsum(
                "grk,grd->gkd",
                grad_zero,
                queries[..., :HEAD_DIM],
                preferred_element_type=jnp.float32,
            )
            * score_scale
        )
        grad_queries = jnp.concatenate([query_zero, back_queries], 2)
        grad_keys = jnp.concatenate([key_zero, back_keys], 2)
        prompt_back = jnp.concatenate([grad_keys[:, :PROMPT], back_values[:, :PROMPT]], 2)
        own_back = lax.psum_scatter(
            prompt_back.astype(jnp.bfloat16), "fsdp", scatter_dimension=1, tiled=True
        ).astype(jnp.float32)
        keys_back = jnp.concatenate([own_back[..., :D], grad_keys[:, PROMPT:]], 1)
        values_back = jnp.concatenate([own_back[..., D:], back_values[:, PROMPT:]], 1)
        grad_joined = (
            jnp.concatenate([grad_queries, keys_back, values_back], 2)
            .astype(jnp.bfloat16)
            .reshape(-1, 3 * D)
        )
        grad_wqkv = jnp.einsum(
            "rd,re->de", normed_one, grad_joined, preferred_element_type=jnp.float32
        )
        grad_bqv = jnp.concatenate(
            [
                jnp.sum(grad_joined[:, :D].astype(jnp.float32), 0),
                jnp.sum(grad_joined[:, 2 * D :].astype(jnp.float32), 0),
            ]
        )
        grad_normed_one = jnp.einsum(
            "re,de->rd", grad_joined, back_set[2], preferred_element_type=jnp.float32
        )
        _, norm_back_one = jax.vjp(
            normalize, flat_x, back_set[0].astype(jnp.float32), back_set[1].astype(jnp.float32)
        )
        grad_input, grad_gain_one, grad_shift_one = norm_back_one(grad_normed_one)
        grad_input = (grad_resid + grad_input).reshape(groups_here, local_rows, D)
        outputs_dxp.append(grad_input[:, :prompt_rows])
        outputs_dxc.append(grad_input[:, prompt_rows:][:, None])
        micro_grads = (
            grad_gain_one,
            grad_shift_one,
            grad_wqkv,
            grad_bqv,
            grad_wout,
            grad_bout,
            grad_gain_two,
            grad_shift_two,
            grad_up,
            grad_bup,
            grad_down,
            grad_bdown,
        )
        totals = tuple((first + second for first, second in zip(totals, micro_grads)))
    results = (
        lax.psum_scatter(totals[0], ("dp", "fsdp"), scatter_dimension=0, tiled=True),
        lax.psum_scatter(totals[1], ("dp", "fsdp"), scatter_dimension=0, tiled=True),
        lax.psum_scatter(totals[2], ("dp", "fsdp"), scatter_dimension=0, tiled=True),
        lax.psum_scatter(totals[3], ("dp", "fsdp"), scatter_dimension=0, tiled=True),
        lax.psum_scatter(totals[4], ("dp", "fsdp"), scatter_dimension=0, tiled=True),
        lax.psum_scatter(totals[5], ("dp", "fsdp"), scatter_dimension=0, tiled=True),
        lax.psum_scatter(totals[6], ("dp", "fsdp"), scatter_dimension=0, tiled=True),
        lax.psum_scatter(totals[7], ("dp", "fsdp"), scatter_dimension=0, tiled=True),
        lax.psum_scatter(totals[8], ("dp", "fsdp"), scatter_dimension=0, tiled=True),
        lax.psum_scatter(totals[9], ("dp", "fsdp"), scatter_dimension=0, tiled=True),
        lax.psum_scatter(totals[10], ("dp", "fsdp"), scatter_dimension=0, tiled=True),
        lax.psum_scatter(totals[11], ("dp", "fsdp"), scatter_dimension=0, tiled=True),
    )
    return (
        jnp.stack(outputs_yp),
        jnp.stack(outputs_yc),
        jnp.stack(outputs_dxp),
        jnp.stack(outputs_dxc),
        results[0],
        results[1],
        results[2],
        results[3],
        results[4],
        results[5],
        results[6],
        results[7],
        results[8],
        results[9],
        results[10],
        results[11],
    )


NCONT = 2
ROWS = PROMPT + NCONT * CONT
SEQ = PROMPT + CONT
SCALE = HEAD_DIM ** (-0.5)
SELECT_GAIN = 4.0 / SEQ
PAIR = 2 * HEAD_DIM
BLOCKS = ((0, 256, 256), (256, 256, 512), (512, 256, 768), (768, 256, 1024), (1024, 64, ROWS))
TAIL = PROMPT - 768
F32 = jnp.float32
B16 = jnp.bfloat16


def mm(a, b):
    return lax.dot_general(a, b, (((1,), (0,)), ((), ())), preferred_element_type=F32)


def mm_nt(a, b):
    return lax.dot_general(a, b, (((1,), (1,)), ((), ())), preferred_element_type=F32)


def masked_half(values, half):
    lane = lax.broadcasted_iota(jnp.int32, values.shape, 1)
    return jnp.where(lane // HEAD_DIM == half, values, 0.0).astype(B16)


def block_masks(place, low=0, high=None):
    first, rows, keys = BLOCKS[place]
    shape = ((high or keys) - low, rows)
    key_id = low + lax.broadcasted_iota(jnp.int32, shape, 0)
    row_id = first + lax.broadcasted_iota(jnp.int32, shape, 1)
    visible = key_id <= row_id
    if first >= SEQ:
        visible = visible & ((key_id < PROMPT) | (key_id >= SEQ))
    chosen = visible & (key_id < row_id) & (key_id > 0)
    return visible, chosen


def split_mm(values, ones):
    high = values.astype(B16)
    low = (values - high.astype(F32)).astype(B16)
    return mm(high, ones) + mm(low, ones)


def triangle(rows, later):
    a = lax.broadcasted_iota(jnp.int32, (rows, rows), 0)
    b = lax.broadcasted_iota(jnp.int32, (rows, rows), 1)
    return jnp.where((a > b) if later else (a < b), 1.0, 0.0).astype(B16)


def chunks_of(keys):
    return [(low, min(low + 256, keys)) for low in range(0, keys, 256)]


def forward_kernel(q_ref, k_ref, v_ref, o_ref, lse_ref, b0, b1, b2, b3, b4, vt_ref, ot_ref, logit_ref, share_ref):
    bias_refs = (b0, b1, b2, b3, b4)
    head = pl.program_id(0)
    half = head % 2
    queries = masked_half(q_ref[...].astype(F32) * SCALE, half)

    @pl.when(head == 0)
    def _():
        carry = None
        for place, (first, rows, keys) in enumerate(BLOCKS):
            scores = mm_nt(k_ref[:keys], queries[first : first + rows])
            visible, chosen = block_masks(place)
            select = jnp.where(chosen, jnp.maximum(scores, 0.0), 0.0)
            penalty = split_mm(select, triangle(rows, False))
            if carry is not None:
                grown = jnp.zeros((keys - carry.shape[0], 1), F32)
                penalty = penalty + jnp.concatenate([carry, grown], 0)
            bias_refs[place][...] = jnp.where(visible, -SELECT_GAIN * penalty, NEG)
            if first + rows == SEQ:
                lane = lax.broadcasted_iota(jnp.int32, select.shape, 1)
                select = jnp.where(lane < TAIL, select, 0.0)
            if place + 1 < len(BLOCKS):
                total = jnp.sum(select, 1, keepdims=True)
                if carry is not None:
                    total = total + jnp.concatenate([carry, grown], 0)
                carry = total

    @pl.when(half == 0)
    def _():
        vt_ref[...] = v_ref[...].astype(F32).T.astype(B16)

    own = pl.ds(pl.multiple_of(half * HEAD_DIM, HEAD_DIM), HEAD_DIM)
    for place, (first, rows, keys) in enumerate(BLOCKS):
        asked = queries[first : first + rows]
        highest = None
        for low, high in chunks_of(keys):
            logits = mm_nt(k_ref[low:high], asked) + bias_refs[place][low:high]
            logit_ref[low:high, first : first + rows] = logits
            top = jnp.max(logits, 0, keepdims=True)
            highest = top if highest is None else jnp.maximum(highest, top)
        total = 0.0
        for low, high in chunks_of(keys):
            raised = jnp.exp(logit_ref[low:high, first : first + rows] - highest)
            total = total + jnp.sum(raised, 0, keepdims=True)
            share_ref[low:high, first : first + rows] = raised.astype(B16)
        mixed = mm(vt_ref[own, :keys], share_ref[:keys, first : first + rows])
        ot_ref[own, first : first + rows] = mixed * (1.0 / total)
        lse_ref[0, :, first : first + rows] = highest + jnp.log(total)

    @pl.when(half == 1)
    def _():
        o_ref[...] = ot_ref[...].T.astype(B16)


def backward_kernel(
    q_ref, k_ref, v_ref, g_ref, o_ref, lse_ref, b0, b1, b2, b3, b4,
    joined_ref,
    kt_ref, dqt_ref, dk_acc, dv_acc, p0, p1, p2, p3, p4, stage_ref, share_ref, grad_ref, inner_ref, sems,
):
    bias_refs = (b0, b1, b2, b3, b4)
    pen_refs = (p0, p1, p2, p3, p4)
    head = HEADS - 1 - pl.program_id(0)
    half = head % 2
    queries = masked_half(q_ref[...].astype(F32) * SCALE, half)
    grads = masked_half(g_ref[...].astype(F32), half)
    own = pl.ds(pl.multiple_of(half * HEAD_DIM, HEAD_DIM), HEAD_DIM)

    @pl.when(head == HEADS - 1)
    def _():
        for pen in pen_refs:
            pen[...] = jnp.zeros_like(pen)

    @pl.when(half == 1)
    def _():
        kt_ref[...] = k_ref[...].astype(F32).T.astype(B16)
        both = (o_ref[...].astype(F32) * g_ref[...].astype(F32)).T
        inner_ref[0] = jnp.sum(both[:HEAD_DIM], 0, keepdims=True)
        inner_ref[1] = jnp.sum(both[HEAD_DIM:], 0, keepdims=True)
        dk_acc[...] = jnp.zeros_like(dk_acc)
        dv_acc[...] = jnp.zeros_like(dv_acc)

    def tile(place, low, high):
        first, rows, _ = BLOCKS[place]
        scores = mm_nt(k_ref[low:high], queries[first : first + rows])
        shares = jnp.exp(
            scores + bias_refs[place][low:high] - lse_ref[0, :, first : first + rows]
        )
        back = mm_nt(v_ref[low:high], grads[first : first + rows])
        share_ref[low:high, first : first + rows] = shares.astype(B16)
        return scores, shares * (back - inner_ref[half, :, first : first + rows])

    def finish(low, high):
        dv_acc[low:high] += mm(share_ref[low:high, low:], grads[low:])
        dk_acc[low:high] += mm(grad_ref[low:high, low:], queries[low:])

    def finish_queries(place):
        first, rows, keys = BLOCKS[place]
        dqt_ref[own, first : first + rows] = mm(
            kt_ref[own, :keys], grad_ref[:keys, first : first + rows]
        )

    @pl.when(head != 0)
    def _():
        for low, high in chunks_of(ROWS):
            for place, (first, rows, keys) in enumerate(BLOCKS):
                if low < keys:
                    _, grad = tile(place, low, high)
                    pen_refs[place][low:high] += grad
                    grad_ref[low:high, first : first + rows] = grad.astype(B16)
            finish(low, high)
            finish_queries(low // 256)

    @pl.when(head == 0)
    def _():
        for low, high in chunks_of(ROWS):
            carry = None
            for place in reversed(range(len(BLOCKS))):
                first, rows, keys = BLOCKS[place]
                if low >= keys:
                    continue
                scores, grad = tile(place, low, high)
                whole = pen_refs[place][low:high] + grad
                later = split_mm(whole, triangle(rows, True))
                total = jnp.sum(whole, 1, keepdims=True)
                if carry is not None:
                    if first + rows == SEQ:
                        lane = lax.broadcasted_iota(jnp.int32, later.shape, 1)
                        later = later + jnp.where(lane < TAIL, carry, 0.0)
                    else:
                        later = later + carry
                    total = total + carry
                carry = total
                chosen = block_masks(place, low, high)[1]
                grad = grad + jnp.where(chosen & (scores > 0.0), -SELECT_GAIN * later, 0.0)
                grad_ref[low:high, first : first + rows] = grad.astype(B16)
            finish(low, high)
            finish_queries(low // 256)

    def copies(pair):
        return [
            pltpu.make_async_copy(
                stage_ref.at[part],
                joined_ref.at[:, pl.ds(pl.multiple_of(part * D + pair * PAIR, PAIR), PAIR)],
                sems.at[part],
            )
            for part in range(3)
        ]

    @pl.when((half == 0) & (head != HEADS - 2))
    def _():
        for copy in copies(head // 2 + 1):
            copy.wait()

    @pl.when(half == 0)
    def _():
        stage_ref[0] = (dqt_ref[...].T * SCALE).astype(B16)
        stage_ref[1] = dk_acc[...].astype(B16)
        stage_ref[2] = dv_acc[...].astype(B16)
        for copy in copies(head // 2):
            copy.start()

    @pl.when(head == 0)
    def _():
        for copy in copies(0):
            copy.wait()


def pair_spec(index):
    return pl.BlockSpec((ROWS, PAIR), index)


def whole_specs():
    return [pl.BlockSpec((keys, rows), lambda i: (0, 0)) for _, rows, keys in BLOCKS]


PAIRS = HEADS // 2


def attend_forward(joined):
    return pl.pallas_call(
        forward_kernel,
        grid=(HEADS,),
        in_specs=[
            pair_spec(lambda i: (0, i // 2)),
            pair_spec(lambda i: (0, PAIRS + i // 2)),
            pair_spec(lambda i: (0, 2 * PAIRS + i // 2)),
        ],
        out_specs=[
            pair_spec(lambda i: (0, i // 2)),
            pl.BlockSpec((1, 1, ROWS), lambda i: (i, 0, 0)),
            *whole_specs(),
        ],
        out_shape=[
            jax.ShapeDtypeStruct((ROWS, D), B16),
            jax.ShapeDtypeStruct((HEADS, 1, ROWS), F32),
            *(jax.ShapeDtypeStruct((keys, rows), F32) for _, rows, keys in BLOCKS),
        ],
        scratch_shapes=[
            pltpu.VMEM((PAIR, ROWS), B16),
            pltpu.VMEM((PAIR, ROWS), F32),
            pltpu.VMEM((ROWS, ROWS), F32),
            pltpu.VMEM((ROWS, ROWS), B16),
        ],
        name="attend_forward",
    )(joined, joined, joined)


def attend_backward(joined, grad_mixed, mixed, lse, biases):
    last = PAIRS - 1
    return pl.pallas_call(
        backward_kernel,
        grid=(HEADS,),
        in_specs=[
            pair_spec(lambda i: (0, last - i // 2)),
            pair_spec(lambda i: (0, PAIRS + last - i // 2)),
            pair_spec(lambda i: (0, 2 * PAIRS + last - i // 2)),
            pair_spec(lambda i: (0, last - i // 2)),
            pair_spec(lambda i: (0, last - i // 2)),
            pl.BlockSpec((1, 1, ROWS), lambda i: (HEADS - 1 - i, 0, 0)),
            *whole_specs(),
        ],
        out_specs=pl.BlockSpec(memory_space=pl.ANY),
        out_shape=jax.ShapeDtypeStruct((ROWS, 3 * D), B16),
        scratch_shapes=[
            pltpu.VMEM((PAIR, ROWS), B16),
            pltpu.VMEM((PAIR, ROWS), F32),
            pltpu.VMEM((ROWS, PAIR), F32),
            pltpu.VMEM((ROWS, PAIR), F32),
            *(pltpu.VMEM((keys, rows), F32) for _, rows, keys in BLOCKS),
            pltpu.VMEM((3, ROWS, PAIR), B16),
            pltpu.VMEM((ROWS, ROWS), B16),
            pltpu.VMEM((ROWS, ROWS), B16),
            pltpu.VMEM((2, 1, ROWS), F32),
            pltpu.SemaphoreType.DMA((3,)),
        ],
        name="attend_backward",
    )(joined, joined, joined, grad_mixed, mixed, lse, *biases)


EVERY = ("dp", "fsdp")
CORE = 2
PLANE = (0, 1, 4, 5)


def device_count():
    return lax.axis_size("dp") * lax.axis_size("fsdp")


def depth():
    return device_count() // 8


def place_of():
    number = lax.axis_index("dp")
    return number // 4, number // 2 % 2, number % 2, lax.axis_index("fsdp")


def swap(value, mask):
    return lax.ppermute(value, EVERY, [(i, i ^ mask) for i in range(device_count())])


def arrange(pieces, own):
    pieces = list(pieces)
    bit = 1
    while bit < len(pieces):
        odd = (own // bit) % 2 == 1
        pieces = [jnp.where(odd, pieces[k ^ bit], pieces[k]) for k in range(len(pieces))]
        bit *= 2
    return pieces


def gather_steps(shard):
    z, x, core, y = place_of()
    column = [shard] + [swap(shard, 8 * k) for k in range(1, depth())]
    value = jnp.stack(arrange(column, z))
    plane = [value] + [swap(value, mask) for mask in PLANE[1:]]
    plane = arrange(plane, 2 * x + y)
    value = jnp.stack([jnp.stack(plane[:2], 1), jnp.stack(plane[2:], 1)], 1)
    value = jnp.stack(arrange([value, swap(value, CORE)], core), 2)
    return value.reshape(-1, shard.shape[1])


def take(value, index, axis):
    return lax.dynamic_index_in_dim(value, index, axis, keepdims=False)


def add_up(pieces):
    total = pieces[0].astype(F32)
    for piece in pieces[1:]:
        total = total + piece.astype(F32)
    return total


def scatter_core(grad):
    core = place_of()[2]
    rows = grad.shape[0] // device_count()
    value = grad.reshape(depth(), 2, 2, 2, rows, grad.shape[1])
    other = swap(take(value, 1 - core, 2), CORE)
    return take(value, core, 2) + other


def scatter_plane(value):
    _, x, _, y = place_of()
    plane = [
        take(take(value, x ^ (mask // 4), 1), y ^ (mask % 2), 1) for mask in PLANE
    ]
    others = [swap(piece, mask) for piece, mask in zip(plane[1:], PLANE[1:])]
    return plane[:1] + others


def scatter_column(plane):
    z = place_of()[0]
    value = add_up(plane).astype(B16)
    column = [take(value, z ^ k, 0) for k in range(depth())]
    others = [swap(column[k], 8 * k) for k in range(1, depth())]
    return add_up(column[:1] + others)


def pack_vectors(vectors):
    rows = D // device_count()
    padded = [jnp.pad(v, (0, 128 - v.shape[0]))[None] for v in vectors]
    return jnp.pad(jnp.concatenate(padded, 0), ((0, rows - len(vectors)), (0, 0)))


def unpack_vectors(columns, sizes):
    rows = columns.reshape(-1, D // device_count(), 128)
    return [rows[:, i, :size].reshape(-1).astype(F32) for i, size in enumerate(sizes)]


def pack_kernel(*refs):
    out_ref = refs[-1]
    devices = out_ref.shape[0]
    out_ref[...] = jnp.zeros_like(out_ref)
    for i, ref in enumerate(refs[:-1]):
        count = ref.shape[1]
        piece = count // devices
        values = ref[...]
        for j in range(devices):
            out_ref[j, i : i + 1, :piece] = values[:, j * piece : (j + 1) * piece]


def pack_grads(vectors):
    devices = device_count()
    return pl.pallas_call(
        pack_kernel,
        out_shape=jax.ShapeDtypeStruct((devices, D // devices, 128), F32),
        name="pack_grads",
    )(*(v.astype(F32)[None] for v in vectors))


def gelu_pair(upward):
    rate = (2.0 / jnp.pi) ** 0.5
    square = upward * upward
    bend = jnp.tanh(upward * (rate + (rate * 0.044715) * square))
    gate = 0.5 + 0.5 * bend
    slope = gate + upward * (1.0 - bend * bend) * (
        0.5 * rate + (1.5 * 0.044715 * rate) * square
    )
    return (upward * gate).astype(B16), slope.astype(B16)


def normalize_back(values, gain, grad):
    center = values - jnp.mean(values, -1, keepdims=True)
    rate = lax.rsqrt(jnp.mean(center * center, -1, keepdims=True) + EPS)
    unit = center * rate
    scaled = grad * gain
    inner = jnp.mean(scaled * unit, -1, keepdims=True)
    back = rate * (scaled - jnp.mean(scaled, -1, keepdims=True) - unit * inner)
    return back, jnp.sum(grad * unit, 0), jnp.sum(grad, 0)


def pick(first, second, when):
    return jnp.where(when, first, second)


def split_rows(prompt, cont):
    low = lax.axis_index("fsdp") == 0
    mine = [pick(t[0], t[1], low).reshape(-1, D) for t in (prompt, cont)]
    away = [pick(t[1], t[0], low).reshape(-1, D) for t in (prompt, cont)]
    return mine, jnp.concatenate(away, 0)


def trade_rows(mine, away):
    low = lax.axis_index("fsdp") == 0
    came = lax.ppermute(away, "fsdp", [(0, 1), (1, 0)])
    half = mine[0].shape[0]
    parts = (came[:half], came[half:])
    return jnp.concatenate(
        [
            pick(mine[0], parts[0], low),
            pick(parts[0], mine[0], low),
            pick(mine[1], parts[1], low),
            pick(parts[1], mine[1], low),
        ],
        0,
    )


def trade_back(whole):
    place = lax.axis_index("fsdp")
    low = place == 0
    half = PROMPT // 2
    parts = (
        (whole[:half], whole[PROMPT:SEQ]),
        (whole[half:PROMPT], whole[SEQ:]),
    )
    mine = [pick(parts[0][i], parts[1][i], low) for i in range(2)]
    away = [pick(parts[1][i], parts[0][i], low) for i in range(2)]
    came = lax.ppermute(jnp.concatenate(away, 0).astype(B16), "fsdp", [(0, 1), (1, 0)])
    return mine, came


def join_rows(mine, came, kind):
    low = lax.axis_index("fsdp") == 0
    came = (came[: PROMPT // 2], came[PROMPT // 2 :])
    out = []
    for i in range(2):
        own, other = mine[i].astype(kind), came[i].astype(kind)
        out.append(jnp.stack([pick(own, other, low), pick(other, own, low)]))
    return out[0][:, None], out[1][:, None, None]


def whole_layer(*args):
    return whole_steps(*args)


def whole_steps(
    x_prompt, x_cont, dy_prompt, dy_cont,
    ln1_gain, ln1_bias, w_qkv, b_qv, w_out, b_out,
    ln2_gain, ln2_bias, w_up, b_up, w_down, b_down,
):
    devices = device_count()
    vectors = (ln1_gain, ln1_bias, b_qv, b_out, ln2_gain, ln2_bias, b_up, b_down)
    sizes = [v.shape[0] for v in vectors]
    chunks = w_down.shape[0] // w_qkv.shape[0]
    rows = w_qkv.shape[0]
    flat_x = trade_rows(*split_rows(x_prompt, x_cont)).astype(F32)
    rest = jnp.concatenate(
        [w_out, *(w_up[:, i * D : (i + 1) * D] for i in range(chunks)), w_down], 0
    )
    full_first = gather_steps(jnp.concatenate([w_qkv, pack_vectors(vectors)], 1))
    full_rest = lax.all_gather(rest, EVERY, axis=0)
    full_qkv = full_first[:, : 3 * D]
    (
        gain_one, shift_one, bias_qv, bias_out, gain_two, shift_two, bias_up, bias_down,
    ) = unpack_vectors(full_first[:, 3 * D :], sizes)
    hidden = w_up.shape[1]
    full_out = full_rest[:, :rows].reshape(D, D)
    full_up = jnp.concatenate(
        [full_rest[:, rows * i : rows * (i + 1)].reshape(D, D) for i in range(1, chunks + 1)], 1
    )
    full_down = full_rest[:, rows * (chunks + 1) :].reshape(hidden, D)

    center = flat_x - jnp.mean(flat_x, -1, keepdims=True)
    rate = lax.rsqrt(jnp.mean(center * center, -1, keepdims=True) + EPS)
    normed_one = (center * rate * gain_one + shift_one).astype(B16)
    bias_joined = jnp.concatenate([bias_qv[:D], jnp.zeros((D,), F32), bias_qv[D:]])
    joined = (
        jnp.dot(normed_one, full_qkv, preferred_element_type=F32) + bias_joined
    ).astype(B16)
    dy_mine, dy_away = split_rows(dy_prompt, dy_cont)
    joined, dy_away = lax.optimization_barrier((joined, dy_away))
    grad_y = trade_rows(dy_mine, dy_away)
    mixed, lse, *biases = attend_forward(joined)
    residual = flat_x + (jnp.dot(mixed, full_out, preferred_element_type=F32) + bias_out)
    normed_two = lax.optimization_barrier(normalize(residual, gain_two, shift_two).astype(B16))
    upward = jnp.dot(normed_two, full_up, preferred_element_type=F32) + bias_up
    active, slope = lax.optimization_barrier(gelu_pair(upward))

    def weight_grad(left, right):
        return jnp.einsum("rd,re->de", left, right, preferred_element_type=F32).astype(B16)

    def through(grad, weight):
        return jnp.einsum("re,de->rd", grad, weight, preferred_element_type=F32)

    def column_sum(values):
        return jnp.sum(values.astype(F32), 0)

    grad_upward = (through(grad_y, full_down) * slope.astype(F32)).astype(B16)
    grad_down = weight_grad(active, grad_y)
    grad_up = weight_grad(normed_two, grad_upward)
    packed_grads = jnp.concatenate(
        [
            *(grad_up[:, i * D : (i + 1) * D].reshape(devices, rows, D) for i in range(chunks)),
            grad_down.reshape(devices, -1, D),
        ],
        1,
    )
    packed_grads, active, grad_upward = lax.optimization_barrier(
        (packed_grads, active, grad_upward)
    )
    own_hidden = lax.psum_scatter(packed_grads, EVERY, scatter_dimension=0).astype(F32)
    grad_w_up = jnp.concatenate(
        [own_hidden[i * rows : (i + 1) * rows] for i in range(chunks)], 1
    )
    grad_w_down = own_hidden[chunks * rows :]
    output = residual + (jnp.dot(active, full_down, preferred_element_type=F32) + bias_down)
    came_y = trade_back(output.astype(B16))

    grad_b_down = column_sum(grad_y)
    grad_b_up = column_sum(grad_upward)
    grad_resid, grad_gain_two, grad_shift_two = normalize_back(
        residual, gain_two, through(grad_upward, full_up)
    )
    grad_resid = grad_y.astype(F32) + grad_resid
    grad_branch = grad_resid.astype(B16)
    out_plane = scatter_plane(scatter_core(weight_grad(mixed, grad_branch)))
    grad_b_out = column_sum(grad_branch)
    grad_mixed = through(grad_branch, full_out).astype(B16)
    grad_joined = attend_backward(joined, grad_mixed, mixed, lse, biases)
    grad_b_qv = jnp.concatenate(
        [column_sum(grad_joined[:, :D]), column_sum(grad_joined[:, 2 * D :])]
    )
    grad_input, grad_gain_one, grad_shift_one = normalize_back(
        flat_x, gain_one, through(grad_joined, full_qkv)
    )
    grad_x = grad_resid + grad_input
    came_x = trade_back(grad_x)
    small = (
        grad_gain_one, grad_shift_one, grad_b_qv, grad_b_out,
        grad_gain_two, grad_shift_two, grad_b_up, grad_b_down,
    )
    small, grad_x, grad_joined = lax.optimization_barrier(
        (pack_grads(small), grad_x, grad_joined)
    )
    grad_qkv = weight_grad(normed_one, grad_joined)
    first = scatter_core(
        jnp.concatenate([grad_qkv, small.reshape(D, 128).astype(B16)], 1)
    )
    first, came_y, out_plane = lax.optimization_barrier((first, came_y, out_plane))
    plane = scatter_plane(first)
    plane, came_x = lax.optimization_barrier((plane, came_x))
    own_first = scatter_column(plane)
    dx_prompt, dx_cont = join_rows(*came_x, F32)
    grad_w_out = scatter_column(out_plane)
    y_prompt, y_cont = join_rows(*came_y, B16)
    grad_w_qkv = own_first[:, : 3 * D]
    own_vectors = own_first[:, 3 * D :]
    pieces = [own_vectors[i, :size] for i, size in enumerate(sizes)]
    return (
        y_prompt, y_cont, dx_prompt, dx_cont,
        pieces[0], pieces[1], grad_w_qkv, pieces[2], grad_w_out, pieces[3],
        pieces[4], pieces[5], grad_w_up, pieces[6], grad_w_down, pieces[7],
    )


def solution(mesh):
    sizes = dict(mesh.shape)
    whole = sizes["fsdp"] == MICRO == NCONT and sizes["dp"] & (sizes["dp"] - 1) == 0
    return jax.shard_map(
        whole_layer if whole else spread_layer,
        mesh=mesh,
        in_specs=(
            P(None, "dp", "fsdp", None),
            P(None, "dp", "fsdp", None, None),
            P(None, "dp", "fsdp", None),
            P(None, "dp", "fsdp", None, None),
            P(("dp", "fsdp")),
            P(("dp", "fsdp")),
            P(("dp", "fsdp"), None),
            P(("dp", "fsdp")),
            P(("dp", "fsdp"), None),
            P(("dp", "fsdp")),
            P(("dp", "fsdp")),
            P(("dp", "fsdp")),
            P(("dp", "fsdp"), None),
            P(("dp", "fsdp")),
            P(("dp", "fsdp"), None),
            P(("dp", "fsdp")),
        ),
        out_specs=(
            P(None, "dp", "fsdp", None),
            P(None, "dp", "fsdp", None, None),
            P(None, "dp", "fsdp", None),
            P(None, "dp", "fsdp", None, None),
            P(("dp", "fsdp")),
            P(("dp", "fsdp")),
            P(("dp", "fsdp"), None),
            P(("dp", "fsdp")),
            P(("dp", "fsdp"), None),
            P(("dp", "fsdp")),
            P(("dp", "fsdp")),
            P(("dp", "fsdp")),
            P(("dp", "fsdp"), None),
            P(("dp", "fsdp")),
            P(("dp", "fsdp"), None),
            P(("dp", "fsdp")),
        ),
        check_vma=False,
    )
```
